32 devices in a mesh: rows: 8 (over z, y), blk: 4 (over x, core).
Axes of the slice: x: 2, y: 2, z: 4, core: 2. Of those that a mesh axis runs over, the one named last changes fastest.
Arguments:
- tokens: bfloat16 [32, 384, 768], P(('rows', 'blk')), may hold values from -6 to 6
- seg_ids: int32 [32, 384], P(('rows', 'blk')), may hold values from -1 to 2, as said below
- target_index: int32 [96, 4, 32], P(('rows', 'blk')), may hold values from 0 to 195, as said below
- qkv_weight: bfloat16 [768, 2304], replicated, may hold values from -0.21875 to 0.21875
- q_bias: float32 [768], replicated, may hold values from -3 to 3
- v_bias: float32 [768], replicated, may hold values from -3 to 3
- out_weight: bfloat16 [768, 768], replicated, may hold values from -1.75 to 1.75
- out_bias: float32 [768], replicated, may hold values from -2 to 2
- norm1_gain: float32 [768], replicated, may hold values from 0.25 to 1.75
- norm1_shift: float32 [768], replicated, may hold values from -2 to 2
- norm2_gain: float32 [768], replicated, may hold values from 0.25 to 1.75
- norm2_shift: float32 [768], replicated, may hold values from -2 to 2
- fc1_weight: bfloat16 [768, 3072], replicated, may hold values from -0.21875 to 0.21875
- fc1_bias: float32 [3072], replicated, may hold values from -3 to 3
- fc2_weight: bfloat16 [3072, 768], replicated, may hold values from -0.109375 to 0.109375
- fc2_bias: float32 [768], replicated, may hold values from -2 to 2
- target_grad: bfloat16 [4, 96, 32, 768], P('blk', 'rows'), may hold values from -6 to 6
Outputs:
- targets: bfloat16 [4, 96, 32, 768], P('blk', 'rows')
- tokens_grad: bfloat16 [32, 384, 768], P(('rows', 'blk'))
- qkv_weight_grad: float32 [768, 2304], replicated
- q_bias_grad: float32 [768], replicated
- v_bias_grad: float32 [768], replicated
- out_weight_grad: float32 [768, 768], replicated
- out_bias_grad: float32 [768], replicated
- norm1_gain_grad: float32 [768], replicated
- norm1_shift_grad: float32 [768], replicated
- norm2_gain_grad: float32 [768], replicated
- norm2_shift_grad: float32 [768], replicated
- fc1_weight_grad: float32 [768, 3072], replicated
- fc1_bias_grad: float32 [3072], replicated
- fc2_weight_grad: float32 [3072, 768], replicated
- fc2_bias_grad: float32 [768], replicated
The draws below stay inside these ranges and needn't reach their ends.
Inputs may be any that keep to these rules, and one draw needn't show every extreme that they name: `seg_ids`: each packed row holds exactly 3 images as segments 0, 1, ... in this order from slot 0, followed by padding slots of segment -1. An image has 48 to 196 patches, and some image has exactly 196. `target_index`: entries of image i are patch positions within segment i % 3 of packed row i // 3, below that image's number of patches; they may repeat. The last patch of an image with 196 patches is named in some block.
All inputs are finite; a program needn't handle non-finite values.
Results may differ from the reference program's by a relative error of at most 0.012.
Values may be sent and summed in bfloat16 or wider, within the bound.
No kernel may reach another device: no remote copies, remote signals or barrier semaphores. Data moves between devices by JAX's collectives and lax.ppermute only.
A program may use at most 192 MiB of HBM per device.

```python
import jax
import jax.numpy as jnp
from jax import lax

D = 768
HEADS = 12
HEAD_DIM = 64
FF = 3072
L = 384
IMG_ROW = 3
MAXLEN = 196
BLOCKS = 4
TGT = 32
ROWS = 32
IMAGES = 96


def image_lengths(key):
    base_key = jax.random.fold_in(key, 7)
    first_key, second_key, third_key, fourth_key = jax.random.split(base_key, 4)
    shortest = L // 8
    entries = jax.random.randint(first_key, (ROWS, IMG_ROW), shortest, L // IMG_ROW + 1, dtype=jnp.int32)
    special = jax.random.randint(second_key, (ROWS, IMG_ROW), shortest, (L - MAXLEN) // (IMG_ROW - 1) + 1, dtype=jnp.int32)
    chosen_row = jax.random.randint(third_key, (), 0, ROWS, dtype=jnp.int32)
    chosen_slot = jax.random.randint(fourth_key, (), 0, IMG_ROW, dtype=jnp.int32)
    column = jnp.arange(IMG_ROW, dtype=jnp.int32)[None, :]
    row_ids = jnp.arange(ROWS, dtype=jnp.int32)[:, None]
    special = jnp.where(column == chosen_slot, MAXLEN, special).astype(jnp.int32)
    return jnp.where(row_ids == chosen_row, special, entries).astype(jnp.int32)


def draw_seg_ids(key, part):
    lengths = image_lengths(key)
    row_ends = jnp.cumsum(lengths, axis=1)
    slot_pos = jnp.arange(L, dtype=jnp.int32)
    segment = jnp.sum((slot_pos[None, :, None] >= row_ends[:, None, :]).astype(jnp.int32), axis=2)
    return jnp.where(segment >= IMG_ROW, -1, segment).astype(jnp.int32)


def draw_target_index(key, part):
    lengths = image_lengths(key)
    patch_key = jax.random.fold_in(key, 11)
    block_key = jax.random.fold_in(key, 13)
    place_key = jax.random.fold_in(key, 17)
    drawn = jax.random.randint(patch_key, (ROWS, IMG_ROW, BLOCKS, TGT), 0, lengths[:, :, None, None], dtype=jnp.int32)
    chosen_block = jax.random.randint(block_key, (), 0, BLOCKS, dtype=jnp.int32)
    chosen_place = jax.random.randint(place_key, (), 0, TGT, dtype=jnp.int32)
    block_ids = jnp.arange(BLOCKS, dtype=jnp.int32)[None, None, :, None]
    place_ids = jnp.arange(TGT, dtype=jnp.int32)[None, None, None, :]
    longest = (lengths == MAXLEN)[:, :, None, None]
    spot = longest & (block_ids == chosen_block) & (place_ids == chosen_place)
    drawn = jnp.where(spot, MAXLEN - 1, drawn).astype(jnp.int32)
    return drawn.reshape(ROWS * IMG_ROW, BLOCKS, TGT).astype(jnp.int32)


def block_levels(own_key, shape, cuts, smallest, largest):
    loudness = 1.0
    for axis_at, blocks in cuts:
        draws = jax.random.uniform(jax.random.fold_in(jax.random.fold_in(own_key, 6), axis_at), (blocks,), jnp.float32, smallest / len(cuts), largest / len(cuts))
        loudness = loudness * jnp.repeat(jnp.exp(draws), shape[axis_at] // blocks).reshape((-1,) + (1,) * (len(shape) - 1 - axis_at))
    return loudness


def normal_values(rng, extent, scale, bound, cuts=(), kind=jnp.bfloat16):
    result = scale * jax.random.normal(rng, extent, jnp.float32)
    if cuts:
        result = result * block_levels(rng, extent, cuts, -0.22, 0.18)
    return jnp.clip(result, -bound, bound).astype(kind)


def setup_inputs(seed: int = 0) -> dict:
    key_of = jax.random.split(jax.random.key(seed), 18)
    return {
        "tokens": normal_values(key_of[0], (ROWS, L, D), 1.0, 6.0, ((0, 32),)),
        "seg_ids": draw_seg_ids(jax.random.fold_in(key_of[17], 71), 0),
        "target_index": draw_target_index(jax.random.fold_in(key_of[17], 71), 0),
        "qkv_weight": normal_values(key_of[3], (D, 3 * D), D ** -0.5, 0.21875),
        "q_bias": normal_values(key_of[4], (D,), 0.5, 3.0, (), jnp.float32),
        "v_bias": normal_values(key_of[5], (D,), 0.5, 3.0, (), jnp.float32),
        "out_weight": normal_values(key_of[6], (D, D), (max(D // 64, 4)) ** -0.5, 1.75),
        "out_bias": normal_values(key_of[7], (D,), 0.3, 2.0, (), jnp.float32),
        "norm1_gain": jnp.clip(1.0 + 0.15 * jax.random.normal(key_of[8], (D,), jnp.float32), 0.25, 1.75),
        "norm1_shift": normal_values(key_of[9], (D,), 0.3, 2.0, (), jnp.float32),
        "norm2_gain": jnp.clip(1.0 + 0.15 * jax.random.normal(key_of[10], (D,), jnp.float32), 0.25, 1.75),
        "norm2_shift": normal_values(key_of[11], (D,), 0.3, 2.0, (), jnp.float32),
        "fc1_weight": normal_values(key_of[12], (D, FF), D ** -0.5, 0.21875),
        "fc1_bias": normal_values(key_of[13], (FF,), 0.5, 3.0, (), jnp.float32),
        "fc2_weight": normal_values(key_of[14], (FF, D), FF ** -0.5, 0.109375),
        "fc2_bias": normal_values(key_of[15], (D,), 0.3, 2.0, (), jnp.float32),
        "target_grad": normal_values(key_of[16], (BLOCKS, IMAGES, TGT, D), 1.0, 6.0, ((0, 4), (1, 8))),
    }


norm_eps = 1e-06
score_scale = 0.125
neg_large = -1e+30
highest = lax.Precision.HIGHEST

@jax.custom_vjp
def low(v):
    return lax.optimization_barrier(v.astype(jnp.bfloat16)).astype(jnp.float32)

@jax.custom_vjp
def low_back(v):
    return v

def low_keep(v):
    return (low(v), None)

def low_pass(kept, grad):
    return (grad,)

def back_keep(v):
    return (v, None)

def back_low(kept, grad):
    return (low(grad),)
low.defvjp(low_keep, low_pass)
low_back.defvjp(back_keep, back_low)

def layer_norm(values, norm_gain, norm_shift):
    center = values - lax.optimization_barrier(jnp.mean(values, axis=-1, keepdims=True))
    spread = lax.optimization_barrier(jnp.mean(center * center, axis=-1, keepdims=True))
    return center * lax.rsqrt(spread + norm_eps) * norm_gain + norm_shift

def token_rows(segments, patches):
    count_rows = segments.shape[0]
    length = segments.shape[1]
    images = patches.shape[0]
    per_row = images // count_rows
    slot_ids = jnp.arange(per_row, dtype=jnp.int32)
    before = (segments[:, None, :] >= 0) & (segments[:, None, :] < slot_ids[None, :, None])
    starts = lax.optimization_barrier(jnp.sum(before.astype(jnp.int32), axis=2)).astype(jnp.int32)
    offset = jnp.arange(count_rows, dtype=jnp.int32)[:, None] * length + starts
    located = offset.reshape(images)[:, None, None] + patches
    return jnp.transpose(located, (1, 0, 2)).astype(jnp.int32)

def attend_row(pieces):
    queries, keys_row, values_row, segment = pieces
    scores = jnp.einsum('qhd,khd->hqk', queries, keys_row, precision=highest) * score_scale
    scores = low_back(scores)
    allowed = segment[:, None] == segment[None, :]
    scores = jnp.where(allowed[None], scores, neg_large)
    row_peak = lax.optimization_barrier(jnp.max(scores, axis=-1, keepdims=True))
    raised = jnp.exp(scores - row_peak)
    attn_prob = low(raised / lax.optimization_barrier(jnp.sum(raised, axis=-1, keepdims=True)))
    return jnp.einsum('hqk,khd->qhd', attn_prob, values_row, precision=highest)

def forward(inputs, params, segments, located):
    qkv_weight, q_bias, v_bias, out_weight, out_bias, norm1_gain, norm1_shift, norm2_gain, norm2_shift, fc1_weight, fc1_bias, fc2_weight, fc2_bias = params
    group_rows = segments.shape[0]
    normed = low(layer_norm(inputs, norm1_gain, norm1_shift))
    joint_out = jnp.dot(normed, qkv_weight, precision=highest)
    queries = low(low_back(joint_out[:, :D] + q_bias))
    keys_all = low(low_back(joint_out[:, D:2 * D]))
    values_all = low(low_back(joint_out[:, 2 * D:] + v_bias))
    shaped = (group_rows, L, HEADS, HEAD_DIM)
    mixed_low = lax.map(jax.checkpoint(attend_row), (queries.reshape(shaped), keys_all.reshape(shaped), values_all.reshape(shaped), segments))
    mixed_low = low(low_back(mixed_low.reshape(group_rows * L, D)))
    branch = low_back(jnp.dot(mixed_low, out_weight, precision=highest) + out_bias)
    middle = inputs + branch
    second_norm = low(layer_norm(middle, norm2_gain, norm2_shift))
    hidden = low_back(jnp.dot(second_norm, fc1_weight, precision=highest) + fc1_bias)
    active = low(jax.nn.gelu(hidden, approximate=False))
    mlp_branch = low_back(jnp.dot(active, fc2_weight, precision=highest) + fc2_bias)
    output = middle + mlp_branch
    return low(output[located])

def reference(tokens, seg_ids, target_index, qkv_weight, q_bias, v_bias, out_weight, out_bias, norm1_gain, norm1_shift, norm2_gain, norm2_shift, fc1_weight, fc1_bias, fc2_weight, fc2_bias, target_grad):
    params = (qkv_weight.astype(jnp.float32), q_bias.astype(jnp.float32), v_bias.astype(jnp.float32), out_weight.astype(jnp.float32), out_bias.astype(jnp.float32), norm1_gain.astype(jnp.float32), norm1_shift.astype(jnp.float32), norm2_gain.astype(jnp.float32), norm2_shift.astype(jnp.float32), fc1_weight.astype(jnp.float32), fc1_bias.astype(jnp.float32), fc2_weight.astype(jnp.float32), fc2_bias.astype(jnp.float32))
    group_count = ROWS // 8
    group_images = 8 * IMG_ROW
    token_groups = tokens.reshape(group_count, 8, L, D)
    seg_groups = seg_ids.reshape(group_count, 8, L)
    index_groups = target_index.reshape(group_count, group_images, BLOCKS, TGT)
    grad_groups = jnp.moveaxis(target_grad.reshape(BLOCKS, group_count, group_images, TGT, D), 1, 0)

    def group_step(totals, pieces):
        block_tokens, block_segs, block_index, block_grad = pieces
        located = token_rows(block_segs, block_index)
        inputs = block_tokens.reshape(8 * L, D).astype(jnp.float32)

        def local_forward(values, weights):
            return forward(values, weights, block_segs, located)
        picked, pullback = jax.vjp(local_forward, inputs, params)
        input_grad, weight_grads = pullback(block_grad.astype(jnp.float32))
        totals = jax.tree.map(jnp.add, totals, weight_grads)
        return (totals, (picked.astype(jnp.bfloat16), input_grad.astype(jnp.bfloat16).reshape(8, L, D)))
    zeros = jax.tree.map(jnp.zeros_like, params)
    totals, stacked = lax.scan(group_step, zeros, (token_groups, seg_groups, index_groups, grad_groups))
    picked_all, input_all = stacked
    targets = jnp.moveaxis(picked_all, 0, 1).reshape(BLOCKS, IMAGES, TGT, D)
    tokens_grad = input_all.reshape(ROWS, L, D)
    return (targets, tokens_grad, totals[0], totals[1], totals[2], totals[3], totals[4], totals[5], totals[6], totals[7], totals[8], totals[9], totals[10], totals[11], totals[12])
```

```python
import jax
import jax.numpy as jnp
from jax import lax
from jax.sharding import PartitionSpec as P

HEADS = 12
HEAD_DIM = 64
AXES = ("rows", "blk")

norm_eps = 1e-06
score_scale = 0.125
neg_large = -1e30


def layer_norm(values, norm_gain, norm_shift):
    center = values - jnp.mean(values, axis=-1, keepdims=True)
    spread = jnp.mean(center * center, axis=-1, keepdims=True)
    return center * lax.rsqrt(spread + norm_eps) * norm_gain + norm_shift


def gelu_exact(values):
    return jax.nn.gelu(values, approximate=False)


class Exchange:
    def __init__(self, rows, blk):
        self.blk = blk
        self.total = rows * blk
        bits = self.total.bit_length() - 1
        assert self.total == 1 << bits and blk == 4
        order = list(range(1, bits))
        self.orders = (order, [order[1], order[0]] + order[2:])
        self.here = lax.axis_index("rows") * blk + lax.axis_index("blk")
        self.core = self.here & 1
        self.steps = len(order)

    def pairs(self, masks):
        return [(i, i ^ masks[i & 1]) for i in range(self.total)]

    def move_core(self, value):
        return lax.ppermute(value, AXES, self.pairs((1, 1)))

    def move(self, step, value):
        masks = tuple(1 << order[step] for order in self.orders)
        return lax.ppermute(value, AXES, self.pairs(masks))

    def bit(self, step):
        first, second = (self.here >> order[step] & 1 for order in self.orders)
        return jnp.where(self.core == 0, first, second)

    def scatter(self, local):
        n = local.shape[0]
        terms = [(local, 0)]
        for step in range(-1, self.steps):
            n //= 2
            bit = self.core if step < 0 else self.bit(step)
            send = self.total_of(terms, (1 - bit) * n, n)
            recv = self.move_core(send) if step < 0 else self.move(step, send)
            terms = [(t, off + bit * n) for t, off in terms] + [(recv, 0)]
        return self.total_of(terms, 0, n)

    def total_of(self, terms, shift, n):
        parts = [
            lax.dynamic_slice_in_dim(t, off + shift, n, 0).astype(jnp.float32) for t, off in terms
        ]
        return sum(parts[1:], parts[0]).astype(jnp.bfloat16)

    def gather(self, piece):
        for step in reversed(range(self.steps)):
            piece = self.join(self.bit(step), piece, self.move(step, piece))
        other = self.move_core(piece)
        low = self.core == 0
        return jnp.where(low, piece, other), jnp.where(low, other, piece)

    def join(self, bit, mine, other):
        low = bit == 0
        return jnp.concatenate([jnp.where(low, mine, other), jnp.where(low, other, mine)], axis=0)

    def small_sum(self, value):
        for step in range(self.steps + 1):
            value = value + lax.ppermute(value, AXES, self.pairs((1 << step, 1 << step)))
        return value

    def swap_blocks(self, pieces):
        mine = self.here & (self.blk - 1)
        got = [lax.dynamic_index_in_dim(pieces, mine, 0, keepdims=False)]
        for hop in range(1, self.blk):
            send = lax.dynamic_index_in_dim(pieces, mine ^ hop, 0, keepdims=False)
            got.append(lax.ppermute(send, AXES, self.pairs((hop, hop))))
        stacked = jnp.stack(got)
        return jnp.stack(
            [
                lax.dynamic_index_in_dim(stacked, mine ^ k, 0, keepdims=False)
                for k in range(self.blk)
            ]
        )


def token_rows(segments, patches):
    count_rows = segments.shape[0]
    length = segments.shape[1]
    images = patches.shape[0]
    per_row = images // count_rows
    slot_ids = jnp.arange(per_row, dtype=jnp.int32)
    before = (segments[:, None, :] >= 0) & (segments[:, None, :] < slot_ids[None, :, None])
    starts = jnp.sum(before.astype(jnp.int32), axis=2)
    offset = jnp.arange(count_rows, dtype=jnp.int32)[:, None] * length + starts
    located = offset.reshape(images)[:, None, None] + patches
    return jnp.transpose(located, (1, 0, 2))


def local(
    mesh_rows,
    mesh_blk,
    tokens,
    seg_ids,
    target_index,
    qkv_weight,
    q_bias,
    v_bias,
    out_weight,
    out_bias,
    norm1_gain,
    norm1_shift,
    norm2_gain,
    norm2_shift,
    fc1_weight,
    fc1_bias,
    fc2_weight,
    fc2_bias,
    target_grad,
):
    ex = Exchange(mesh_rows, mesh_blk)
    count_rows, length, columns = tokens.shape
    tokens_here = count_rows * length
    shaped = (count_rows, length, HEADS, HEAD_DIM)
    blocks, images, patches = target_grad.shape[0] * mesh_blk, target_grad.shape[1], target_grad.shape[2]
    per_device = images // mesh_blk
    returned = ex.swap_blocks(target_grad.reshape(mesh_blk, per_device, patches, columns))
    inputs = tokens.reshape(tokens_here, columns).astype(jnp.float32)
    normed = layer_norm(inputs, norm1_gain, norm1_shift).astype(jnp.bfloat16)
    joint_out = jnp.dot(normed, qkv_weight, preferred_element_type=jnp.float32)
    bias_joint = jnp.concatenate([q_bias, jnp.zeros_like(q_bias), v_bias])
    joint_low = (joint_out + bias_joint).astype(jnp.bfloat16)
    queries = joint_low[:, :columns].reshape(shaped)
    keys_all = joint_low[:, columns : 2 * columns].reshape(shaped)
    values_all = joint_low[:, 2 * columns :].reshape(shaped)
    scores = (
        jnp.einsum("rqhd,rkhd->rhqk", queries, keys_all, preferred_element_type=jnp.float32)
        * score_scale
    )
    allowed = (seg_ids[:, :, None] == seg_ids[:, None, :])[:, None]
    scores = jnp.where(allowed, scores, neg_large)
    row_peak = jnp.max(scores, axis=-1, keepdims=True)
    raised = jnp.exp(scores - row_peak)
    attn_prob = raised / jnp.sum(raised, axis=-1, keepdims=True)
    prob_low = attn_prob.astype(jnp.bfloat16)
    mixed_low = jnp.einsum(
        "rhqk,rkhd->rqhd", prob_low, values_all, preferred_element_type=jnp.float32
    )
    mixed_low = mixed_low.reshape(tokens_here, columns).astype(jnp.bfloat16)
    middle = inputs + (
        jnp.dot(mixed_low, out_weight, preferred_element_type=jnp.float32) + out_bias
    )
    second_norm = layer_norm(middle, norm2_gain, norm2_shift).astype(jnp.bfloat16)
    hidden = jnp.dot(second_norm, fc1_weight, preferred_element_type=jnp.float32) + fc1_bias
    active = gelu_exact(hidden).astype(jnp.bfloat16)
    output = middle + (jnp.dot(active, fc2_weight, preferred_element_type=jnp.float32) + fc2_bias)
    located = token_rows(seg_ids, target_index)
    flat_index = located.reshape(-1)
    onehot = (
        flat_index[:, None] == jnp.arange(tokens_here, dtype=jnp.int32)[None, :]
    ).astype(jnp.bfloat16)
    picked = jnp.einsum(
        "jn,nd->jd", onehot, output.astype(jnp.bfloat16), preferred_element_type=jnp.float32
    ).astype(jnp.bfloat16)
    targets = ex.swap_blocks(picked.reshape(located.shape + (columns,)))
    targets = targets.reshape(1, images, patches, columns)
    out_grad = jnp.einsum(
        "jn,jd->nd", onehot, returned.reshape(-1, columns), preferred_element_type=jnp.float32
    )
    mlp_low = out_grad.astype(jnp.bfloat16)
    fc2_weight_grad = jnp.einsum("nf,nd->fd", active, mlp_low, preferred_element_type=jnp.float32)
    fc2_bias_grad = jnp.sum(mlp_low.astype(jnp.float32), axis=0)
    active_grad = jnp.einsum("nd,fd->nf", mlp_low, fc2_weight, preferred_element_type=jnp.float32)
    _, gelu_pull = jax.vjp(gelu_exact, hidden)
    hidden_low = gelu_pull(active_grad)[0].astype(jnp.bfloat16)
    ff = fc1_weight.shape[1]
    tiles = ff // columns
    fc1_tiles = [
        jnp.einsum(
            "nd,nf->df",
            second_norm,
            hidden_low[:, k * columns : (k + 1) * columns],
            preferred_element_type=jnp.float32,
        ).astype(jnp.bfloat16)
        for k in range(tiles)
    ]
    fc2_low = fc2_weight_grad.astype(jnp.bfloat16)
    half = tiles // 2
    mlp_sums = []
    for k in range(2):
        chunk = jnp.concatenate(
            [fc2_low[k * half * columns : (k + 1) * half * columns]]
            + fc1_tiles[k * half : (k + 1) * half],
            axis=0,
        )
        mlp_sums.append(ex.gather(ex.scatter(chunk)))
    fc1_bias_grad = jnp.sum(hidden_low.astype(jnp.float32), axis=0)
    second_grad = jnp.einsum(
        "nf,df->nd", hidden_low, fc1_weight, preferred_element_type=jnp.float32
    )
    _, second_pull = jax.vjp(layer_norm, middle, norm2_gain, norm2_shift)
    middle_part, norm2_gain_grad, norm2_shift_grad = second_pull(second_grad)
    middle_grad = out_grad + middle_part
    branch_low = middle_grad.astype(jnp.bfloat16)
    out_weight_grad = jnp.einsum(
        "nd,ne->de", mixed_low, branch_low, preferred_element_type=jnp.float32
    )
    out_bias_grad = jnp.sum(branch_low.astype(jnp.float32), axis=0)
    mixed_grad = jnp.einsum("ne,de->nd", branch_low, out_weight, preferred_element_type=jnp.float32)
    mixed_grad = mixed_grad.astype(jnp.bfloat16).reshape(shaped)
    prob_grad = jnp.einsum(
        "rqhd,rkhd->rhqk", mixed_grad, values_all, preferred_element_type=jnp.float32
    )
    center = jnp.sum(attn_prob * prob_grad, axis=-1, keepdims=True)
    score_low = (attn_prob * (prob_grad - center)).astype(jnp.bfloat16)
    query_grad = (
        jnp.einsum("rhqk,rkhd->rqhd", score_low, keys_all, preferred_element_type=jnp.float32)
        * score_scale
    )
    key_grad = (
        jnp.einsum("rhqk,rqhd->rkhd", score_low, queries, preferred_element_type=jnp.float32)
        * score_scale
    )
    value_grad = jnp.einsum(
        "rhqk,rqhd->rkhd", prob_low, mixed_grad, preferred_element_type=jnp.float32
    )
    joint_parts = [
        part.reshape(tokens_here, columns).astype(jnp.bfloat16)
        for part in (query_grad, key_grad, value_grad)
    ]
    chunk = jnp.concatenate(
        [
            jnp.einsum("nd,ne->de", normed, part, preferred_element_type=jnp.float32).astype(
                jnp.bfloat16
            )
            for part in joint_parts
        ]
        + [out_weight_grad.astype(jnp.bfloat16)],
        axis=0,
    )
    first_half, second_half = ex.gather(ex.scatter(chunk))
    joint_grad_low = jnp.concatenate(joint_parts, axis=1)
    q_bias_grad = jnp.sum(joint_parts[0].astype(jnp.float32), axis=0)
    v_bias_grad = jnp.sum(joint_parts[2].astype(jnp.float32), axis=0)
    normed_grad = jnp.einsum(
        "ne,de->nd", joint_grad_low, qkv_weight, preferred_element_type=jnp.float32
    )
    _, first_pull = jax.vjp(layer_norm, inputs, norm1_gain, norm1_shift)
    input_part, norm1_gain_grad, norm1_shift_grad = first_pull(normed_grad)
    tokens_grad = (
        (middle_grad + input_part).astype(jnp.bfloat16).reshape(count_rows, length, columns)
    )
    vectors = [
        q_bias_grad,
        v_bias_grad,
        out_bias_grad,
        norm1_gain_grad,
        norm1_shift_grad,
        norm2_gain_grad,
        norm2_shift_grad,
        fc2_bias_grad,
    ]
    small = jnp.concatenate(
        [jnp.stack(vectors), fc1_bias_grad.reshape(tiles, columns)], axis=0
    )
    small = ex.small_sum(small)
    f32 = jnp.float32
    fc2_full = jnp.concatenate([pair[0] for pair in mlp_sums], axis=0).astype(f32)
    fc1_full = jnp.concatenate(
        [
            pair[1][k * columns : (k + 1) * columns]
            for pair in mlp_sums
            for k in range(half)
        ],
        axis=1,
    ).astype(f32)
    qkv_full = jnp.concatenate(
        [first_half[:columns], first_half[columns:], second_half[:columns]], axis=1
    ).astype(f32)
    out_full = second_half[columns:].astype(f32)
    count = len(vectors)
    return (
        targets,
        tokens_grad,
        qkv_full,
        small[0],
        small[1],
        out_full,
        small[2],
        small[3],
        small[4],
        small[5],
        small[6],
        fc1_full,
        small[count:].reshape(ff),
        fc2_full,
        small[7],
    )


def solution(mesh):
    rows, blk = mesh.shape["rows"], mesh.shape["blk"]

    def body(*args):
        return local(rows, blk, *args)

    return jax.shard_map(
        body,
        mesh=mesh,
        in_specs=(
            P(("rows", "blk"), None, None),
            P(("rows", "blk"), None),
            P(("rows", "blk"), None, None),
        )
        + (P(),) * 13
        + (P("blk", "rows", None, None),),
        out_specs=(
            P("blk", "rows", None, None),
            P(("rows", "blk"), None, None),
        )
        + (P(),) * 13,
        check_vma=False,
    )
```

```python
import functools

import jax
import jax.numpy as jnp
from jax import lax
from jax.experimental import pallas as pl
from jax.experimental.pallas import tpu as pltpu
from jax.sharding import PartitionSpec as P

HEADS = 12
HEAD_DIM = 64
GROUP = 4
WIDE = GROUP * HEAD_DIM
AXES = ("rows", "blk")
F32 = jnp.float32
BF16 = jnp.bfloat16

norm_eps = 1e-06
score_scale = 0.125
neg_large = -1e30


def dot(a, b):
    return lax.dot_general(a, b, (((1,), (0,)), ((), ())), preferred_element_type=F32)


def dot_nt(a, b):
    return lax.dot_general(a, b, (((1,), (1,)), ((), ())), preferred_element_type=F32)


def dot_tn(a, b):
    return lax.dot_general(a, b, (((0,), (0,)), ((), ())), preferred_element_type=F32)


def standardize(values):
    center = values - jnp.mean(values, axis=-1, keepdims=True)
    spread = jnp.mean(center * center, axis=-1, keepdims=True)
    scale = lax.rsqrt(spread + norm_eps)
    return center * scale, scale


def norm_back(grad, xhat, scale, gain):
    e = grad * gain
    mean_e = jnp.mean(e, axis=-1, keepdims=True)
    mean_ex = jnp.mean(e * xhat, axis=-1, keepdims=True)
    return (e - mean_e - xhat * mean_ex) * scale


def head_mask(rows, h):
    lane = lax.broadcasted_iota(jnp.int32, (rows, WIDE), 1)
    return (lane >= h * HEAD_DIM) & (lane < (h + 1) * HEAD_DIM)


def vec(ref):
    return ref[...].reshape(1, -1)


def stack_heads(values, length):
    return jnp.concatenate(
        [jnp.where(head_mask(length, h), values, jnp.zeros_like(values)) for h in range(GROUP)],
        axis=0,
    )


def unstack_heads(stacked, length):
    total = stacked[:length]
    for h in range(1, GROUP):
        total = jnp.where(head_mask(length, h), stacked[h * length : (h + 1) * length], total)
    return total


def attend_kernel(
    tok, seg, wq, wk, wv, wo, qb, vb, ob, g1, s1, g2, s2,
    normed_o, q_o, k_o, v_o, p_o, mixed_o, middle_o, second_o,
    acc, score_s, biases,
):
    step = pl.program_id(0)
    length, width = tok.shape
    cols = pl.ds(pl.multiple_of(step * WIDE, WIDE), WIDE)

    @pl.when(step == 0)
    def _():
        xhat, _ = standardize(tok[...].astype(F32))
        normed_o[...] = (xhat * vec(g1) + vec(s1)).astype(BF16)
        acc[...] = jnp.zeros_like(acc)
        biases[0:1, :] = vec(qb)
        biases[1:2, :] = vec(vb)

    normed = normed_o[...]
    q = (dot(normed, wq[...]) + biases[0:1, cols]).astype(BF16)
    k = dot(normed, wk[...]).astype(BF16)
    v = (dot(normed, wv[...]) + biases[1:2, cols]).astype(BF16)
    q_o[...] = q
    k_o[...] = k
    v_o[...] = v
    score_s[...] = dot_nt(q * jnp.asarray(score_scale, BF16), stack_heads(k, length))
    seg_row = seg[...]
    seg_col = jnp.broadcast_to(seg_row.astype(F32), (128, length)).T[:, :1].astype(jnp.int32)
    rows = 64
    for top in range(0, length, rows):
        at = slice(top, top + rows)
        allowed = seg_col[at] == seg_row
        for h in range(GROUP):
            span = slice(h * length, (h + 1) * length)
            scores = jnp.where(allowed, score_s[at, span], neg_large)
            raised = jnp.exp(scores - jnp.max(scores, axis=-1, keepdims=True))
            share = 1.0 / jnp.sum(raised, axis=-1, keepdims=True)
            p_o[0, at, span] = (raised * share).astype(BF16)
    mixed = dot(p_o[0], stack_heads(v, length)).astype(BF16)
    mixed_o[...] = mixed
    acc[...] += dot(mixed, wo[...])

    @pl.when(step == pl.num_programs(0) - 1)
    def _():
        middle = tok[...].astype(F32) + (acc[...] + vec(ob))
        middle_o[...] = middle
        xhat, _ = standardize(middle)
        second_o[...] = (xhat * vec(g2) + vec(s2)).astype(BF16)


def located(seg, tgt, blocks, length):
    rows = []
    starts = [
        jnp.sum(((seg[...] >= 0) & (seg[...] < image)).astype(jnp.int32))
        for image in range(tgt.shape[0])
    ]
    for block in blocks:
        for image, start in enumerate(starts):
            rows.append(tgt[image, pl.ds(block, 1), :] + start)
    row = jnp.concatenate(rows, axis=1)
    slots = lax.broadcasted_iota(jnp.int32, (length, row.shape[1]), 0)
    return (slots == row).astype(F32).astype(BF16)


def tile_bias(bias_s, skip, width):
    start = (pl.program_id(0) + skip) * width
    return bias_s[:, pl.ds(pl.multiple_of(start, width), width)]


def mlp_steps(info, sn, low, w1, w2, bias, keep_o, send_o, out_o, grad_o, b1_o, both):
    width = low.shape[1]
    piece = 256
    for j in range(width // piece):
        cols = slice(j * piece, (j + 1) * piece)
        hidden = dot(sn, w1[:, cols]) + bias[:, cols]
        phi_cum = 0.5 + 0.5 * lax.erf(hidden * 0.7071067811865476)
        density = 0.3989422804014327 * jnp.exp(hidden * hidden * -0.5)
        active = (hidden * phi_cum).astype(BF16)
        hidden_grad = dot_nt(low, w2[cols, :]) * (phi_cum + hidden * density)
        hidden_low = hidden_grad.astype(BF16)
        b1_o[:, cols] = jnp.sum(hidden_low.astype(F32), axis=0, keepdims=True)
        both[0, cols, :] = dot_tn(active, low).astype(BF16)
        both[1, :, cols] = dot_tn(sn, hidden_low).astype(BF16)
        out_o[...] += dot(active, w2[cols, :])
        grad_o[...] += dot_nt(hidden_low, w1[:, cols])
    first = info[1] == 0
    keep_o[0] = jnp.where(first, both[0], both[1])
    send_o[0] = jnp.where(first, both[1], both[0])


def first_mlp_kernel(
    info, second, seg, tgt, own, got1, got2, got3, w1, w2, b1,
    keep_o, send_o, out_o, grad_o, b1_o, out_grad_o, mlp_o, bias_o,
    both, bias_s,
):
    @pl.when(pl.program_id(0) == 0)
    def _():
        bias_s[...] = vec(b1)
        me = info[0]
        places = located(seg, tgt, [me, me ^ 1, me ^ 2, me ^ 3], second.shape[0])
        pieces = jnp.concatenate([own[...], got1[...], got2[...], got3[...]], axis=0)
        total = dot(places, pieces)
        out_grad_o[...] = total
        low = total.astype(BF16)
        mlp_o[...] = low
        bias_o[...] = jnp.sum(low.astype(F32), axis=0, keepdims=True)
        out_o[...] = jnp.zeros_like(out_o)
        grad_o[...] = jnp.zeros_like(grad_o)

    bias = tile_bias(bias_s, 0, second.shape[1])
    mlp_steps(info, second[...], mlp_o[...], w1, w2, bias, keep_o, send_o, out_o, grad_o, b1_o, both)


def second_mlp_kernel(
    info, second, mlp, w1, w2, b1, out_in, grad_in, middle, out_grad, gain,
    keep_o, send_o, out_o, b1_o, middle_grad_o, branch_o, gain_o, shift_o, bias_o,
    both, grad_s, bias_s,
):
    step = pl.program_id(0)

    @pl.when(step == 0)
    def _():
        bias_s[...] = vec(b1)
        out_o[...] = out_in[...]
        grad_s[...] = grad_in[...]

    bias = tile_bias(bias_s, pl.num_programs(0), second.shape[1])
    mlp_steps(info, second[...], mlp[...], w1, w2, bias, keep_o, send_o, out_o, grad_s, b1_o, both)

    @pl.when(step == pl.num_programs(0) - 1)
    def _():
        grad = grad_s[...]
        xhat, scale = standardize(middle[...])
        gain_o[...] = jnp.sum(grad * xhat, axis=0, keepdims=True)
        shift_o[...] = jnp.sum(grad, axis=0, keepdims=True)
        middle_grad = out_grad[...] + norm_back(grad, xhat, scale, vec(gain))
        middle_grad_o[...] = middle_grad
        branch = middle_grad.astype(BF16)
        branch_o[...] = branch
        bias_o[...] = jnp.sum(branch.astype(F32), axis=0, keepdims=True)


def attend_back_kernel(
    info, normed, mixed, branch, q, k, v, p, wo,
    keep_o, send_o, dq_o, dk_o, dv_o, qb_o, vb_o,
    grad_s, score_s, both,
):
    step = pl.program_id(0)
    length = normed.shape[0]
    mixed_grad = dot_nt(branch[...], wo[...]).astype(BF16)
    cols = pl.ds(pl.multiple_of(step * WIDE, WIDE), WIDE)
    grad_s[...] = dot_nt(mixed_grad, stack_heads(v[...], length))
    both[3] = dot_tn(mixed[...], branch[:, cols]).astype(BF16)
    dv = unstack_heads(dot_tn(p[0], mixed_grad), length).astype(BF16)
    rows = 64
    for top in range(0, length, rows):
        at = slice(top, top + rows)
        for h in range(GROUP):
            span = slice(h * length, (h + 1) * length)
            prob = p[0, at, span].astype(F32)
            weighted = prob * grad_s[at, span]
            center = jnp.sum(weighted, axis=-1, keepdims=True)
            score_s[at, span] = (weighted - prob * center).astype(BF16)
    dq = (dot(score_s[...], stack_heads(k[...], length)) * score_scale).astype(BF16)
    dk = (unstack_heads(dot_tn(score_s[...], q[...]), length) * score_scale).astype(BF16)
    dq_o[...] = dq
    dk_o[...] = dk
    dv_o[...] = dv
    qb_o[...] = jnp.sum(dq.astype(F32), axis=0, keepdims=True)
    vb_o[...] = jnp.sum(dv.astype(F32), axis=0, keepdims=True)
    both[0] = dot_tn(normed[...], dq).astype(BF16)
    both[1] = dot_tn(normed[...], dk).astype(BF16)
    both[2] = dot_tn(normed[...], dv).astype(BF16)
    first = info[1] == 0
    for t in range(2):
        keep_o[t] = jnp.where(first, both[t], both[2 + t])
        send_o[t] = jnp.where(first, both[2 + t], both[t])


def finish_kernel(
    tok, middle_grad, dq, dk, dv, wq, wk, wv, g1,
    middle, out_sum, b2, seg, tgt,
    qb, vb, ob, n2g, n2s, b2g, b1a, b1b,
    tokens_o, small_o, picked_o,
    acc,
):
    step = pl.program_id(0)

    @pl.when(step == 0)
    def _():
        acc[...] = jnp.zeros_like(acc)
        output = (middle[...] + (out_sum[...] + vec(b2))).astype(BF16)
        blocks, entries, width = picked_o.shape
        places = located(seg, tgt, list(range(blocks)), output.shape[0])
        picked = dot_tn(places, output).astype(BF16)
        picked_o[...] = picked.reshape(blocks, entries, width)

    acc[...] += dot_nt(dq[...], wq[...]) + dot_nt(dk[...], wk[...]) + dot_nt(dv[...], wv[...])

    @pl.when(step == pl.num_programs(0) - 1)
    def _():
        grad = acc[...]
        xhat, scale = standardize(tok[...].astype(F32))
        tokens_o[...] = (middle_grad[...] + norm_back(grad, xhat, scale, vec(g1))).astype(BF16)
        width = grad.shape[1]
        small_o[0:1, :] = qb[...]
        small_o[1:2, :] = vb[...]
        small_o[2:3, :] = ob[...]
        small_o[3:4, :] = jnp.sum(grad * xhat, axis=0, keepdims=True)
        small_o[4:5, :] = jnp.sum(grad, axis=0, keepdims=True)
        small_o[5:6, :] = n2g[...]
        small_o[6:7, :] = n2s[...]
        small_o[7:8, :] = b2g[...]
        row = 8
        for part in (b1a, b1b):
            for j in range(part.shape[1] // width):
                small_o[row : row + 1, :] = part[:, j * width : (j + 1) * width]
                row += 1


def call(kernel, grid, ins, outs, scratch=(), flops=0, bytes_=0, vmem=60):
    return pl.pallas_call(
        kernel,
        grid=grid,
        in_specs=[spec for spec in ins],
        out_specs=[spec for spec, _ in outs],
        out_shape=[shape for _, shape in outs],
        scratch_shapes=list(scratch),
        compiler_params=pltpu.CompilerParams(vmem_limit_bytes=vmem * 2**20),
        cost_estimate=pl.CostEstimate(flops=flops, bytes_accessed=bytes_, transcendentals=0),
    )


def full(*shape):
    return pl.BlockSpec(shape, lambda *_: (0,) * len(shape))


def block(shape, index):
    return pl.BlockSpec(shape, index)


def sds(shape, dtype):
    return jax.ShapeDtypeStruct(shape, dtype)


class Exchange:
    def __init__(self, rows, blk):
        self.blk = blk
        self.total = rows * blk
        bits = self.total.bit_length() - 1
        assert self.total == 1 << bits and blk == 4
        order = list(range(1, bits))
        self.orders = (order, [order[1], order[0]] + order[2:])
        self.here = lax.axis_index("rows") * blk + lax.axis_index("blk")
        self.core = self.here & 1
        self.steps = len(order)

    def pairs(self, masks):
        return [(i, i ^ masks[i & 1]) for i in range(self.total)]

    def move_core(self, value):
        return lax.ppermute(value, AXES, self.pairs((1, 1)))

    def move(self, step, value):
        masks = tuple(1 << order[step] for order in self.orders)
        return lax.ppermute(value, AXES, self.pairs(masks))

    def bit(self, step):
        first, second = (self.here >> order[step] & 1 for order in self.orders)
        return jnp.where(self.core == 0, first, second)

    def scatter(self, keep, send):
        n = keep.shape[0]
        terms = [(keep, 0), (self.move_core(send), 0)]
        for step in range(self.steps):
            n //= 2
            bit = self.bit(step)
            recv = self.move(step, self.total_of(terms, (1 - bit) * n, n))
            terms = [(t, off + bit * n) for t, off in terms] + [(recv, 0)]
        return self.total_of(terms, 0, n)

    def total_of(self, terms, shift, n):
        parts = [
            lax.dynamic_slice_in_dim(t, off + shift, n, 0).astype(jnp.float32) for t, off in terms
        ]
        return sum(parts[1:], parts[0]).astype(jnp.bfloat16)

    def gather(self, piece):
        for step in reversed(range(self.steps)):
            piece = self.join(self.bit(step), piece, self.move(step, piece))
        other = self.move_core(piece)
        low = self.core == 0
        return jnp.where(low, piece, other), jnp.where(low, other, piece)

    def join(self, bit, mine, other):
        low = bit == 0
        return jnp.concatenate([jnp.where(low, mine, other), jnp.where(low, other, mine)], axis=0)

    def small_sum(self, value):
        for step in range(self.steps + 1):
            value = value + lax.ppermute(value, AXES, self.pairs((1 << step, 1 << step)))
        return value

    def swap_blocks(self, pieces):
        mine = self.here & (self.blk - 1)
        got = [lax.dynamic_index_in_dim(pieces, mine, 0, keepdims=False)]
        for hop in range(1, self.blk):
            send = lax.dynamic_index_in_dim(pieces, mine ^ hop, 0, keepdims=False)
            got.append(lax.ppermute(send, AXES, self.pairs((hop, hop))))
        return got

    def in_order(self, got):
        mine = self.here & (self.blk - 1)
        low, high = mine & 1, mine >> 1
        pairs = [
            (jnp.where(low == 0, a, b), jnp.where(low == 0, b, a))
            for a, b in (got[:2], got[2:])
        ]
        first = [jnp.where(high == 0, a, b) for a, b in zip(pairs[0], pairs[1])]
        second = [jnp.where(high == 0, b, a) for a, b in zip(pairs[0], pairs[1])]
        return jnp.concatenate(first + second, axis=0)


def local(
    mesh_rows, mesh_blk,
    tokens, seg_ids, target_index,
    qkv_weight, q_bias, v_bias, out_weight, out_bias,
    norm1_gain, norm1_shift, norm2_gain, norm2_shift,
    fc1_weight, fc1_bias, fc2_weight, fc2_bias,
    target_grad,
):
    ex = Exchange(mesh_rows, mesh_blk)
    count_rows, length, d = tokens.shape
    assert count_rows == 1
    ff = fc1_weight.shape[1]
    tiles = ff // d
    images, patches = target_grad.shape[1], target_grad.shape[2]
    per = images // mesh_blk
    groups = d // WIDE
    pieces = target_grad.reshape(mesh_blk, per * patches, d)
    got = ex.swap_blocks(pieces)
    tok = tokens.reshape(length, d)
    seg = seg_ids
    col = lambda g: (0, g)
    third = lambda n: lambda g: (0, n * groups + g)
    act = sds((length, d), BF16)
    act32 = sds((length, d), F32)
    one = sds((1, d), F32)
    vd = full(d)
    smem = pl.BlockSpec(memory_space=pltpu.SMEM)
    whole = full(length, d)
    strip = block((length, WIDE), col)
    wide = GROUP * length
    wide_spec = block((1, length, wide), lambda g: (g, 0, 0))

    normed, q, k, v, prob, mixed, middle, second = call(
        attend_kernel,
        (groups,),
        [
            whole, full(1, length),
            block((d, WIDE), third(0)), block((d, WIDE), third(1)), block((d, WIDE), third(2)),
            block((WIDE, d), lambda g: (g, 0)),
            vd, vd, vd, vd, vd, vd, vd,
        ],
        [
            (whole, act), (strip, act), (strip, act), (strip, act),
            (wide_spec, sds((groups, length, wide), BF16)),
            (strip, act), (whole, act32), (whole, act),
        ],
        [
            pltpu.VMEM((length, d), F32),
            pltpu.VMEM((length, wide), F32),
            pltpu.VMEM((2, d), F32),
        ],
        flops=4 * 10**9, bytes_=12 * 10**6,
    )(
        tok, seg, qkv_weight, qkv_weight, qkv_weight, out_weight, q_bias, v_bias, out_bias,
        norm1_gain, norm1_shift, norm2_gain, norm2_shift,
    )

    info = jnp.stack([ex.here & (mesh_blk - 1), ex.core]).astype(jnp.int32)
    half = tiles // 2

    def mlp_specs(part):
        return [
            block((d, d), lambda j: (0, part * half + j)),
            block((d, d), lambda j: (part * half + j, 0)),
            full(ff),
        ]

    tile_spec = block((1, d, d), lambda j: (j, 0, 0))
    tile_out = (tile_spec, sds((half, d, d), BF16))
    b1_out = (block((1, d), col), sds((1, half * d), F32))
    both = pltpu.VMEM((2, d, d), BF16)
    piece = full(per * patches, d)
    keep1, send1, out_sum, second_grad, b1a, out_grad, mlp_low, b2_grad = call(
        first_mlp_kernel,
        (half,),
        [smem, whole, full(1, length), full(*target_index.shape)] + [piece] * 4 + mlp_specs(0),
        [
            tile_out, tile_out, (whole, act32), (whole, act32), b1_out,
            (whole, act32), (whole, act), (full(1, d), one),
        ],
        [both, pltpu.VMEM((1, ff), F32)],
        flops=6 * 10**9, bytes_=12 * 10**6,
    )(info, second, seg, target_index, *got, fc1_weight, fc2_weight, fc1_bias)
    keep2, send2, out_sum, b1b, middle_grad, branch, n2g, n2s, ob_grad = call(
        second_mlp_kernel,
        (half,),
        [smem, whole, whole] + mlp_specs(1) + [whole] * 4 + [vd],
        [
            tile_out, tile_out, (whole, act32), b1_out,
            (whole, act32), (whole, act), (full(1, d), one), (full(1, d), one), (full(1, d), one),
        ],
        [both, pltpu.VMEM((length, d), F32), pltpu.VMEM((1, ff), F32)],
        flops=6 * 10**9, bytes_=12 * 10**6,
    )(
        info, second, mlp_low, fc1_weight, fc2_weight, fc1_bias,
        out_sum, second_grad, middle, out_grad, norm2_gain,
    )

    pair_out = (block((2, d, WIDE), lambda g: (0, 0, g)), sds((2, d, d), BF16))
    keep3, send3, dq, dk, dv, qb_grad, vb_grad = call(
        attend_back_kernel,
        (groups,),
        [
            smem, whole, whole, whole, strip, strip, strip, wide_spec,
            block((WIDE, d), lambda g: (g, 0)),
        ],
        [
            pair_out, pair_out, (strip, act), (strip, act), (strip, act),
            (block((1, WIDE), col), one), (block((1, WIDE), col), one),
        ],
        [
            pltpu.VMEM((length, wide), F32),
            pltpu.VMEM((length, wide), BF16),
            pltpu.VMEM((4, d, WIDE), BF16),
        ],
        flops=6 * 10**9, bytes_=12 * 10**6,
    )(info, normed, mixed, branch, q, k, v, prob, out_weight)

    tokens_grad, small, picked = call(
        finish_kernel,
        (groups,),
        [
            whole, whole, strip, strip, strip,
            block((d, WIDE), third(0)), block((d, WIDE), third(1)), block((d, WIDE), third(2)),
            vd, whole, whole, vd, full(1, length), full(*target_index.shape),
        ]
        + [full(1, d)] * 6 + [full(1, half * d)] * 2,
        [
            (whole, act),
            (full(8 + tiles, d), sds((8 + tiles, d), F32)),
            (full(mesh_blk, per * patches, d), sds((mesh_blk, per * patches, d), BF16)),
        ],
        [pltpu.VMEM((length, d), F32)],
        flops=2 * 10**9, bytes_=10 * 10**6,
    )(
        tok, middle_grad, dq, dk, dv, qkv_weight, qkv_weight, qkv_weight, norm1_gain,
        middle, out_sum, fc2_bias, seg, target_index,
        qb_grad, vb_grad, ob_grad, n2g, n2s, b2_grad, b1a, b1b,
    )

    sums = [
        ex.gather(ex.scatter(keep.reshape(2 * d, d), send.reshape(2 * d, d)))
        for keep, send in ((keep1, send1), (keep2, send2), (keep3, send3))
    ]
    small = ex.small_sum(small)
    targets = ex.in_order(ex.swap_blocks(picked)).reshape(1, images, patches, d)

    mlp_sums, (qk, vo) = sums[:2], sums[2]
    fc2_full = jnp.concatenate([pair[0] for pair in mlp_sums], axis=0).astype(F32)
    fc1_full = jnp.concatenate(
        [pair[1][j * d : (j + 1) * d] for pair in mlp_sums for j in range(half)], axis=1
    ).astype(F32)
    qkv_full = jnp.concatenate([qk[:d], qk[d:], vo[:d]], axis=1).astype(F32)
    out_full = vo[d:].astype(F32)
    return (
        targets,
        tokens_grad.reshape(count_rows, length, d),
        qkv_full,
        small[0], small[1],
        out_full,
        small[2], small[3], small[4], small[5], small[6],
        fc1_full,
        small[8:].reshape(ff),
        fc2_full,
        small[7],
    )


def solution(mesh):
    rows, blk = mesh.shape["rows"], mesh.shape["blk"]

    def body(*args):
        return local(rows, blk, *args)

    return jax.shard_map(
        body,
        mesh=mesh,
        in_specs=(
            P(("rows", "blk"), None, None),
            P(("rows", "blk"), None),
            P(("rows", "blk"), None, None),
        )
        + (P(),) * 13
        + (P("blk", "rows", None, None),),
        out_specs=(
            P("blk", "rows", None, None),
            P(("rows", "blk"), None, None),
        )
        + (P(),) * 13,
        check_vma=False,
    )
```

```python
import functools

import jax
import jax.numpy as jnp
from jax import lax
from jax.experimental import pallas as pl
from jax.experimental.pallas import tpu as pltpu
from jax.sharding import PartitionSpec as P

HEADS = 12
HEAD_DIM = 64
GROUP = 4
WIDE = GROUP * HEAD_DIM
LEVELS = 4
PACE = 10
STEP = 4
MOVE = 10
SPANS = 8
AXES = ("rows", "blk")
SCHEDULE = (
    "K0", "K1", "M1 c", "K2a", "M1 r0", "K2b", "M2 c", "K3", "M1 r1", "M2 r0", "Q c", "K4",
    "s", "T", "M1 r2", "Q r0", "M2 r1", "S", "s", "M1 r3", "M1 f", "M1 g0", "M1 g1", "M2 r2",
    "Q r1", "M1 g2", "S", "s", "Q r2", "M1 j", "M1 cA", "M1 g3", "M1 g4", "M2 r3", "S", "s",
    "Q r3", "M1 g5", "M1 cB", "M1 cC", "M2 f", "M2 g0", "M1 vAB", "M2 g1", "M1 cD", "Q f", "Q g0", "M1 vCD",
    "M2 g2", "Q g1", "Q g2", "S", "s", "M2 j", "M2 cA", "M2 g3", "M2 g4", "Q j", "Q cA", "Q g3",
    "Q g4", "S", "t", "M2 g5", "M2 cB", "M2 vAB", "M2 cC", "Q g5", "Q cB", "Q cC", "Q vAB", "M2 cD",
    "M2 vCD", "Q cD", "Q vCD",
)
ORDERS = (((0, 1, 2, 3), (1, 0, 2, 3)), ((0, 1, 2, 3), (1, 0, 2, 3)), ((0, 1, 2, 3), (1, 0, 2, 3)))
F32 = jnp.float32
BF16 = jnp.bfloat16

norm_eps = 1e-06
score_scale = 0.125
neg_large = -1e30


def dot(a, b):
    return lax.dot_general(a, b, (((1,), (0,)), ((), ())), preferred_element_type=F32)


def dot_nt(a, b):
    return lax.dot_general(a, b, (((1,), (1,)), ((), ())), preferred_element_type=F32)


def dot_tn(a, b):
    return lax.dot_general(a, b, (((0,), (0,)), ((), ())), preferred_element_type=F32)


def standardize(values):
    center = values - jnp.mean(values, axis=-1, keepdims=True)
    spread = jnp.mean(center * center, axis=-1, keepdims=True)
    scale = lax.rsqrt(spread + norm_eps)
    return center * scale, scale


def norm_back(grad, xhat, scale, gain):
    e = grad * gain
    mean_e = jnp.mean(e, axis=-1, keepdims=True)
    mean_ex = jnp.mean(e * xhat, axis=-1, keepdims=True)
    return (e - mean_e - xhat * mean_ex) * scale


def head_mask(rows, h):
    lane = lax.broadcasted_iota(jnp.int32, (rows, WIDE), 1)
    return (lane >= h * HEAD_DIM) & (lane < (h + 1) * HEAD_DIM)


def vec(ref):
    return ref[...].reshape(1, -1)


def stack_heads(values, length):
    return jnp.concatenate(
        [jnp.where(head_mask(length, h), values, jnp.zeros_like(values)) for h in range(GROUP)],
        axis=0,
    )


def unstack_heads(stacked, length):
    total = stacked[:length]
    for h in range(1, GROUP):
        total = jnp.where(head_mask(length, h), stacked[h * length : (h + 1) * length], total)
    return total


def attend_kernel(
    tok, seg, wq, wk, wv, wo, qb, vb, ob, g1, s1, g2, s2,
    normed_o, q_o, k_o, v_o, p_o, mixed_o, middle_o, second_o,
    acc, score_s, biases,
):
    step = pl.program_id(0)
    length, width = tok.shape
    cols = pl.ds(pl.multiple_of(step * WIDE, WIDE), WIDE)

    @pl.when(step == 0)
    def _():
        xhat, _ = standardize(tok[...].astype(F32))
        normed_o[...] = (xhat * vec(g1) + vec(s1)).astype(BF16)
        acc[...] = jnp.zeros_like(acc)
        biases[0:1, :] = vec(qb)
        biases[1:2, :] = vec(vb)

    normed = normed_o[...]
    q = (dot(normed, wq[...]) + biases[0:1, cols]).astype(BF16)
    k = dot(normed, wk[...]).astype(BF16)
    v = (dot(normed, wv[...]) + biases[1:2, cols]).astype(BF16)
    q_o[...] = q
    k_o[...] = k
    v_o[...] = v
    score_s[...] = dot_nt(q * jnp.asarray(score_scale, BF16), stack_heads(k, length))
    seg_row = seg[...]
    seg_col = jnp.broadcast_to(seg_row.astype(F32), (128, length)).T[:, :1].astype(jnp.int32)
    rows = 64
    for top in range(0, length, rows):
        at = slice(top, top + rows)
        allowed = seg_col[at] == seg_row
        for h in range(GROUP):
            span = slice(h * length, (h + 1) * length)
            scores = jnp.where(allowed, score_s[at, span], neg_large)
            raised = jnp.exp(scores - jnp.max(scores, axis=-1, keepdims=True))
            share = 1.0 / jnp.sum(raised, axis=-1, keepdims=True)
            p_o[0, at, span] = (raised * share).astype(BF16)
    mixed = dot(p_o[0], stack_heads(v, length)).astype(BF16)
    mixed_o[...] = mixed
    acc[...] += dot(mixed, wo[...])

    @pl.when(step == pl.num_programs(0) - 1)
    def _():
        middle = tok[...].astype(F32) + (acc[...] + vec(ob))
        middle_o[...] = middle
        xhat, _ = standardize(middle)
        second_o[...] = (xhat * vec(g2) + vec(s2)).astype(BF16)


def located(seg, tgt, blocks, length):
    rows = []
    starts = [
        jnp.sum(((seg[...] >= 0) & (seg[...] < image)).astype(jnp.int32))
        for image in range(tgt.shape[0])
    ]
    for block in blocks:
        for image, start in enumerate(starts):
            rows.append(tgt[image, pl.ds(block, 1), :] + start)
    row = jnp.concatenate(rows, axis=1)
    slots = lax.broadcasted_iota(jnp.int32, (length, row.shape[1]), 0)
    return (slots == row).astype(F32).astype(BF16)


def tile_bias(bias_s, skip, width):
    start = (pl.program_id(0) + skip) * width
    return bias_s[:, pl.ds(pl.multiple_of(start, width), width)]


def relative_store(info, pair, keep_o, send_o, keep_at, send_at, height):
    first = info[1] == 0
    rows = height // SPANS
    for n in range(SPANS):
        low, high = pair(slice(n * rows, (n + 1) * rows))
        keep_o[keep_at, pl.ds(pl.multiple_of((n ^ info[3]) * rows, rows), rows), :] = jnp.where(first, low, high)
        send_o[send_at, pl.ds(pl.multiple_of((n ^ info[5]) * rows, rows), rows), :] = jnp.where(first, high, low)


def mlp_steps(info, sn, low, w1, w2, bias, keep_o, send_o, out_o, grad_o, b1_o, both):
    width = low.shape[1]
    piece = 256
    for j in range(width // piece):
        cols = slice(j * piece, (j + 1) * piece)
        hidden = dot(sn, w1[:, cols]) + bias[:, cols]
        phi_cum = 0.5 + 0.5 * lax.erf(hidden * 0.7071067811865476)
        density = 0.3989422804014327 * jnp.exp(hidden * hidden * -0.5)
        active = (hidden * phi_cum).astype(BF16)
        hidden_grad = dot_nt(low, w2[cols, :]) * (phi_cum + hidden * density)
        hidden_low = hidden_grad.astype(BF16)
        b1_o[:, cols] = jnp.sum(hidden_low.astype(F32), axis=0, keepdims=True)
        both[0, cols, :] = dot_tn(active, low).astype(BF16)
        both[1, :, cols] = dot_tn(sn, hidden_low).astype(BF16)
        out_o[...] += dot(active, w2[cols, :])
        grad_o[...] += dot_nt(hidden_low, w1[:, cols])
    relative_store(info, lambda rows: (both[0, rows], both[1, rows]), keep_o, send_o, 0, 0, width)


def first_mlp_kernel(
    info, second, seg, tgt, own, got1, got2, got3, w1, w2, b1,
    keep_o, send_o, out_o, grad_o, b1_o, out_grad_o, mlp_o, bias_o,
    both, bias_s,
):
    @pl.when(pl.program_id(0) == 0)
    def _():
        bias_s[...] = vec(b1)
        me = info[0]
        places = located(seg, tgt, [me, me ^ 1, me ^ 2, me ^ 3], second.shape[0])
        pieces = jnp.concatenate([own[...], got1[...], got2[...], got3[...]], axis=0)
        total = dot(places, pieces)
        out_grad_o[...] = total
        low = total.astype(BF16)
        mlp_o[...] = low
        bias_o[...] = jnp.sum(low.astype(F32), axis=0, keepdims=True)
        out_o[...] = jnp.zeros_like(out_o)
        grad_o[...] = jnp.zeros_like(grad_o)

    bias = tile_bias(bias_s, 0, second.shape[1])
    mlp_steps(info, second[...], mlp_o[...], w1, w2, bias, keep_o, send_o, out_o, grad_o, b1_o, both)


def middle_mlp_kernel(
    first, info, second, mlp, w1, w2, b1, out_in, grad_in,
    keep_o, send_o, out_o, grad_o, b1_o,
    both, bias_s,
):
    @pl.when(pl.program_id(0) == 0)
    def _():
        bias_s[...] = vec(b1)
        out_o[...] = out_in[...]
        grad_o[...] = grad_in[...]

    bias = tile_bias(bias_s, first, second.shape[1])
    mlp_steps(info, second[...], mlp[...], w1, w2, bias, keep_o, send_o, out_o, grad_o, b1_o, both)


def second_mlp_kernel(
    first, info, second, mlp, w1, w2, b1, out_in, grad_in, middle, out_grad, gain, keep_in, send_in,
    keep_o, send_o, out_o, b1_o, middle_grad_o, branch_o, gain_o, shift_o, bias_o,
    both, grad_s, bias_s,
):
    step = pl.program_id(0)

    @pl.when(step == 0)
    def _():
        bias_s[...] = vec(b1)
        out_o[...] = out_in[...]
        grad_s[...] = grad_in[...]

    bias = tile_bias(bias_s, first, second.shape[1])
    mlp_steps(info, second[...], mlp[...], w1, w2, bias, keep_o, send_o, out_o, grad_s, b1_o, both)

    @pl.when(step == pl.num_programs(0) - 1)
    def _():
        grad = grad_s[...]
        xhat, scale = standardize(middle[...])
        gain_o[...] = jnp.sum(grad * xhat, axis=0, keepdims=True)
        shift_o[...] = jnp.sum(grad, axis=0, keepdims=True)
        middle_grad = out_grad[...] + norm_back(grad, xhat, scale, vec(gain))
        middle_grad_o[...] = middle_grad
        branch = middle_grad.astype(BF16)
        branch_o[...] = branch
        bias_o[...] = jnp.sum(branch.astype(F32), axis=0, keepdims=True)


def attend_back_kernel(
    info, normed, mixed, branch, q, k, v, p, wo,
    keep_o, send_o, dq_o, dk_o, dv_o, qb_o, vb_o,
    grad_s, score_s, both,
):
    step = pl.program_id(0)
    length = normed.shape[0]
    mixed_grad = dot_nt(branch[...], wo[...]).astype(BF16)
    cols = pl.ds(pl.multiple_of(step * WIDE, WIDE), WIDE)
    grad_s[...] = dot_nt(mixed_grad, stack_heads(v[...], length))
    both[3] = dot_tn(mixed[...], branch[:, cols]).astype(BF16)
    dv = unstack_heads(dot_tn(p[0], mixed_grad), length).astype(BF16)
    rows = 64
    for top in range(0, length, rows):
        at = slice(top, top + rows)
        for h in range(GROUP):
            span = slice(h * length, (h + 1) * length)
            prob = p[0, at, span].astype(F32)
            weighted = prob * grad_s[at, span]
            center = jnp.sum(weighted, axis=-1, keepdims=True)
            score_s[at, span] = (weighted - prob * center).astype(BF16)
    dq = (dot(score_s[...], stack_heads(k[...], length)) * score_scale).astype(BF16)
    dk = (unstack_heads(dot_tn(score_s[...], q[...]), length) * score_scale).astype(BF16)
    dq_o[...] = dq
    dk_o[...] = dk
    dv_o[...] = dv
    qb_o[...] = jnp.sum(dq.astype(F32), axis=0, keepdims=True)
    vb_o[...] = jnp.sum(dv.astype(F32), axis=0, keepdims=True)
    both[0] = dot_tn(normed[...], dq).astype(BF16)
    both[1] = dot_tn(normed[...], dk).astype(BF16)
    both[2] = dot_tn(normed[...], dv).astype(BF16)
    for t in range(2):
        relative_store(
            info, lambda rows: (both[t, rows], both[2 + t, rows]),
            keep_o, send_o, t ^ info[2], t ^ info[4], normed.shape[1],
        )


def finish_kernel(
    info, tok, middle_grad, dq, dk, dv, wq, wk, wv, g1,
    middle, out_sum, b2, seg, tgt,
    qb, vb, ob, n2g, n2s, b2g, b1a, b1b, b1c,
    tokens_o, small_o, own_o, hop1_o, hop2_o, hop3_o,
    acc,
):
    step = pl.program_id(0)

    @pl.when(step == 0)
    def _():
        acc[...] = jnp.zeros_like(acc)
        output = (middle[...] + (out_sum[...] + vec(b2))).astype(BF16)
        places = located(seg, tgt, [info[0] ^ hop for hop in range(4)], output.shape[0])
        picked = dot_tn(places, output).astype(BF16)
        for hop, out in enumerate((own_o, hop1_o, hop2_o, hop3_o)):
            out[...] = picked[hop * out.shape[0] : (hop + 1) * out.shape[0]]

    acc[...] += dot_nt(dq[...], wq[...]) + dot_nt(dk[...], wk[...]) + dot_nt(dv[...], wv[...])

    @pl.when(step == pl.num_programs(0) - 1)
    def _():
        grad = acc[...]
        xhat, scale = standardize(tok[...].astype(F32))
        tokens_o[...] = (middle_grad[...] + norm_back(grad, xhat, scale, vec(g1))).astype(BF16)
        width = grad.shape[1]
        small_o[0:1, :] = qb[...]
        small_o[1:2, :] = vb[...]
        small_o[2:3, :] = ob[...]
        small_o[3:4, :] = jnp.sum(grad * xhat, axis=0, keepdims=True)
        small_o[4:5, :] = jnp.sum(grad, axis=0, keepdims=True)
        small_o[5:6, :] = n2g[...]
        small_o[6:7, :] = n2s[...]
        small_o[7:8, :] = b2g[...]
        row = 8
        for part in (b1a, b1b, b1c):
            for j in range(part.shape[1] // width):
                small_o[row : row + 1, :] = part[:, j * width : (j + 1) * width]
                row += 1


def place_kernel(part, names, first_call, *refs):
    info = refs[0]
    count = 2 * len(names)
    quarters = refs[1 : 1 + count]
    outs = refs[1 + count + (0 if first_call else 2) :][:2]
    mark, low_s, stage, in_sems, sems = refs[-5:]
    mark[...] = jnp.zeros_like(mark)
    half, width = quarters[0].shape
    rows = 2 * half // SPANS

    def send(n, k, side, tile, span):
        source = stage.at[n, pl.ds(k * rows, rows), :]
        at = pl.ds(pl.multiple_of(span * rows, rows), rows)
        sem = sems.at[n, k]
        columns = lambda t: pl.ds(pl.multiple_of(t * width, width), width)
        if part is not None:
            if side == 0:
                start = (tile + 2 * part) * width + span * rows
                target = outs[0].at[pl.ds(pl.multiple_of(start, rows), rows), :]
            else:
                target = outs[1].at[at, columns(tile + 2 * part)]
            pltpu.make_async_copy(source, target, sem).start()
        elif side == 0:
            pltpu.make_async_copy(source, outs[0].at[at, columns(tile)], sem).start()
        else:

            @pl.when(tile == 0)
            def _():
                pltpu.make_async_copy(source, outs[0].at[at, columns(2)], sem).start()

            @pl.when(tile == 1)
            def _():
                pltpu.make_async_copy(source, outs[1].at[at, :], sem).start()

    for n in range(count):
        pltpu.make_async_copy(quarters[n], low_s.at[n], in_sems.at[n]).start()
    for n in range(count):
        name, other = names[n // 2], n % 2
        tile = (name // 2) ^ info[2 + 2 * other]
        pltpu.make_async_copy(quarters[n], low_s.at[n], in_sems.at[n]).wait()
        for k in range(half // rows):
            stage[n, k * rows : (k + 1) * rows, :] = low_s[n, k * rows : (k + 1) * rows, :].astype(F32)
            span = ((name % 2) * (SPANS // 2) + k) ^ info[3 + 2 * other]
            for side in range(2):

                @pl.when((info[1] ^ other) == side)
                def _():
                    send(n, k, side, tile, span)

    for n in range(count):
        for k in range(half // rows):
            here = stage.at[n, pl.ds(k * rows, rows), :]
            pltpu.make_async_copy(here, here, sems.at[n, k]).wait()


def cost(micros):
    return pl.CostEstimate(
        flops=int(micros * 9e8), bytes_accessed=int(micros * 3.4e6), transcendentals=0
    )


def call(kernel, grid, ins, outs, scratch=(), micros=4, vmem=26, prefetch=0, aliases={}, line=None):
    extra = [] if line is None or line.last is None else [line.last]
    known = len(ins) + prefetch
    body = (lambda *refs: kernel(*refs[:known], *refs[known + 1 :])) if extra else kernel
    inner = pl.pallas_call(
        body,
        grid_spec=pltpu.PrefetchScalarGridSpec(
            num_scalar_prefetch=prefetch,
            grid=grid,
            in_specs=list(ins) + [pl.BlockSpec(memory_space=pl.ANY)] * len(extra),
            out_specs=[spec for spec, _ in outs],
            scratch_shapes=list(scratch),
        ),
        out_shape=[shape for _, shape in outs],
        input_output_aliases=aliases,
        compiler_params=pltpu.CompilerParams(vmem_limit_bytes=vmem * 2**20),
        cost_estimate=cost(micros),
    )
    return lambda *args: inner(
        *(pltpu.with_memory_space_constraint(a.array, a.space) if isinstance(a, Far) else a for a in args),
        *extra,
    )


class Far:
    space = pltpu.HBM

    def __init__(self, array):
        self.array = array


class Near(Far):
    space = pltpu.VMEM


def full(*shape):
    return pl.BlockSpec(shape, lambda *_: (0,) * len(shape))


def block(shape, index):
    return pl.BlockSpec(shape, index)


def sds(shape, dtype):
    return jax.ShapeDtypeStruct(shape, dtype)


def place(part, names, info, values, shapes, outs, line):
    half, width = values[0].shape
    rows = 2 * half // SPANS
    anywhere = pl.BlockSpec(memory_space=pl.ANY)
    count = len(values)
    outs = call(
        functools.partial(place_kernel, part, names, not outs),
        (),
        [pl.BlockSpec(memory_space=pltpu.SMEM)]
        + [anywhere] * (count + len(outs)),
        [(anywhere, pltpu.HBM(shape.shape, shape.dtype)) for shape in shapes]
        + [(pl.BlockSpec(memory_space=pltpu.VMEM), pltpu.VMEM((8, 128), F32))],
        [
            pltpu.VMEM((count, half, width), BF16),
            pltpu.VMEM((count, half, width), F32),
            pltpu.SemaphoreType.DMA((count,)),
            pltpu.SemaphoreType.DMA((count, half // rows)),
        ],
        micros=MOVE,
        vmem=16,
        line=line,
        aliases={1 + count + n: n for n in range(len(outs))},
    )(info, *values, *outs)
    line.last = outs[2]
    return outs[:2]


class Exchange:
    def __init__(self, rows, blk):
        self.blk = blk
        self.total = rows * blk
        self.bits = self.total.bit_length() - 1
        assert self.total == 1 << self.bits and blk == 4
        self.here = lax.axis_index("rows") * blk + lax.axis_index("blk")
        self.core = self.here & 1
        self.steps = self.bits - 1

    def pairs(self, masks):
        return [(i, i ^ masks[i & 1]) for i in range(self.total)]

    def move_core(self, value):
        return lax.ppermute(value, AXES, self.pairs((1, 1)))

    def swap_blocks(self, pieces):
        mine = self.here & (self.blk - 1)
        got = [lax.dynamic_index_in_dim(pieces, mine, 0, keepdims=False)]
        for hop in range(1, self.blk):
            send = lax.dynamic_index_in_dim(pieces, mine ^ hop, 0, keepdims=False)
            got.append(lax.ppermute(send, AXES, self.pairs((hop, hop))))
        return got


class Chunk:
    def __init__(self, ex, line, perms):
        self.ex = ex
        self.line = line
        base = list(range(1, ex.bits))
        self.orders = [[base[n] for n in perm] + base[LEVELS:] for perm in perms]

    def bits_of(self, order):
        return [(self.ex.here >> bit) & 1 for bit in order]

    def info(self):
        places = []
        for order in self.orders:
            bit = self.bits_of(order)
            places.append((bit[0], bit[1] * 4 + bit[2] * 2 + bit[3]))
        core = self.ex.core
        own = [jnp.where(core == 0, a, b) for a, b in zip(*places)]
        other = [jnp.where(core == 0, b, a) for a, b in zip(*places)]
        return jnp.stack([self.ex.here & (self.ex.blk - 1), core] + own + other).astype(jnp.int32)

    def move(self, level, value):
        masks = tuple(1 << order[level] for order in self.orders)
        return lax.ppermute(value, AXES, self.ex.pairs(masks))

    def add(self, level, which):
        rows = self.keep.shape[1] >> level
        width = self.keep.shape[2]
        if level == 0:
            self.got = []
        tile = pl.BlockSpec((None, rows, width), lambda _: (int(level == 0), which if level else 0, 0))
        strip = pl.BlockSpec((rows, width), lambda _: (which, 0))
        return self.line.run(
            add_kernel,
            [self.keep, self.recv] + self.got,
            [sds((rows, width), BF16)],
            [tile] * 2 + [strip] * len(self.got),
        )

    def total(self):
        span = self.add(LEVELS - 1, 0)
        rows = span.shape[0]
        bits = [
            jnp.where(self.ex.core == 0, a, b)
            for a, b in zip(*(self.bits_of(order)[LEVELS:] for order in self.orders))
        ]
        for level, bit in enumerate(bits, LEVELS):
            rows //= 2
            recv = self.move(level, lax.dynamic_slice_in_dim(span, (1 - bit) * rows, rows, 0))
            span = add_up([lax.dynamic_slice_in_dim(span, bit * rows, rows, 0), recv])
        for level, bit in reversed(list(enumerate(bits, LEVELS))):
            recv = self.move(level, span)
            low = jnp.where(bit == 0, span, recv)
            span = jnp.concatenate([low, jnp.where(bit == 0, recv, span)], axis=0)
        self.spans = [span]

    def do(self, step):
        if step == "c":
            self.recv = self.ex.move_core(self.send)
        elif step[0] == "r":
            level = int(step[1])
            total = self.add(level, 1)
            self.got.append(self.move(level, total))
        elif step == "f":
            self.total()
        elif step == "g0":
            self.spans.append(self.move(3, self.spans[0]))
        elif step in ("g1", "g2"):
            self.spans.append(self.move(2, self.spans[step == "g2"]))
        elif step == "j":
            rows, width = self.spans[0].shape
            self.quarters = {"A": self.line.run(join_kernel, self.spans, [sds((4 * rows, width), BF16)])}
        elif step == "g3":
            self.quarters["B"] = self.move(1, self.quarters["A"])
        elif step == "g4":
            self.quarters["C"] = self.move(0, self.quarters["A"])
        elif step == "g5":
            self.quarters["D"] = self.move(0, self.quarters["B"])
        else:
            name = step[1]
            self.others[name] = self.ex.move_core(self.quarters[name])


class Line:
    def __init__(self):
        self.last = None

    def run(self, kernel, ins, out_shapes, specs=None, vmem=16):
        after = [] if self.last is None else [self.last]
        near = pl.BlockSpec(memory_space=pltpu.VMEM)
        outs = pl.pallas_call(
            functools.partial(skip, len(after), kernel),
            grid=() if specs is None else (1,),
            in_specs=[pl.BlockSpec(memory_space=pl.ANY)] * len(after) + (specs or [near] * len(ins)),
            out_specs=[near if specs is None else full(*shape.shape) for shape in out_shapes],
            out_shape=out_shapes,
            compiler_params=pltpu.CompilerParams(vmem_limit_bytes=vmem * 2**20),
            cost_estimate=cost(STEP),
        )(*after, *ins)
        self.last = outs[0]
        return outs[0]


def skip(count, kernel, *refs):
    kernel(*refs[count:])


def add_kernel(*refs):
    out = refs[-1]
    height = 32 if out.shape[0] % 32 == 0 else out.shape[0]

    def body(n, _):
        at = pl.ds(pl.multiple_of(n * height, height), height)
        total = refs[0][at, :].astype(F32)
        for ref in refs[1:-1]:
            total = total + ref[at, :].astype(F32)
        out[at, :] = total.astype(BF16)
        return 0

    lax.fori_loop(0, out.shape[0] // height, body, 0)


def join_kernel(*refs):
    start = 0
    for ref in refs[:-1]:
        refs[-1][start : start + ref.shape[0], :] = ref[...]
        start += ref.shape[0]


def order_kernel(info, *refs):
    rows = refs[0].shape[0]
    for hop, ref in enumerate(refs[:-1]):
        refs[-1][pl.ds(pl.multiple_of((info[0] ^ hop) * rows, rows), rows), :] = ref[...]


def sum_kernel(one, other, out):
    out[...] = one[...] + other[...]


def add_up(terms):
    total = terms[0].astype(F32)
    for term in terms[1:]:
        total = total + term.astype(F32)
    return total.astype(BF16)


def local(
    mesh_rows, mesh_blk,
    tokens, seg_ids, target_index,
    qkv_weight, q_bias, v_bias, out_weight, out_bias,
    norm1_gain, norm1_shift, norm2_gain, norm2_shift,
    fc1_weight, fc1_bias, fc2_weight, fc2_bias,
    target_grad,
):
    ex = Exchange(mesh_rows, mesh_blk)
    count_rows, length, d = tokens.shape
    assert count_rows == 1
    ff = fc1_weight.shape[1]
    tiles = ff // d
    images, patches = target_grad.shape[1], target_grad.shape[2]
    per = images // mesh_blk
    groups = d // WIDE
    pieces = target_grad.reshape(mesh_blk, per * patches, d)
    got = ex.swap_blocks(pieces)
    tok = Far(tokens.reshape(length, d))
    seg, target_index = Far(seg_ids), Far(target_index)
    qkv_weight, q_bias, v_bias, out_weight, out_bias = map(
        Far, (qkv_weight, q_bias, v_bias, out_weight, out_bias)
    )
    norm1_gain, norm1_shift, norm2_gain, norm2_shift = map(
        Far, (norm1_gain, norm1_shift, norm2_gain, norm2_shift)
    )
    fc1_weight, fc1_bias, fc2_weight, fc2_bias = map(
        Far, (fc1_weight, fc1_bias, fc2_weight, fc2_bias)
    )
    picks = full(*target_index.array.shape)
    col = lambda g: (0, g)
    third = lambda n: lambda g: (0, n * groups + g)
    act = pltpu.VMEM((length, d), BF16)
    act32 = pltpu.VMEM((length, d), F32)
    act_far = pltpu.HBM((length, d), BF16)
    one = pltpu.VMEM((1, d), F32)
    vd = full(d)
    smem = pl.BlockSpec(memory_space=pltpu.SMEM)
    whole = full(length, d)
    strip = block((length, WIDE), col)
    wide = GROUP * length
    wide_spec = block((1, length, wide), lambda g: (g, 0, 0))

    line = Line()
    links = [Chunk(ex, line, perms) for perms in ORDERS]
    infos = [link.info() for link in links]
    for link, info in zip(links, infos):
        link.info_ref = info
    half = tiles // 2

    def mlp_specs(skip):
        return [
            block((d, d), lambda j, info: (0, skip + j)),
            block((d, d), lambda j, info: (skip + j, 0)),
            full(ff),
        ]

    def tile_outs(skip):
        return [
            (block((1, d, d), lambda j, info, n=n: ((j + skip) ^ info[n], 0, 0)), pltpu.HBM((half, d, d), BF16))
            for n in (2, 4)
        ]

    def b1_out(tiles):
        return block((1, d), lambda j, info: (0, j)), pltpu.VMEM((1, tiles * d), F32)

    both = pltpu.VMEM((2, d, d), BF16)
    piece = full(per * patches, d)
    pair_out = (block((2, d, WIDE), lambda g: (0, 0, g)), pltpu.HBM((2, d, d), BF16))
    links_by_name = dict(zip(("M1", "M2", "Q"), links))
    for link in links:
        link.others = {}
    fc_out = qkv_out = ()
    small_step = 0
    for step in SCHEDULE:
        if step == "K0":
            normed, q, k, v, prob, mixed, middle, second = call(
                attend_kernel,
                (groups,),
                [
                    whole, full(1, length),
                    block((d, WIDE), third(0)), block((d, WIDE), third(1)), block((d, WIDE), third(2)),
                    block((WIDE, d), lambda g: (g, 0)),
                    vd, vd, vd, vd, vd, vd, vd,
                ],
                [
                    (whole, act_far), (strip, act_far), (strip, act_far), (strip, act_far),
                    (wide_spec, pltpu.HBM((groups, length, wide), BF16)),
                    (strip, act_far), (whole, act32), (whole, act),
                ],
                [
                    pltpu.VMEM((length, d), F32),
                    pltpu.VMEM((length, wide), F32),
                    pltpu.VMEM((2, d), F32),
                ],
                micros=11 * PACE, line=line,
            )(
                tok, seg, qkv_weight, qkv_weight, qkv_weight, out_weight, q_bias, v_bias, out_bias,
                norm1_gain, norm1_shift, norm2_gain, norm2_shift,
            )
        elif step == "K1":
            links[0].keep, links[0].send, out_sum, second_grad, b1a, out_grad, mlp_low, b2_grad = call(
                first_mlp_kernel,
                (half,),
                [whole, full(1, length), picks] + [piece] * 4 + mlp_specs(0),
                [
                    *tile_outs(0), (whole, act32), (whole, act32), b1_out(half),
                    (whole, act32), (whole, act), (full(1, d), one),
                ],
                [both, pltpu.VMEM((1, ff), F32)],
                micros=12 * PACE, prefetch=1, line=line,
            )(infos[0], Near(second), seg, target_index, *got, fc1_weight, fc2_weight, fc1_bias)
            line.last = b2_grad
        elif step == "K2a":
            links[1].keep, links[1].send, out_sum, second_grad, b1b = call(
                functools.partial(middle_mlp_kernel, half),
                (1,),
                [whole, whole] + mlp_specs(half) + [whole] * 2,
                [*tile_outs(0), (whole, act32), (whole, act32), b1_out(1)],
                [both, pltpu.VMEM((1, ff), F32)],
                micros=6 * PACE, prefetch=1, line=line,
            )(infos[1], Near(second), Near(mlp_low), fc1_weight, fc2_weight, fc1_bias, Near(out_sum), Near(second_grad))
            line.last = b1b
        elif step == "K2b":
            links[1].keep, links[1].send, out_sum, b1c, middle_grad, branch, n2g, n2s, ob_grad = call(
                functools.partial(second_mlp_kernel, half + 1),
                (1,),
                [whole, whole] + mlp_specs(half + 1) + [whole] * 4 + [vd] + [pl.BlockSpec(memory_space=pl.ANY)] * 2,
                [
                    *tile_outs(1), (whole, act32), b1_out(1),
                    (whole, act32), (whole, act), (full(1, d), one), (full(1, d), one), (full(1, d), one),
                ],
                [both, pltpu.VMEM((length, d), F32), pltpu.VMEM((1, ff), F32)],
                micros=7 * PACE, prefetch=1, line=line, aliases={11: 0, 12: 1},
            )(
                infos[1], Near(second), Near(mlp_low), fc1_weight, fc2_weight, fc1_bias,
                *map(Near, (out_sum, second_grad, middle, out_grad)), norm2_gain,
                Far(links[1].keep), Far(links[1].send),
            )
            line.last = ob_grad
        elif step == "K3":
            links[2].keep, links[2].send, dq, dk, dv, qb_grad, vb_grad = call(
                attend_back_kernel,
                (groups,),
                [
                    smem, whole, whole, whole, strip, strip, strip, wide_spec,
                    block((WIDE, d), lambda g: (g, 0)),
                ],
                [
                    pair_out, pair_out, (strip, act_far), (strip, act_far), (strip, act_far),
                    (block((1, WIDE), col), one), (block((1, WIDE), col), one),
                ],
                [
                    pltpu.VMEM((length, wide), F32),
                    pltpu.VMEM((length, wide), BF16),
                    pltpu.VMEM((4, d, WIDE), BF16),
                ],
                micros=13.5 * PACE, line=line,
            )(infos[2], Far(normed), Far(mixed), Near(branch), *map(Far, (q, k, v, prob)), out_weight)
            line.last = vb_grad
        elif step == "K4":
            tokens_grad, small, *picked = call(
                finish_kernel,
                (groups,),
                [
                    smem, whole, whole, strip, strip, strip,
                    block((d, WIDE), third(0)), block((d, WIDE), third(1)), block((d, WIDE), third(2)),
                    vd, whole, whole, vd, full(1, length), picks,
                ]
                + [full(1, d)] * 6 + [full(1, half * d)] + [full(1, d)] * 2,
                [
                    (whole, pltpu.HBM((length, d), BF16)),
                    (full(8 + tiles, d), sds((8 + tiles, d), F32)),
                    *[(full(per * patches, d), sds((per * patches, d), BF16))] * 4,
                ],
                [pltpu.VMEM((length, d), F32)],
                micros=7 * PACE, line=line,
            )(
                infos[0], tok, Near(middle_grad), *map(Far, (dq, dk, dv)), qkv_weight, qkv_weight, qkv_weight, norm1_gain,
                Near(middle), Near(out_sum), fc2_bias, seg, target_index,
                *map(Near, (qb_grad, vb_grad, ob_grad, n2g, n2s, b2_grad, b1a, b1b, b1c)),
            )
            line.last = small
        elif step == "T":
            swapped = picked[:1] + [
                lax.ppermute(picked[hop], AXES, ex.pairs((hop, hop))) for hop in range(1, mesh_blk)
            ]
        elif step == "t":
            targets = line.run(
                order_kernel,
                [infos[0], *swapped],
                [sds((images * patches, d), BF16)],
                [smem] + [full(per * patches, d)] * mesh_blk,
            )
        elif step == "S":
            small = line.run(sum_kernel, [small, small_recv], [sds(small.shape, F32)])
            small_step += 1
        elif step == "s":
            small_recv = lax.ppermute(small, AXES, ex.pairs((1 << small_step,) * 2))
        else:
            name, step = step.split()
            link = links_by_name[name]
            if step[0] != "v":
                link.do(step)
                continue
            names = ["ABCD".index(n) for n in step[1:]]
            values = [v for n in step[1:] for v in (link.quarters[n], link.others[n])]
            if name == "Q":
                shapes = [sds((d, 3 * d), F32), sds((d, d), F32)]
                qkv_out = place(None, names, link.info_ref, values, shapes, qkv_out, line)
            else:
                shapes = [sds((ff, d), F32), sds((d, ff), F32)]
                fc_out = place(int(name[1]) - 1, names, link.info_ref, values, shapes, fc_out, line)
    for _ in range(small_step, ex.bits):
        small = small + lax.ppermute(small, AXES, ex.pairs((1 << small_step,) * 2))
        small_step += 1
    fc2_full, fc1_full = fc_out
    qkv_full, out_full = qkv_out
    return (
        targets.reshape(1, images, patches, d),
        tokens_grad.reshape(count_rows, length, d),
        qkv_full,
        small[0], small[1],
        out_full,
        small[2], small[3], small[4], small[5], small[6],
        fc1_full,
        small[8:].reshape(ff),
        fc2_full,
        small[7],
    )


def solution(mesh):
    rows, blk = mesh.shape["rows"], mesh.shape["blk"]

    def body(*args):
        return local(rows, blk, *args)

    return jax.shard_map(
        body,
        mesh=mesh,
        in_specs=(
            P(("rows", "blk"), None, None),
            P(("rows", "blk"), None),
            P(("rows", "blk"), None, None),
        )
        + (P(),) * 13
        + (P("blk", "rows", None, None),),
        out_specs=(
            P("blk", "rows", None, None),
            P(("rows", "blk"), None, None),
        )
        + (P(),) * 13,
        check_vma=False,
    )
```

```python
import functools

import jax
import jax.numpy as jnp
from jax import lax
from jax.experimental import pallas as pl
from jax.experimental.pallas import tpu as pltpu
from jax.sharding import PartitionSpec as P

HEADS = 12
HEAD_DIM = 64
GROUP = 4
WIDE = GROUP * HEAD_DIM
LEVELS = 4
PACE = 1
STEP = 7
MOVE = 25
WEIGHTS = {
    "K1": 1,
    "K2a": 3,
    "K4": 40,
    "M1 f": 10,
    "M1 r0": 1,
    "M1 r1": 0,
    "M1 r3": 3,
    "M1 vABCD": 3,
    "M2 f": 40,
    "M2 j": 3,
    "M2 r3": 20,
    "M2 vABCD": 40,
    "Q r3": 3,
    "Q vAB": 80,
    "Q vCD": 200,
    "S": 0,
}
FIRST = 1
SPANS = 8
AXES = ("rows", "blk")
SCHEDULE = (
    "K0", "K1", "M1 c", "K2a", "M1 r0", "K2b", "K3", "M1 r1", "M2 c", "M2 r0", "Q c", "K4",
    "M1 r2", "s", "T", "Q r0", "S", "M1 r3", "M2 r1", "s", "M1 f", "M1 g1", "M2 r2", "Q r1",
    "M1 g0", "M1 g2", "S", "s", "M2 r3", "Q r2", "M1 j", "M1 g3", "M1 cA", "S", "s", "M1 g5",
    "M1 cB", "M1 g4", "M1 cC", "M2 f", "S", "Q r3", "Q f", "M2 g0", "M2 g1", "Q g0", "M1 cD", "Q g2",
    "s", "Q g1", "M2 g2", "M2 j", "M2 cA", "M2 g3", "M2 g4", "M2 g5", "M1 vABCD", "Q j", "Q cA", "M2 cC",
    "Q g4", "M2 cD", "Q g3", "M2 cB", "Q g5", "M2 vABCD", "S", "Q cB", "Q vAB", "Q cC", "Q cD", "Q vCD",
    "t",
)
ORDERS = (((0, 1, 2, 3), (1, 0, 2, 3)), ((0, 1, 2, 3), (1, 0, 2, 3)), ((0, 1, 2, 3), (1, 0, 2, 3)))
F32 = jnp.float32
BF16 = jnp.bfloat16

norm_eps = 1e-06
score_scale = 0.125
neg_large = -1e30


def dot(a, b):
    return lax.dot_general(a, b, (((1,), (0,)), ((), ())), preferred_element_type=F32)


def dot_nt(a, b):
    return lax.dot_general(a, b, (((1,), (1,)), ((), ())), preferred_element_type=F32)


def dot_tn(a, b):
    return lax.dot_general(a, b, (((0,), (0,)), ((), ())), preferred_element_type=F32)


def standardize(values):
    center = values - jnp.mean(values, axis=-1, keepdims=True)
    spread = jnp.mean(center * center, axis=-1, keepdims=True)
    scale = lax.rsqrt(spread + norm_eps)
    return center * scale, scale


def norm_back(grad, xhat, scale, gain):
    e = grad * gain
    mean_e = jnp.mean(e, axis=-1, keepdims=True)
    mean_ex = jnp.mean(e * xhat, axis=-1, keepdims=True)
    return (e - mean_e - xhat * mean_ex) * scale


def head_mask(rows, h):
    lane = lax.broadcasted_iota(jnp.int32, (rows, WIDE), 1)
    return (lane >= h * HEAD_DIM) & (lane < (h + 1) * HEAD_DIM)


def vec(ref):
    return ref[...].reshape(1, -1)


def stack_heads(values, length):
    return jnp.concatenate(
        [jnp.where(head_mask(length, h), values, jnp.zeros_like(values)) for h in range(GROUP)],
        axis=0,
    )


def unstack_heads(stacked, length):
    total = stacked[:length]
    for h in range(1, GROUP):
        total = jnp.where(head_mask(length, h), stacked[h * length : (h + 1) * length], total)
    return total


def attend_kernel(
    tok, seg, wq, wk, wv, wo, qb, vb, ob, g1, s1, g2, s2,
    normed_o, q_o, k_o, v_o, p_o, mixed_o, middle_o, second_o,
    acc, score_s, biases,
):
    step = pl.program_id(0)
    length, width = tok.shape
    cols = pl.ds(pl.multiple_of(step * WIDE, WIDE), WIDE)

    @pl.when(step == 0)
    def _():
        xhat, _ = standardize(tok[...].astype(F32))
        normed_o[...] = (xhat * vec(g1) + vec(s1)).astype(BF16)
        acc[...] = jnp.zeros_like(acc)
        biases[0:1, :] = vec(qb)
        biases[1:2, :] = vec(vb)

    normed = normed_o[...]
    q = (dot(normed, wq[...]) + biases[0:1, cols]).astype(BF16)
    k = dot(normed, wk[...]).astype(BF16)
    v = (dot(normed, wv[...]) + biases[1:2, cols]).astype(BF16)
    q_o[...] = q
    k_o[...] = k
    v_o[...] = v
    score_s[...] = dot_nt(q * jnp.asarray(score_scale, BF16), stack_heads(k, length))
    seg_row = seg[...]
    seg_col = jnp.broadcast_to(seg_row.astype(F32), (128, length)).T[:, :1].astype(jnp.int32)
    rows = 64
    for top in range(0, length, rows):
        at = slice(top, top + rows)
        allowed = seg_col[at] == seg_row
        for h in range(GROUP):
            span = slice(h * length, (h + 1) * length)
            scores = jnp.where(allowed, score_s[at, span], neg_large)
            raised = jnp.exp(scores - jnp.max(scores, axis=-1, keepdims=True))
            share = 1.0 / jnp.sum(raised, axis=-1, keepdims=True)
            p_o[0, at, span] = (raised * share).astype(BF16)
    mixed = dot(p_o[0], stack_heads(v, length)).astype(BF16)
    mixed_o[...] = mixed
    acc[...] += dot(mixed, wo[...])

    @pl.when(step == pl.num_programs(0) - 1)
    def _():
        middle = tok[...].astype(F32) + (acc[...] + vec(ob))
        middle_o[...] = middle
        xhat, _ = standardize(middle)
        second_o[...] = (xhat * vec(g2) + vec(s2)).astype(BF16)


def located(seg, tgt, blocks, length):
    rows = []
    starts = [
        jnp.sum(((seg[...] >= 0) & (seg[...] < image)).astype(jnp.int32))
        for image in range(tgt.shape[0])
    ]
    for block in blocks:
        for image, start in enumerate(starts):
            rows.append(tgt[image, pl.ds(block, 1), :] + start)
    row = jnp.concatenate(rows, axis=1)
    slots = lax.broadcasted_iota(jnp.int32, (length, row.shape[1]), 0)
    return (slots == row).astype(F32).astype(BF16)


def tile_bias(bias_s, skip, width):
    start = (pl.program_id(0) + skip) * width
    return bias_s[:, pl.ds(pl.multiple_of(start, width), width)]


def relative_store(info, pair, keep_o, send_o, keep_at, send_at, height):
    first = info[1] == 0
    rows = height // SPANS
    for n in range(SPANS):
        low, high = pair(slice(n * rows, (n + 1) * rows))
        keep_o[keep_at, pl.ds(pl.multiple_of((n ^ info[3]) * rows, rows), rows), :] = jnp.where(first, low, high)
        send_o[send_at, pl.ds(pl.multiple_of((n ^ info[5]) * rows, rows), rows), :] = jnp.where(first, high, low)


def mlp_steps(info, sn, low, w1, w2, bias, keep_o, send_o, out_o, grad_o, b1_o, both):
    width = low.shape[1]
    piece = 256
    for j in range(width // piece):
        cols = slice(j * piece, (j + 1) * piece)
        hidden = dot(sn, w1[:, cols]) + bias[:, cols]
        phi_cum = 0.5 + 0.5 * lax.erf(hidden * 0.7071067811865476)
        density = 0.3989422804014327 * jnp.exp(hidden * hidden * -0.5)
        active = (hidden * phi_cum).astype(BF16)
        hidden_grad = dot_nt(low, w2[cols, :]) * (phi_cum + hidden * density)
        hidden_low = hidden_grad.astype(BF16)
        b1_o[:, cols] = jnp.sum(hidden_low.astype(F32), axis=0, keepdims=True)
        both[0, cols, :] = dot_tn(active, low).astype(BF16)
        both[1, :, cols] = dot_tn(sn, hidden_low).astype(BF16)
        out_o[...] += dot(active, w2[cols, :])
        grad_o[...] += dot_nt(hidden_low, w1[:, cols])
    relative_store(info, lambda rows: (both[0, rows], both[1, rows]), keep_o, send_o, 0, 0, width)


def first_mlp_kernel(
    info, second, seg, tgt, own, got1, got2, got3, w1, w2, b1,
    keep_o, send_o, out_o, grad_o, b1_o, out_grad_o, mlp_o, bias_o,
    both, bias_s,
):
    @pl.when(pl.program_id(0) == 0)
    def _():
        bias_s[...] = vec(b1)
        me = info[0]
        places = located(seg, tgt, [me, me ^ 1, me ^ 2, me ^ 3], second.shape[0])
        pieces = jnp.concatenate([own[...], got1[...], got2[...], got3[...]], axis=0)
        total = dot(places, pieces)
        out_grad_o[...] = total
        low = total.astype(BF16)
        mlp_o[...] = low
        bias_o[...] = jnp.sum(low.astype(F32), axis=0, keepdims=True)
        out_o[...] = jnp.zeros_like(out_o)
        grad_o[...] = jnp.zeros_like(grad_o)

    bias = tile_bias(bias_s, 0, second.shape[1])
    mlp_steps(info, second[...], mlp_o[...], w1, w2, bias, keep_o, send_o, out_o, grad_o, b1_o, both)


def middle_mlp_kernel(
    first, info, second, mlp, w1, w2, b1, out_in, grad_in,
    keep_o, send_o, out_o, grad_o, b1_o,
    both, bias_s,
):
    @pl.when(pl.program_id(0) == 0)
    def _():
        bias_s[...] = vec(b1)
        out_o[...] = out_in[...]
        grad_o[...] = grad_in[...]

    bias = tile_bias(bias_s, first, second.shape[1])
    mlp_steps(info, second[...], mlp[...], w1, w2, bias, keep_o, send_o, out_o, grad_o, b1_o, both)


def second_mlp_kernel(
    first, info, second, mlp, w1, w2, b1, out_in, grad_in, middle, out_grad, gain, keep_in, send_in,
    keep_o, send_o, out_o, b1_o, middle_grad_o, branch_o, gain_o, shift_o, bias_o,
    both, grad_s, bias_s,
):
    step = pl.program_id(0)

    @pl.when(step == 0)
    def _():
        bias_s[...] = vec(b1)
        out_o[...] = out_in[...]
        grad_s[...] = grad_in[...]

    bias = tile_bias(bias_s, first, second.shape[1])
    mlp_steps(info, second[...], mlp[...], w1, w2, bias, keep_o, send_o, out_o, grad_s, b1_o, both)

    @pl.when(step == pl.num_programs(0) - 1)
    def _():
        grad = grad_s[...]
        xhat, scale = standardize(middle[...])
        gain_o[...] = jnp.sum(grad * xhat, axis=0, keepdims=True)
        shift_o[...] = jnp.sum(grad, axis=0, keepdims=True)
        middle_grad = out_grad[...] + norm_back(grad, xhat, scale, vec(gain))
        middle_grad_o[...] = middle_grad
        branch = middle_grad.astype(BF16)
        branch_o[...] = branch
        bias_o[...] = jnp.sum(branch.astype(F32), axis=0, keepdims=True)


def attend_back_kernel(
    skip, count, info, normed, mixed, branch, q, k, v, p, wo, *refs
):
    refs = refs[count:]
    (
        keep_o, send_o, dq_o, dk_o, dv_o, qb_o, vb_o,
        grad_s, score_s, both,
    ) = refs
    step = pl.program_id(0) + skip
    length = normed.shape[0]
    mixed_grad = dot_nt(branch[...], wo[...]).astype(BF16)
    cols = pl.ds(pl.multiple_of(step * WIDE, WIDE), WIDE)
    grad_s[...] = dot_nt(mixed_grad, stack_heads(v[...], length))
    both[3] = dot_tn(mixed[...], branch[:, cols]).astype(BF16)
    dv = unstack_heads(dot_tn(p[0], mixed_grad), length).astype(BF16)
    rows = 64
    for top in range(0, length, rows):
        at = slice(top, top + rows)
        for h in range(GROUP):
            span = slice(h * length, (h + 1) * length)
            prob = p[0, at, span].astype(F32)
            weighted = prob * grad_s[at, span]
            center = jnp.sum(weighted, axis=-1, keepdims=True)
            score_s[at, span] = (weighted - prob * center).astype(BF16)
    dq = (dot(score_s[...], stack_heads(k[...], length)) * score_scale).astype(BF16)
    dk = (unstack_heads(dot_tn(score_s[...], q[...]), length) * score_scale).astype(BF16)
    dq_o[...] = dq
    dk_o[...] = dk
    dv_o[...] = dv
    qb_o[...] = jnp.sum(dq.astype(F32), axis=0, keepdims=True)
    vb_o[...] = jnp.sum(dv.astype(F32), axis=0, keepdims=True)
    both[0] = dot_tn(normed[...], dq).astype(BF16)
    both[1] = dot_tn(normed[...], dk).astype(BF16)
    both[2] = dot_tn(normed[...], dv).astype(BF16)
    for t in range(2):
        relative_store(
            info, lambda rows: (both[t, rows], both[2 + t, rows]),
            keep_o, send_o, t ^ info[2], t ^ info[4], normed.shape[1],
        )


def finish_kernel(
    info, tok, middle_grad, dq, dk, dv, wq, wk, wv, g1,
    middle, out_sum, b2, seg, tgt,
    qb, vb, ob, n2g, n2s, b2g, b1a, b1b, b1c,
    tokens_o, small_o, own_o, hop1_o, hop2_o, hop3_o,
    acc,
):
    step = pl.program_id(0)

    @pl.when(step == 0)
    def _():
        acc[...] = jnp.zeros_like(acc)
        output = (middle[...] + (out_sum[...] + vec(b2))).astype(BF16)
        places = located(seg, tgt, [info[0] ^ hop for hop in range(4)], output.shape[0])
        picked = dot_tn(places, output).astype(BF16)
        for hop, out in enumerate((own_o, hop1_o, hop2_o, hop3_o)):
            out[...] = picked[hop * out.shape[0] : (hop + 1) * out.shape[0]]

    acc[...] += dot_nt(dq[...], wq[...]) + dot_nt(dk[...], wk[...]) + dot_nt(dv[...], wv[...])

    @pl.when(step == pl.num_programs(0) - 1)
    def _():
        grad = acc[...]
        xhat, scale = standardize(tok[...].astype(F32))
        tokens_o[...] = (middle_grad[...] + norm_back(grad, xhat, scale, vec(g1))).astype(BF16)
        width = grad.shape[1]
        small_o[0:1, :] = qb[...]
        small_o[1:2, :] = vb[...]
        small_o[2:3, :] = ob[...]
        small_o[3:4, :] = jnp.sum(grad * xhat, axis=0, keepdims=True)
        small_o[4:5, :] = jnp.sum(grad, axis=0, keepdims=True)
        small_o[5:6, :] = n2g[...]
        small_o[6:7, :] = n2s[...]
        small_o[7:8, :] = b2g[...]
        row = 8
        for part in (b1a, b1b, b1c):
            for j in range(part.shape[1] // width):
                small_o[row : row + 1, :] = part[:, j * width : (j + 1) * width]
                row += 1


def place_kernel(part, names, first_call, *refs):
    info = refs[0]
    count = 2 * len(names)
    quarters = refs[1 : 1 + count]
    outs = refs[1 + count + (0 if first_call else 2) :][:2]
    mark, low_s, stage, in_sems, sems = refs[-5:]
    mark[...] = jnp.zeros_like(mark)
    half, width = quarters[0].shape
    rows = 2 * half // SPANS

    def send(n, k, side, tile, span):
        source = stage.at[n, pl.ds(k * rows, rows), :]
        at = pl.ds(pl.multiple_of(span * rows, rows), rows)
        sem = sems.at[n, k]
        columns = lambda t: pl.ds(pl.multiple_of(t * width, width), width)
        if part is not None:
            if side == 0:
                start = (tile + 2 * part) * width + span * rows
                target = outs[0].at[pl.ds(pl.multiple_of(start, rows), rows), :]
            else:
                target = outs[1].at[at, columns(tile + 2 * part)]
            pltpu.make_async_copy(source, target, sem).start()
        elif side == 0:
            pltpu.make_async_copy(source, outs[0].at[at, columns(tile)], sem).start()
        else:

            @pl.when(tile == 0)
            def _():
                pltpu.make_async_copy(source, outs[0].at[at, columns(2)], sem).start()

            @pl.when(tile == 1)
            def _():
                pltpu.make_async_copy(source, outs[1].at[at, :], sem).start()

    for n in range(count):
        pltpu.make_async_copy(quarters[n], low_s.at[n], in_sems.at[n]).start()
    for n in range(count):
        name, other = names[n // 2], n % 2
        tile = (name // 2) ^ info[2 + 2 * other]
        pltpu.make_async_copy(quarters[n], low_s.at[n], in_sems.at[n]).wait()
        for k in range(half // rows):
            stage[n, k * rows : (k + 1) * rows, :] = low_s[n, k * rows : (k + 1) * rows, :].astype(F32)
            span = ((name % 2) * (SPANS // 2) + k) ^ info[3 + 2 * other]
            for side in range(2):

                @pl.when((info[1] ^ other) == side)
                def _():
                    send(n, k, side, tile, span)

    for n in range(count):
        for k in range(half // rows):
            here = stage.at[n, pl.ds(k * rows, rows), :]
            pltpu.make_async_copy(here, here, sems.at[n, k]).wait()


def cost(micros):
    return pl.CostEstimate(
        flops=int(micros * 9e8), bytes_accessed=int(micros * 3.4e6), transcendentals=0
    )


def call(kernel, grid, ins, outs, scratch=(), micros=4, vmem=26, prefetch=0, aliases={}, line=None):
    extra = [] if line is None or line.last is None else [line.last]
    known = len(ins) + prefetch
    body = (lambda *refs: kernel(*refs[:known], *refs[known + 1 :])) if extra else kernel
    inner = pl.pallas_call(
        body,
        grid_spec=pltpu.PrefetchScalarGridSpec(
            num_scalar_prefetch=prefetch,
            grid=grid,
            in_specs=list(ins) + [pl.BlockSpec(memory_space=pl.ANY)] * len(extra),
            out_specs=[spec for spec, _ in outs],
            scratch_shapes=list(scratch),
        ),
        out_shape=[shape for _, shape in outs],
        input_output_aliases=aliases,
        compiler_params=pltpu.CompilerParams(vmem_limit_bytes=vmem * 2**20),
        cost_estimate=cost(micros if line is None or line.weight is None else line.weight),
    )
    return lambda *args: inner(
        *(pltpu.with_memory_space_constraint(a.array, a.space) if isinstance(a, Far) else a for a in args),
        *extra,
    )


class Far:
    space = pltpu.HBM

    def __init__(self, array):
        self.array = array


class Near(Far):
    space = pltpu.VMEM


def full(*shape):
    return pl.BlockSpec(shape, lambda *_: (0,) * len(shape))


def block(shape, index):
    return pl.BlockSpec(shape, index)


def sds(shape, dtype):
    return jax.ShapeDtypeStruct(shape, dtype)


def place(part, names, info, values, shapes, outs, line):
    half, width = values[0].shape
    rows = 2 * half // SPANS
    anywhere = pl.BlockSpec(memory_space=pl.ANY)
    count = len(values)
    outs = call(
        functools.partial(place_kernel, part, names, not outs),
        (),
        [pl.BlockSpec(memory_space=pltpu.SMEM)]
        + [anywhere] * (count + len(outs)),
        [(anywhere, pltpu.HBM(shape.shape, shape.dtype)) for shape in shapes]
        + [(pl.BlockSpec(memory_space=pltpu.VMEM), pltpu.VMEM((8, 128), F32))],
        [
            pltpu.VMEM((count, half, width), BF16),
            pltpu.VMEM((count, half, width), F32),
            pltpu.SemaphoreType.DMA((count,)),
            pltpu.SemaphoreType.DMA((count, half // rows)),
        ],
        micros=MOVE,
        vmem=16,
        line=line,
        aliases={1 + count + n: n for n in range(len(outs))},
    )(info, *values, *outs)
    line.last = outs[2]
    return outs[:2]


class Exchange:
    def __init__(self, rows, blk):
        self.blk = blk
        self.total = rows * blk
        self.bits = self.total.bit_length() - 1
        assert self.total == 1 << self.bits and blk == 4
        self.here = lax.axis_index("rows") * blk + lax.axis_index("blk")
        self.core = self.here & 1
        self.steps = self.bits - 1

    def pairs(self, masks):
        return [(i, i ^ masks[i & 1]) for i in range(self.total)]

    def move_core(self, value):
        return lax.ppermute(value, AXES, self.pairs((1, 1)))

    def swap_blocks(self, pieces):
        mine = self.here & (self.blk - 1)
        got = [lax.dynamic_index_in_dim(pieces, mine, 0, keepdims=False)]
        for hop in range(1, self.blk):
            send = lax.dynamic_index_in_dim(pieces, mine ^ hop, 0, keepdims=False)
            got.append(lax.ppermute(send, AXES, self.pairs((hop, hop))))
        return got


class Chunk:
    def __init__(self, ex, line, perms):
        self.ex = ex
        self.line = line
        base = list(range(1, ex.bits))
        self.orders = [[base[n] for n in perm] + base[LEVELS:] for perm in perms]

    def bits_of(self, order):
        return [(self.ex.here >> bit) & 1 for bit in order]

    def info(self):
        places = []
        for order in self.orders:
            bit = self.bits_of(order)
            places.append((bit[0], bit[1] * 4 + bit[2] * 2 + bit[3]))
        core = self.ex.core
        own = [jnp.where(core == 0, a, b) for a, b in zip(*places)]
        other = [jnp.where(core == 0, b, a) for a, b in zip(*places)]
        return jnp.stack([self.ex.here & (self.ex.blk - 1), core] + own + other).astype(jnp.int32)

    def move(self, level, value):
        masks = tuple(1 << order[level] for order in self.orders)
        return lax.ppermute(value, AXES, self.ex.pairs(masks))

    def add(self, level, which):
        rows = self.keep.shape[1] >> level
        width = self.keep.shape[2]
        if level == 0:
            self.got = []
        tile = pl.BlockSpec((None, rows, width), lambda _: (int(level == 0), which if level else 0, 0))
        strip = pl.BlockSpec((rows, width), lambda _: (which, 0))
        return self.line.run(
            add_kernel,
            [self.keep, self.recv] + self.got,
            [sds((rows, width), BF16)],
            [tile] * 2 + [strip] * len(self.got),
        )

    def total(self):
        span = self.add(LEVELS - 1, 0)
        rows = span.shape[0]
        bits = [
            jnp.where(self.ex.core == 0, a, b)
            for a, b in zip(*(self.bits_of(order)[LEVELS:] for order in self.orders))
        ]
        for level, bit in enumerate(bits, LEVELS):
            rows //= 2
            recv = self.move(level, lax.dynamic_slice_in_dim(span, (1 - bit) * rows, rows, 0))
            span = add_up([lax.dynamic_slice_in_dim(span, bit * rows, rows, 0), recv])
        for level, bit in reversed(list(enumerate(bits, LEVELS))):
            recv = self.move(level, span)
            low = jnp.where(bit == 0, span, recv)
            span = jnp.concatenate([low, jnp.where(bit == 0, recv, span)], axis=0)
        self.spans = {"p": span}

    def join(self):
        spans = [self.spans[name] for name in ("p", "g0", "g1", "g2") if name in self.spans]
        rows, width = spans[0].shape
        return self.line.run(join_kernel, spans, [sds((len(spans) * rows, width), BF16)])

    def do(self, step):
        if step == "c":
            self.recv = self.ex.move_core(self.send)
        elif step[0] == "r":
            level = int(step[1])
            total = self.add(level, 1)
            self.got.append(self.move(level, total))
        elif step == "f":
            self.total()
        elif step == "g0":
            self.spans[step] = self.move(3, self.spans["p"])
        elif step in ("g1", "g2"):
            self.spans[step] = self.move(2, self.spans["p" if step == "g1" else "g0"])
        elif step == "h":
            self.spans = {"p": self.join()}
        elif step == "j":
            self.quarters = {"A": self.join()}
        elif step == "g3":
            self.quarters["B"] = self.move(1, self.quarters["A"])
        elif step == "g4":
            self.quarters["C"] = self.move(0, self.quarters["A"])
        elif step == "g5":
            self.quarters["D"] = self.move(0, self.quarters["B"])
        else:
            name = step[1]
            self.others[name] = self.ex.move_core(self.quarters[name])


class Line:
    def __init__(self):
        self.last = None
        self.weight = None

    def run(self, kernel, ins, out_shapes, specs=None, vmem=16):
        after = [] if self.last is None else [self.last]
        near = pl.BlockSpec(memory_space=pltpu.VMEM)
        outs = pl.pallas_call(
            functools.partial(skip, len(after), kernel),
            grid=() if specs is None else (1,),
            in_specs=[pl.BlockSpec(memory_space=pl.ANY)] * len(after) + (specs or [near] * len(ins)),
            out_specs=[near if specs is None else full(*shape.shape) for shape in out_shapes],
            out_shape=out_shapes,
            compiler_params=pltpu.CompilerParams(vmem_limit_bytes=vmem * 2**20),
            cost_estimate=cost(STEP if self.weight is None else self.weight),
        )(*after, *ins)
        self.last = outs[0]
        return outs[0]


def skip(count, kernel, *refs):
    kernel(*refs[count:])


def add_kernel(*refs):
    out = refs[-1]
    height = 32 if out.shape[0] % 32 == 0 else out.shape[0]

    def body(n, _):
        at = pl.ds(pl.multiple_of(n * height, height), height)
        total = refs[0][at, :].astype(F32)
        for ref in refs[1:-1]:
            total = total + ref[at, :].astype(F32)
        out[at, :] = total.astype(BF16)
        return 0

    lax.fori_loop(0, out.shape[0] // height, body, 0)


def join_kernel(*refs):
    start = 0
    for ref in refs[:-1]:
        refs[-1][start : start + ref.shape[0], :] = ref[...]
        start += ref.shape[0]


def order_kernel(info, *refs):
    rows = refs[0].shape[0]
    for hop, ref in enumerate(refs[:-1]):
        refs[-1][pl.ds(pl.multiple_of((info[0] ^ hop) * rows, rows), rows), :] = ref[...]


def sum_kernel(one, other, out):
    out[...] = one[...] + other[...]


def add_up(terms):
    total = terms[0].astype(F32)
    for term in terms[1:]:
        total = total + term.astype(F32)
    return total.astype(BF16)


def local(
    mesh_rows, mesh_blk,
    tokens, seg_ids, target_index,
    qkv_weight, q_bias, v_bias, out_weight, out_bias,
    norm1_gain, norm1_shift, norm2_gain, norm2_shift,
    fc1_weight, fc1_bias, fc2_weight, fc2_bias,
    target_grad,
):
    ex = Exchange(mesh_rows, mesh_blk)
    count_rows, length, d = tokens.shape
    assert count_rows == 1
    ff = fc1_weight.shape[1]
    tiles = ff // d
    images, patches = target_grad.shape[1], target_grad.shape[2]
    per = images // mesh_blk
    groups = d // WIDE
    pieces = target_grad.reshape(mesh_blk, per * patches, d)
    got = ex.swap_blocks(pieces)
    tok = Far(tokens.reshape(length, d))
    seg, target_index = Far(seg_ids), Far(target_index)
    qkv_weight, q_bias, v_bias, out_weight, out_bias = map(
        Far, (qkv_weight, q_bias, v_bias, out_weight, out_bias)
    )
    norm1_gain, norm1_shift, norm2_gain, norm2_shift = map(
        Far, (norm1_gain, norm1_shift, norm2_gain, norm2_shift)
    )
    fc1_weight, fc1_bias, fc2_weight, fc2_bias = map(
        Far, (fc1_weight, fc1_bias, fc2_weight, fc2_bias)
    )
    picks = full(*target_index.array.shape)
    col = lambda g: (0, g)
    third = lambda n: lambda g: (0, n * groups + g)
    act = pltpu.VMEM((length, d), BF16)
    act32 = pltpu.VMEM((length, d), F32)
    act_far = pltpu.HBM((length, d), BF16)
    one = pltpu.VMEM((1, d), F32)
    vd = full(d)
    smem = pl.BlockSpec(memory_space=pltpu.SMEM)
    whole = full(length, d)
    strip = block((length, WIDE), col)
    wide = GROUP * length
    wide_spec = block((1, length, wide), lambda g: (g, 0, 0))

    line = Line()
    links = [Chunk(ex, line, perms) for perms in ORDERS]
    infos = [link.info() for link in links]
    for link, info in zip(links, infos):
        link.info_ref = info
    half = tiles // 2

    def mlp_specs(skip):
        return [
            block((d, d), lambda j, info: (0, skip + j)),
            block((d, d), lambda j, info: (skip + j, 0)),
            full(ff),
        ]

    def tile_outs(skip):
        return [
            (block((1, d, d), lambda j, info, n=n: ((j + skip) ^ info[n], 0, 0)), pltpu.HBM((half, d, d), BF16))
            for n in (2, 4)
        ]

    def b1_out(tiles):
        return block((1, d), lambda j, info: (0, j)), pltpu.VMEM((1, tiles * d), F32)

    both = pltpu.VMEM((2, d, d), BF16)
    piece = full(per * patches, d)
    pair_out = (block((2, d, WIDE), lambda g: (0, 0, g)), pltpu.HBM((2, d, d), BF16))
    links_by_name = dict(zip(("M1", "M2", "Q"), links))
    for link in links:
        link.others = {}
    fc_out = qkv_out = ()
    small_step = 0
    for step in SCHEDULE:
        line.weight = WEIGHTS.get(step)
        if step == "K0":
            normed, q, k, v, prob, mixed, middle, second = call(
                attend_kernel,
                (groups,),
                [
                    whole, full(1, length),
                    block((d, WIDE), third(0)), block((d, WIDE), third(1)), block((d, WIDE), third(2)),
                    block((WIDE, d), lambda g: (g, 0)),
                    vd, vd, vd, vd, vd, vd, vd,
                ],
                [
                    (whole, act_far), (strip, act_far), (strip, act_far), (strip, act_far),
                    (wide_spec, pltpu.HBM((groups, length, wide), BF16)),
                    (strip, act_far), (whole, act32), (whole, act),
                ],
                [
                    pltpu.VMEM((length, d), F32),
                    pltpu.VMEM((length, wide), F32),
                    pltpu.VMEM((2, d), F32),
                ],
                micros=11 * PACE, line=line,
            )(
                tok, seg, qkv_weight, qkv_weight, qkv_weight, out_weight, q_bias, v_bias, out_bias,
                norm1_gain, norm1_shift, norm2_gain, norm2_shift,
            )
        elif step == "K1":
            links[0].keep, links[0].send, out_sum, second_grad, b1a, out_grad, mlp_low, b2_grad = call(
                first_mlp_kernel,
                (half,),
                [whole, full(1, length), picks] + [piece] * 4 + mlp_specs(0),
                [
                    *tile_outs(0), (whole, act32), (whole, act32), b1_out(half),
                    (whole, act32), (whole, act), (full(1, d), one),
                ],
                [both, pltpu.VMEM((1, ff), F32)],
                micros=12 * PACE, prefetch=1, line=line,
            )(infos[0], Near(second), seg, target_index, *got, fc1_weight, fc2_weight, fc1_bias)
            line.last = b2_grad
        elif step == "K2a":
            links[1].keep, links[1].send, out_sum, second_grad, b1b = call(
                functools.partial(middle_mlp_kernel, half),
                (1,),
                [whole, whole] + mlp_specs(half) + [whole] * 2,
                [*tile_outs(0), (whole, act32), (whole, act32), b1_out(1)],
                [both, pltpu.VMEM((1, ff), F32)],
                micros=6 * PACE, prefetch=1, line=line,
            )(infos[1], Near(second), Near(mlp_low), fc1_weight, fc2_weight, fc1_bias, Near(out_sum), Near(second_grad))
            line.last = b1b
        elif step == "K2b":
            links[1].keep, links[1].send, out_sum, b1c, middle_grad, branch, n2g, n2s, ob_grad = call(
                functools.partial(second_mlp_kernel, half + 1),
                (1,),
                [whole, whole] + mlp_specs(half + 1) + [whole] * 4 + [vd] + [pl.BlockSpec(memory_space=pl.ANY)] * 2,
                [
                    *tile_outs(1), (whole, act32), b1_out(1),
                    (whole, act32), (whole, act), (full(1, d), one), (full(1, d), one), (full(1, d), one),
                ],
                [both, pltpu.VMEM((length, d), F32), pltpu.VMEM((1, ff), F32)],
                micros=7 * PACE, prefetch=1, line=line, aliases={11: 0, 12: 1},
            )(
                infos[1], Near(second), Near(mlp_low), fc1_weight, fc2_weight, fc1_bias,
                *map(Near, (out_sum, second_grad, middle, out_grad)), norm2_gain,
                Far(links[1].keep), Far(links[1].send),
            )
            line.last = ob_grad
        elif step in ("K3", "K3a", "K3b"):
            skip = FIRST if step == "K3b" else 0
            count = {"K3": groups, "K3a": FIRST, "K3b": groups - FIRST}[step]
            at = lambda g, skip=skip: (0, g + skip)
            some = block((length, WIDE), at)
            pair_out = (block((2, d, WIDE), lambda g, skip=skip: (0, 0, g + skip)), pltpu.HBM((2, d, d), BF16))
            row_out = (block((1, WIDE), at), pltpu.HBM((1, d), F32))
            earlier = [] if step != "K3b" else [links[2].keep, links[2].send, dq, dk, dv, qb_grad, vb_grad]
            links[2].keep, links[2].send, dq, dk, dv, qb_grad, vb_grad = call(
                functools.partial(attend_back_kernel, skip, len(earlier)),
                (count,),
                [
                    smem, whole, whole, whole, some, some, some,
                    block((1, length, wide), lambda g, skip=skip: (g + skip, 0, 0)),
                    block((WIDE, d), lambda g, skip=skip: (g + skip, 0)),
                ]
                + [pl.BlockSpec(memory_space=pl.ANY)] * len(earlier),
                [pair_out, pair_out, *[(some, act_far)] * 3, row_out, row_out],
                [
                    pltpu.VMEM((length, wide), F32),
                    pltpu.VMEM((length, wide), BF16),
                    pltpu.VMEM((4, d, WIDE), BF16),
                ],
                micros=4.5 * count * PACE, line=line,
                aliases={9 + n: n for n in range(len(earlier))},
            )(
                infos[2], Far(normed), Far(mixed), Near(branch), *map(Far, (q, k, v, prob)), out_weight,
                *map(Far, earlier),
            )
            line.last = dq
        elif step == "K4":
            tokens_grad, small, *picked = call(
                finish_kernel,
                (groups,),
                [
                    smem, whole, whole, strip, strip, strip,
                    block((d, WIDE), third(0)), block((d, WIDE), third(1)), block((d, WIDE), third(2)),
                    vd, whole, whole, vd, full(1, length), picks,
                ]
                + [full(1, d)] * 6 + [full(1, half * d)] + [full(1, d)] * 2,
                [
                    (whole, pltpu.HBM((length, d), BF16)),
                    (full(8 + tiles, d), sds((8 + tiles, d), F32)),
                    *[(full(per * patches, d), sds((per * patches, d), BF16))] * 4,
                ],
                [pltpu.VMEM((length, d), F32)],
                micros=7 * PACE, line=line,
            )(
                infos[0], tok, Near(middle_grad), *map(Far, (dq, dk, dv)), qkv_weight, qkv_weight, qkv_weight, norm1_gain,
                Near(middle), Near(out_sum), fc2_bias, seg, target_index,
                Far(qb_grad), Far(vb_grad), *map(Near, (ob_grad, n2g, n2s, b2_grad, b1a, b1b, b1c)),
            )
            line.last = small
        elif step == "T":
            swapped = picked[:1] + [
                lax.ppermute(picked[hop], AXES, ex.pairs((hop, hop))) for hop in range(1, mesh_blk)
            ]
        elif step == "t":
            targets = line.run(
                order_kernel,
                [infos[0], *swapped],
                [sds((images * patches, d), BF16)],
                [smem] + [full(per * patches, d)] * mesh_blk,
            )
        elif step == "S":
            small = line.run(sum_kernel, [small, small_recv], [sds(small.shape, F32)])
            small_step += 1
        elif step == "s":
            small_recv = lax.ppermute(small, AXES, ex.pairs((1 << small_step,) * 2))
        else:
            name, step = step.split()
            link = links_by_name[name]
            if step[0] != "v":
                link.do(step)
                continue
            names = ["ABCD".index(n) for n in step[1:]]
            values = [v for n in step[1:] for v in (link.quarters[n], link.others[n])]
            if name == "Q":
                shapes = [sds((d, 3 * d), F32), sds((d, d), F32)]
                qkv_out = place(None, names, link.info_ref, values, shapes, qkv_out, line)
            else:
                shapes = [sds((ff, d), F32), sds((d, ff), F32)]
                fc_out = place(int(name[1]) - 1, names, link.info_ref, values, shapes, fc_out, line)
    for _ in range(small_step, ex.bits):
        small = small + lax.ppermute(small, AXES, ex.pairs((1 << small_step,) * 2))
        small_step += 1
    fc2_full, fc1_full = fc_out
    qkv_full, out_full = qkv_out
    return (
        targets.reshape(1, images, patches, d),
        tokens_grad.reshape(count_rows, length, d),
        qkv_full,
        small[0], small[1],
        out_full,
        small[2], small[3], small[4], small[5], small[6],
        fc1_full,
        small[8:].reshape(ff),
        fc2_full,
        small[7],
    )


def solution(mesh):
    rows, blk = mesh.shape["rows"], mesh.shape["blk"]

    def body(*args):
        return local(rows, blk, *args)

    return jax.shard_map(
        body,
        mesh=mesh,
        in_specs=(
            P(("rows", "blk"), None, None),
            P(("rows", "blk"), None),
            P(("rows", "blk"), None, None),
        )
        + (P(),) * 13
        + (P("blk", "rows", None, None),),
        out_specs=(
            P("blk", "rows", None, None),
            P(("rows", "blk"), None, None),
        )
        + (P(),) * 13,
        check_vma=False,
    )
```

```python
import functools

import jax
import jax.numpy as jnp
from jax import lax
from jax.experimental import pallas as pl
from jax.experimental.pallas import tpu as pltpu
from jax.sharding import PartitionSpec as P

HEADS = 12
HEAD_DIM = 64
GROUP = 4
WIDE = GROUP * HEAD_DIM
LEVELS = 4
PIECE = 256
PACE = 1
STEP = 7
MOVE = 25
WEIGHTS = {
    "K1": 1,
    "K2a": 3,
    "K4": 40,
    "M1 f": 10,
    "M1 r0": 1,
    "M1 r1": 0,
    "M1 r3": 3,
    "M1 vABCD": 3,
    "M2 f": 40,
    "M2 j": 3,
    "M2 r3": 20,
    "M2 vABCD": 40,
    "Q r3": 3,
    "Q vAB": 80,
    "Q vCD": 200,
    "S": 0,
}
FIRST = 1
SPANS = 8
AXES = ("rows", "blk")
SCHEDULE = (
    "K0", "K1", "M1 c", "K2a", "M1 r0", "K2b", "K3", "M1 r1", "M2 c", "M2 r0", "Q c", "K4",
    "M1 r2", "s", "T", "Q r0", "S", "M1 r3", "M2 r1", "s", "M1 f", "M1 g1", "M2 r2", "Q r1",
    "M1 g0", "M1 g2", "S", "s", "M2 r3", "Q r2", "M1 j", "M1 g3", "M1 cA", "S", "s", "M1 g5",
    "M1 cB", "M1 g4", "M1 cC", "M2 f", "S", "Q r3", "Q f", "M2 g0", "M2 g1", "Q g0", "M1 cD", "Q g2",
    "s", "Q g1", "M2 g2", "M2 j", "M2 cA", "M2 g3", "M2 g4", "M2 g5", "M1 vABCD", "Q j", "Q cA", "M2 cC",
    "Q g4", "M2 cD", "Q g3", "M2 cB", "Q g5", "M2 vABCD", "S", "Q cB", "Q vAB", "Q cC", "Q cD", "Q vCD",
    "t",
)
ORDERS = (((0, 1, 2, 3), (1, 0, 2, 3)), ((0, 1, 2, 3), (1, 0, 2, 3)), ((0, 1, 2, 3), (1, 0, 2, 3)))
F32 = jnp.float32
BF16 = jnp.bfloat16

norm_eps = 1e-06
score_scale = 0.125
neg_large = -1e30


def dot(a, b):
    return lax.dot_general(a, b, (((1,), (0,)), ((), ())), preferred_element_type=F32)


def dot_nt(a, b):
    return lax.dot_general(a, b, (((1,), (1,)), ((), ())), preferred_element_type=F32)


def dot_tn(a, b):
    return lax.dot_general(a, b, (((0,), (0,)), ((), ())), preferred_element_type=F32)


def standardize(values):
    center = values - jnp.mean(values, axis=-1, keepdims=True)
    spread = jnp.mean(center * center, axis=-1, keepdims=True)
    scale = lax.rsqrt(spread + norm_eps)
    return center * scale, scale


def norm_back(grad, xhat, scale, gain):
    e = grad * gain
    mean_e = jnp.mean(e, axis=-1, keepdims=True)
    mean_ex = jnp.mean(e * xhat, axis=-1, keepdims=True)
    return (e - mean_e - xhat * mean_ex) * scale


def head_mask(rows, h):
    lane = lax.broadcasted_iota(jnp.int32, (rows, WIDE), 1)
    return (lane >= h * HEAD_DIM) & (lane < (h + 1) * HEAD_DIM)


def vec(ref):
    return ref[...].reshape(1, -1)


def stack_heads(values, length):
    return jnp.concatenate(
        [jnp.where(head_mask(length, h), values, jnp.zeros_like(values)) for h in range(GROUP)],
        axis=0,
    )


def unstack_heads(stacked, length):
    total = stacked[:length]
    for h in range(1, GROUP):
        total = jnp.where(head_mask(length, h), stacked[h * length : (h + 1) * length], total)
    return total


def attend_kernel(
    tok, seg, wq, wk, wv, wo, qb, vb, ob, g1, s1, g2, s2,
    normed_o, q_o, k_o, v_o, p_o, mixed_o, middle_o, second_o,
    acc, score_s, biases,
):
    step = pl.program_id(0)
    length, width = tok.shape
    cols = pl.ds(pl.multiple_of(step * WIDE, WIDE), WIDE)

    @pl.when(step == 0)
    def _():
        xhat, _ = standardize(tok[...].astype(F32))
        normed_o[...] = (xhat * vec(g1) + vec(s1)).astype(BF16)
        acc[...] = jnp.zeros_like(acc)
        biases[0:1, :] = vec(qb)
        biases[1:2, :] = vec(vb)

    normed = normed_o[...]
    q = (dot(normed, wq[...]) + biases[0:1, cols]).astype(BF16)
    k = dot(normed, wk[...]).astype(BF16)
    v = (dot(normed, wv[...]) + biases[1:2, cols]).astype(BF16)
    q_o[...] = q
    k_o[...] = k
    v_o[...] = v
    score_s[...] = dot_nt(q * jnp.asarray(score_scale, BF16), stack_heads(k, length))
    seg_row = seg[...]
    seg_col = jnp.broadcast_to(seg_row.astype(F32), (128, length)).T[:, :1].astype(jnp.int32)
    rows = 64
    for top in range(0, length, rows):
        at = slice(top, top + rows)
        allowed = seg_col[at] == seg_row
        for h in range(GROUP):
            span = slice(h * length, (h + 1) * length)
            scores = jnp.where(allowed, score_s[at, span], neg_large)
            raised = jnp.exp(scores - jnp.max(scores, axis=-1, keepdims=True))
            share = 1.0 / jnp.sum(raised, axis=-1, keepdims=True)
            p_o[0, at, span] = (raised * share).astype(BF16)
    mixed = dot(p_o[0], stack_heads(v, length)).astype(BF16)
    mixed_o[...] = mixed
    acc[...] += dot(mixed, wo[...])

    @pl.when(step == pl.num_programs(0) - 1)
    def _():
        middle = tok[...].astype(F32) + (acc[...] + vec(ob))
        middle_o[...] = middle
        xhat, _ = standardize(middle)
        second_o[...] = (xhat * vec(g2) + vec(s2)).astype(BF16)


def located(seg, tgt, blocks, length):
    rows = []
    starts = [
        jnp.sum(((seg[...] >= 0) & (seg[...] < image)).astype(jnp.int32))
        for image in range(tgt.shape[0])
    ]
    for block in blocks:
        for image, start in enumerate(starts):
            rows.append(tgt[image, pl.ds(block, 1), :] + start)
    row = jnp.concatenate(rows, axis=1)
    slots = lax.broadcasted_iota(jnp.int32, (length, row.shape[1]), 0)
    return (slots == row).astype(F32).astype(BF16)


def tile_bias(bias_s, skip, width):
    start = (pl.program_id(0) + skip) * width
    return bias_s[:, pl.ds(pl.multiple_of(start, width), width)]


def relative_store(info, pair, keep_o, send_o, keep_at, send_at, height):
    first = info[1] == 0
    rows = height // SPANS
    for n in range(SPANS):
        low, high = pair(slice(n * rows, (n + 1) * rows))
        keep_o[keep_at, pl.ds(pl.multiple_of((n ^ info[3]) * rows, rows), rows), :] = jnp.where(first, low, high)
        send_o[send_at, pl.ds(pl.multiple_of((n ^ info[5]) * rows, rows), rows), :] = jnp.where(first, high, low)


def mlp_steps(info, sn, low, w1, w2, bias, keep_o, send_o, out_o, grad_o, b1_o, both, active_s, hidden_s):
    width = low.shape[1]
    piece = PIECE
    for j in range(width // piece):
        cols = slice(j * piece, (j + 1) * piece)
        hidden = dot(sn, w1[:, cols]) + bias[:, cols]
        phi_cum = 0.5 + 0.5 * lax.erf(hidden * 0.7071067811865476)
        density = 0.3989422804014327 * jnp.exp(hidden * hidden * -0.5)
        active_s[:, cols] = (hidden * phi_cum).astype(BF16)
        hidden_grad = dot_nt(low, w2[cols, :]) * (phi_cum + hidden * density)
        hidden_low = hidden_grad.astype(BF16)
        b1_o[:, cols] = jnp.sum(hidden_low.astype(F32), axis=0, keepdims=True)
        hidden_s[:, cols] = hidden_low
    both[0] = dot_tn(active_s[...], low).astype(BF16)
    both[1] = dot_tn(sn, hidden_s[...]).astype(BF16)
    out_o[...] += dot(active_s[...], w2[...])
    grad_o[...] += dot_nt(hidden_s[...], w1[...])
    relative_store(info, lambda rows: (both[0, rows], both[1, rows]), keep_o, send_o, 0, 0, width)


def first_mlp_kernel(
    info, second, seg, tgt, own, got1, got2, got3, w1, w2, b1,
    keep_o, send_o, out_o, grad_o, b1_o, out_grad_o, mlp_o, bias_o,
    both, bias_s, active_s, hidden_s,
):
    @pl.when(pl.program_id(0) == 0)
    def _():
        bias_s[...] = vec(b1)
        me = info[0]
        places = located(seg, tgt, [me, me ^ 1, me ^ 2, me ^ 3], second.shape[0])
        pieces = jnp.concatenate([own[...], got1[...], got2[...], got3[...]], axis=0)
        total = dot(places, pieces)
        out_grad_o[...] = total
        low = total.astype(BF16)
        mlp_o[...] = low
        bias_o[...] = jnp.sum(low.astype(F32), axis=0, keepdims=True)
        out_o[...] = jnp.zeros_like(out_o)
        grad_o[...] = jnp.zeros_like(grad_o)

    bias = tile_bias(bias_s, 0, second.shape[1])
    mlp_steps(info, second[...], mlp_o[...], w1, w2, bias, keep_o, send_o, out_o, grad_o, b1_o, both, active_s, hidden_s)


def middle_mlp_kernel(
    first, info, second, mlp, w1, w2, b1, out_in, grad_in,
    keep_o, send_o, out_o, grad_o, b1_o,
    both, bias_s, active_s, hidden_s,
):
    @pl.when(pl.program_id(0) == 0)
    def _():
        bias_s[...] = vec(b1)
        out_o[...] = out_in[...]
        grad_o[...] = grad_in[...]

    bias = tile_bias(bias_s, first, second.shape[1])
    mlp_steps(info, second[...], mlp[...], w1, w2, bias, keep_o, send_o, out_o, grad_o, b1_o, both, active_s, hidden_s)


def second_mlp_kernel(
    first, info, second, mlp, w1, w2, b1, out_in, grad_in, middle, out_grad, gain, keep_in, send_in,
    keep_o, send_o, out_o, b1_o, middle_grad_o, branch_o, gain_o, shift_o, bias_o,
    both, grad_s, bias_s, active_s, hidden_s,
):
    step = pl.program_id(0)

    @pl.when(step == 0)
    def _():
        bias_s[...] = vec(b1)
        out_o[...] = out_in[...]
        grad_s[...] = grad_in[...]

    bias = tile_bias(bias_s, first, second.shape[1])
    mlp_steps(info, second[...], mlp[...], w1, w2, bias, keep_o, send_o, out_o, grad_s, b1_o, both, active_s, hidden_s)

    @pl.when(step == pl.num_programs(0) - 1)
    def _():
        grad = grad_s[...]
        xhat, scale = standardize(middle[...])
        gain_o[...] = jnp.sum(grad * xhat, axis=0, keepdims=True)
        shift_o[...] = jnp.sum(grad, axis=0, keepdims=True)
        middle_grad = out_grad[...] + norm_back(grad, xhat, scale, vec(gain))
        middle_grad_o[...] = middle_grad
        branch = middle_grad.astype(BF16)
        branch_o[...] = branch
        bias_o[...] = jnp.sum(branch.astype(F32), axis=0, keepdims=True)


def attend_back_kernel(
    skip, count, info, normed, mixed, branch, q, k, v, p, wo, *refs
):
    refs = refs[count:]
    (
        keep_o, send_o, dq_o, dk_o, dv_o, qb_o, vb_o,
        grad_s, score_s, both,
    ) = refs
    step = pl.program_id(0) + skip
    length = normed.shape[0]
    mixed_grad = dot_nt(branch[...], wo[...]).astype(BF16)
    cols = pl.ds(pl.multiple_of(step * WIDE, WIDE), WIDE)
    grad_s[...] = dot_nt(mixed_grad, stack_heads(v[...], length))
    both[3] = dot_tn(mixed[...], branch[:, cols]).astype(BF16)
    dv = unstack_heads(dot_tn(p[0], mixed_grad), length).astype(BF16)
    rows = 64
    for top in range(0, length, rows):
        at = slice(top, top + rows)
        for h in range(GROUP):
            span = slice(h * length, (h + 1) * length)
            prob = p[0, at, span].astype(F32)
            weighted = prob * grad_s[at, span]
            center = jnp.sum(weighted, axis=-1, keepdims=True)
            score_s[at, span] = (weighted - prob * center).astype(BF16)
    dq = (dot(score_s[...], stack_heads(k[...], length)) * score_scale).astype(BF16)
    dk = (unstack_heads(dot_tn(score_s[...], q[...]), length) * score_scale).astype(BF16)
    dq_o[...] = dq
    dk_o[...] = dk
    dv_o[...] = dv
    qb_o[...] = jnp.sum(dq.astype(F32), axis=0, keepdims=True)
    vb_o[...] = jnp.sum(dv.astype(F32), axis=0, keepdims=True)
    both[0] = dot_tn(normed[...], dq).astype(BF16)
    both[1] = dot_tn(normed[...], dk).astype(BF16)
    both[2] = dot_tn(normed[...], dv).astype(BF16)
    for t in range(2):
        relative_store(
            info, lambda rows: (both[t, rows], both[2 + t, rows]),
            keep_o, send_o, t ^ info[2], t ^ info[4], normed.shape[1],
        )


def finish_kernel(
    info, tok, middle_grad, dq, dk, dv, wq, wk, wv, g1,
    middle, out_sum, b2, seg, tgt,
    qb, vb, ob, n2g, n2s, b2g, b1a, b1b, b1c,
    tokens_o, small_o, own_o, hop1_o, hop2_o, hop3_o,
    acc,
):
    step = pl.program_id(0)

    @pl.when(step == 0)
    def _():
        acc[...] = jnp.zeros_like(acc)
        output = (middle[...] + (out_sum[...] + vec(b2))).astype(BF16)
        places = located(seg, tgt, [info[0] ^ hop for hop in range(4)], output.shape[0])
        picked = dot_tn(places, output).astype(BF16)
        for hop, out in enumerate((own_o, hop1_o, hop2_o, hop3_o)):
            out[...] = picked[hop * out.shape[0] : (hop + 1) * out.shape[0]]

    acc[...] += dot_nt(dq[...], wq[...]) + dot_nt(dk[...], wk[...]) + dot_nt(dv[...], wv[...])

    @pl.when(step == pl.num_programs(0) - 1)
    def _():
        grad = acc[...]
        xhat, scale = standardize(tok[...].astype(F32))
        tokens_o[...] = (middle_grad[...] + norm_back(grad, xhat, scale, vec(g1))).astype(BF16)
        width = grad.shape[1]
        small_o[0:1, :] = qb[...]
        small_o[1:2, :] = vb[...]
        small_o[2:3, :] = ob[...]
        small_o[3:4, :] = jnp.sum(grad * xhat, axis=0, keepdims=True)
        small_o[4:5, :] = jnp.sum(grad, axis=0, keepdims=True)
        small_o[5:6, :] = n2g[...]
        small_o[6:7, :] = n2s[...]
        small_o[7:8, :] = b2g[...]
        row = 8
        for part in (b1a, b1b, b1c):
            for j in range(part.shape[1] // width):
                small_o[row : row + 1, :] = part[:, j * width : (j + 1) * width]
                row += 1


def place_kernel(part, names, first_call, *refs):
    info = refs[0]
    count = 2 * len(names)
    quarters = refs[1 : 1 + count]
    outs = refs[1 + count + (0 if first_call else 2) :][:2]
    mark, low_s, stage, in_sems, sems = refs[-5:]
    mark[...] = jnp.zeros_like(mark)
    half, width = quarters[0].shape
    rows = 2 * half // SPANS

    def send(n, k, side, tile, span):
        source = stage.at[n, pl.ds(k * rows, rows), :]
        at = pl.ds(pl.multiple_of(span * rows, rows), rows)
        sem = sems.at[n, k]
        columns = lambda t: pl.ds(pl.multiple_of(t * width, width), width)
        if part is not None:
            if side == 0:
                start = (tile + 2 * part) * width + span * rows
                target = outs[0].at[pl.ds(pl.multiple_of(start, rows), rows), :]
            else:
                target = outs[1].at[at, columns(tile + 2 * part)]
            pltpu.make_async_copy(source, target, sem).start()
        elif side == 0:
            pltpu.make_async_copy(source, outs[0].at[at, columns(tile)], sem).start()
        else:

            @pl.when(tile == 0)
            def _():
                pltpu.make_async_copy(source, outs[0].at[at, columns(2)], sem).start()

            @pl.when(tile == 1)
            def _():
                pltpu.make_async_copy(source, outs[1].at[at, :], sem).start()

    for n in range(count):
        pltpu.make_async_copy(quarters[n], low_s.at[n], in_sems.at[n]).start()
    for n in range(count):
        name, other = names[n // 2], n % 2
        tile = (name // 2) ^ info[2 + 2 * other]
        pltpu.make_async_copy(quarters[n], low_s.at[n], in_sems.at[n]).wait()
        for k in range(half // rows):
            stage[n, k * rows : (k + 1) * rows, :] = low_s[n, k * rows : (k + 1) * rows, :].astype(F32)
            span = ((name % 2) * (SPANS // 2) + k) ^ info[3 + 2 * other]
            for side in range(2):

                @pl.when((info[1] ^ other) == side)
                def _():
                    send(n, k, side, tile, span)

    for n in range(count):
        for k in range(half // rows):
            here = stage.at[n, pl.ds(k * rows, rows), :]
            pltpu.make_async_copy(here, here, sems.at[n, k]).wait()


def cost(micros):
    return pl.CostEstimate(
        flops=int(micros * 9e8), bytes_accessed=int(micros * 3.4e6), transcendentals=0
    )


def call(kernel, grid, ins, outs, scratch=(), micros=4, vmem=26, prefetch=0, aliases={}, line=None):
    extra = [] if line is None or line.last is None else [line.last]
    known = len(ins) + prefetch
    body = (lambda *refs: kernel(*refs[:known], *refs[known + 1 :])) if extra else kernel
    inner = pl.pallas_call(
        body,
        grid_spec=pltpu.PrefetchScalarGridSpec(
            num_scalar_prefetch=prefetch,
            grid=grid,
            in_specs=list(ins) + [pl.BlockSpec(memory_space=pl.ANY)] * len(extra),
            out_specs=[spec for spec, _ in outs],
            scratch_shapes=list(scratch),
        ),
        out_shape=[shape for _, shape in outs],
        input_output_aliases=aliases,
        compiler_params=pltpu.CompilerParams(vmem_limit_bytes=vmem * 2**20),
        cost_estimate=cost(micros if line is None or line.weight is None else line.weight),
    )
    return lambda *args: inner(
        *(pltpu.with_memory_space_constraint(a.array, a.space) if isinstance(a, Far) else a for a in args),
        *extra,
    )


class Far:
    space = pltpu.HBM

    def __init__(self, array):
        self.array = array


class Near(Far):
    space = pltpu.VMEM


def full(*shape):
    return pl.BlockSpec(shape, lambda *_: (0,) * len(shape))


def block(shape, index):
    return pl.BlockSpec(shape, index)


def sds(shape, dtype):
    return jax.ShapeDtypeStruct(shape, dtype)


def place(part, names, info, values, shapes, outs, line):
    half, width = values[0].shape
    rows = 2 * half // SPANS
    anywhere = pl.BlockSpec(memory_space=pl.ANY)
    count = len(values)
    outs = call(
        functools.partial(place_kernel, part, names, not outs),
        (),
        [pl.BlockSpec(memory_space=pltpu.SMEM)]
        + [anywhere] * (count + len(outs)),
        [(anywhere, pltpu.HBM(shape.shape, shape.dtype)) for shape in shapes]
        + [(pl.BlockSpec(memory_space=pltpu.VMEM), pltpu.VMEM((8, 128), F32))],
        [
            pltpu.VMEM((count, half, width), BF16),
            pltpu.VMEM((count, half, width), F32),
            pltpu.SemaphoreType.DMA((count,)),
            pltpu.SemaphoreType.DMA((count, half // rows)),
        ],
        micros=MOVE,
        vmem=16,
        line=line,
        aliases={1 + count + n: n for n in range(len(outs))},
    )(info, *values, *outs)
    line.last = outs[2]
    return outs[:2]


class Exchange:
    def __init__(self, rows, blk):
        self.blk = blk
        self.total = rows * blk
        self.bits = self.total.bit_length() - 1
        assert self.total == 1 << self.bits and blk == 4
        self.here = lax.axis_index("rows") * blk + lax.axis_index("blk")
        self.core = self.here & 1
        self.steps = self.bits - 1

    def pairs(self, masks):
        return [(i, i ^ masks[i & 1]) for i in range(self.total)]

    def move_core(self, value):
        return lax.ppermute(value, AXES, self.pairs((1, 1)))

    def swap_blocks(self, pieces):
        mine = self.here & (self.blk - 1)
        got = [lax.dynamic_index_in_dim(pieces, mine, 0, keepdims=False)]
        for hop in range(1, self.blk):
            send = lax.dynamic_index_in_dim(pieces, mine ^ hop, 0, keepdims=False)
            got.append(lax.ppermute(send, AXES, self.pairs((hop, hop))))
        return got


class Chunk:
    def __init__(self, ex, line, perms):
        self.ex = ex
        self.line = line
        base = list(range(1, ex.bits))
        self.orders = [[base[n] for n in perm] + base[LEVELS:] for perm in perms]

    def bits_of(self, order):
        return [(self.ex.here >> bit) & 1 for bit in order]

    def info(self):
        places = []
        for order in self.orders:
            bit = self.bits_of(order)
            places.append((bit[0], bit[1] * 4 + bit[2] * 2 + bit[3]))
        core = self.ex.core
        own = [jnp.where(core == 0, a, b) for a, b in zip(*places)]
        other = [jnp.where(core == 0, b, a) for a, b in zip(*places)]
        return jnp.stack([self.ex.here & (self.ex.blk - 1), core] + own + other).astype(jnp.int32)

    def move(self, level, value):
        masks = tuple(1 << order[level] for order in self.orders)
        return lax.ppermute(value, AXES, self.ex.pairs(masks))

    def add(self, level, which):
        rows = self.keep.shape[1] >> level
        width = self.keep.shape[2]
        if level == 0:
            self.got = []
        tile = pl.BlockSpec((None, rows, width), lambda _: (int(level == 0), which if level else 0, 0))
        strip = pl.BlockSpec((rows, width), lambda _: (which, 0))
        return self.line.run(
            add_kernel,
            [self.keep, self.recv] + self.got,
            [sds((rows, width), BF16)],
            [tile] * 2 + [strip] * len(self.got),
        )

    def total(self):
        span = self.add(LEVELS - 1, 0)
        rows = span.shape[0]
        bits = [
            jnp.where(self.ex.core == 0, a, b)
            for a, b in zip(*(self.bits_of(order)[LEVELS:] for order in self.orders))
        ]
        for level, bit in enumerate(bits, LEVELS):
            rows //= 2
            recv = self.move(level, lax.dynamic_slice_in_dim(span, (1 - bit) * rows, rows, 0))
            span = add_up([lax.dynamic_slice_in_dim(span, bit * rows, rows, 0), recv])
        for level, bit in reversed(list(enumerate(bits, LEVELS))):
            recv = self.move(level, span)
            low = jnp.where(bit == 0, span, recv)
            span = jnp.concatenate([low, jnp.where(bit == 0, recv, span)], axis=0)
        self.spans = {"p": span}

    def join(self):
        spans = [self.spans[name] for name in ("p", "g0", "g1", "g2") if name in self.spans]
        rows, width = spans[0].shape
        return self.line.run(join_kernel, spans, [sds((len(spans) * rows, width), BF16)])

    def do(self, step):
        if step == "c":
            self.recv = self.ex.move_core(self.send)
        elif step[0] == "r":
            level = int(step[1])
            total = self.add(level, 1)
            self.got.append(self.move(level, total))
        elif step == "f":
            self.total()
        elif step == "g0":
            self.spans[step] = self.move(3, self.spans["p"])
        elif step in ("g1", "g2"):
            self.spans[step] = self.move(2, self.spans["p" if step == "g1" else "g0"])
        elif step == "h":
            self.spans = {"p": self.join()}
        elif step == "j":
            self.quarters = {"A": self.join()}
        elif step == "g3":
            self.quarters["B"] = self.move(1, self.quarters["A"])
        elif step == "g4":
            self.quarters["C"] = self.move(0, self.quarters["A"])
        elif step == "g5":
            self.quarters["D"] = self.move(0, self.quarters["B"])
        else:
            name = step[1]
            self.others[name] = self.ex.move_core(self.quarters[name])


class Line:
    def __init__(self):
        self.last = None
        self.weight = None

    def run(self, kernel, ins, out_shapes, specs=None, vmem=16):
        after = [] if self.last is None else [self.last]
        near = pl.BlockSpec(memory_space=pltpu.VMEM)
        outs = pl.pallas_call(
            functools.partial(skip, len(after), kernel),
            grid=() if specs is None else (1,),
            in_specs=[pl.BlockSpec(memory_space=pl.ANY)] * len(after) + (specs or [near] * len(ins)),
            out_specs=[near if specs is None else full(*shape.shape) for shape in out_shapes],
            out_shape=out_shapes,
            compiler_params=pltpu.CompilerParams(vmem_limit_bytes=vmem * 2**20),
            cost_estimate=cost(STEP if self.weight is None else self.weight),
        )(*after, *ins)
        self.last = outs[0]
        return outs[0]


def skip(count, kernel, *refs):
    kernel(*refs[count:])


def add_kernel(*refs):
    out = refs[-1]
    height = 32 if out.shape[0] % 32 == 0 else out.shape[0]

    def body(n, _):
        at = pl.ds(pl.multiple_of(n * height, height), height)
        total = refs[0][at, :].astype(F32)
        for ref in refs[1:-1]:
            total = total + ref[at, :].astype(F32)
        out[at, :] = total.astype(BF16)
        return 0

    lax.fori_loop(0, out.shape[0] // height, body, 0)


def join_kernel(*refs):
    start = 0
    for ref in refs[:-1]:
        refs[-1][start : start + ref.shape[0], :] = ref[...]
        start += ref.shape[0]


def order_kernel(info, *refs):
    rows = refs[0].shape[0]
    for hop, ref in enumerate(refs[:-1]):
        refs[-1][pl.ds(pl.multiple_of((info[0] ^ hop) * rows, rows), rows), :] = ref[...]


def sum_kernel(one, other, out):
    out[...] = one[...] + other[...]


def add_up(terms):
    total = terms[0].astype(F32)
    for term in terms[1:]:
        total = total + term.astype(F32)
    return total.astype(BF16)


def local(
    mesh_rows, mesh_blk,
    tokens, seg_ids, target_index,
    qkv_weight, q_bias, v_bias, out_weight, out_bias,
    norm1_gain, norm1_shift, norm2_gain, norm2_shift,
    fc1_weight, fc1_bias, fc2_weight, fc2_bias,
    target_grad,
):
    ex = Exchange(mesh_rows, mesh_blk)
    count_rows, length, d = tokens.shape
    assert count_rows == 1
    ff = fc1_weight.shape[1]
    tiles = ff // d
    images, patches = target_grad.shape[1], target_grad.shape[2]
    per = images // mesh_blk
    groups = d // WIDE
    pieces = target_grad.reshape(mesh_blk, per * patches, d)
    got = ex.swap_blocks(pieces)
    tok = Far(tokens.reshape(length, d))
    seg, target_index = Far(seg_ids), Far(target_index)
    qkv_weight, q_bias, v_bias, out_weight, out_bias = map(
        Far, (qkv_weight, q_bias, v_bias, out_weight, out_bias)
    )
    norm1_gain, norm1_shift, norm2_gain, norm2_shift = map(
        Far, (norm1_gain, norm1_shift, norm2_gain, norm2_shift)
    )
    fc1_weight, fc1_bias, fc2_weight, fc2_bias = map(
        Far, (fc1_weight, fc1_bias, fc2_weight, fc2_bias)
    )
    picks = full(*target_index.array.shape)
    col = lambda g: (0, g)
    third = lambda n: lambda g: (0, n * groups + g)
    act = pltpu.VMEM((length, d), BF16)
    act32 = pltpu.VMEM((length, d), F32)
    act_far = pltpu.HBM((length, d), BF16)
    one = pltpu.VMEM((1, d), F32)
    vd = full(d)
    smem = pl.BlockSpec(memory_space=pltpu.SMEM)
    whole = full(length, d)
    strip = block((length, WIDE), col)
    wide = GROUP * length
    wide_spec = block((1, length, wide), lambda g: (g, 0, 0))

    line = Line()
    links = [Chunk(ex, line, perms) for perms in ORDERS]
    infos = [link.info() for link in links]
    for link, info in zip(links, infos):
        link.info_ref = info
    half = tiles // 2

    def mlp_specs(skip):
        return [
            block((d, d), lambda j, info: (0, skip + j)),
            block((d, d), lambda j, info: (skip + j, 0)),
            full(ff),
        ]

    def tile_outs(skip):
        return [
            (block((1, d, d), lambda j, info, n=n: ((j + skip) ^ info[n], 0, 0)), pltpu.HBM((half, d, d), BF16))
            for n in (2, 4)
        ]

    def b1_out(tiles):
        return block((1, d), lambda j, info: (0, j)), pltpu.VMEM((1, tiles * d), F32)

    both = pltpu.VMEM((2, d, d), BF16)
    saved = [pltpu.VMEM((length, d), BF16)] * 2
    piece = full(per * patches, d)
    pair_out = (block((2, d, WIDE), lambda g: (0, 0, g)), pltpu.HBM((2, d, d), BF16))
    links_by_name = dict(zip(("M1", "M2", "Q"), links))
    for link in links:
        link.others = {}
    fc_out = qkv_out = ()
    small_step = 0
    for step in SCHEDULE:
        line.weight = WEIGHTS.get(step)
        if step == "K0":
            normed, q, k, v, prob, mixed, middle, second = call(
                attend_kernel,
                (groups,),
                [
                    whole, full(1, length),
                    block((d, WIDE), third(0)), block((d, WIDE), third(1)), block((d, WIDE), third(2)),
                    block((WIDE, d), lambda g: (g, 0)),
                    vd, vd, vd, vd, vd, vd, vd,
                ],
                [
                    (whole, act_far), (strip, act_far), (strip, act_far), (strip, act_far),
                    (wide_spec, pltpu.HBM((groups, length, wide), BF16)),
                    (strip, act_far), (whole, act32), (whole, act),
                ],
                [
                    pltpu.VMEM((length, d), F32),
                    pltpu.VMEM((length, wide), F32),
                    pltpu.VMEM((2, d), F32),
                ],
                micros=11 * PACE, line=line,
            )(
                tok, seg, qkv_weight, qkv_weight, qkv_weight, out_weight, q_bias, v_bias, out_bias,
                norm1_gain, norm1_shift, norm2_gain, norm2_shift,
            )
        elif step == "K1":
            links[0].keep, links[0].send, out_sum, second_grad, b1a, out_grad, mlp_low, b2_grad = call(
                first_mlp_kernel,
                (half,),
                [whole, full(1, length), picks] + [piece] * 4 + mlp_specs(0),
                [
                    *tile_outs(0), (whole, act32), (whole, act32), b1_out(half),
                    (whole, act32), (whole, act), (full(1, d), one),
                ],
                [both, pltpu.VMEM((1, ff), F32), *saved],
                micros=12 * PACE, prefetch=1, line=line,
            )(infos[0], Near(second), seg, target_index, *got, fc1_weight, fc2_weight, fc1_bias)
            line.last = b2_grad
        elif step == "K2a":
            links[1].keep, links[1].send, out_sum, second_grad, b1b = call(
                functools.partial(middle_mlp_kernel, half),
                (1,),
                [whole, whole] + mlp_specs(half) + [whole] * 2,
                [*tile_outs(0), (whole, act32), (whole, act32), b1_out(1)],
                [both, pltpu.VMEM((1, ff), F32), *saved],
                micros=6 * PACE, prefetch=1, line=line,
            )(infos[1], Near(second), Near(mlp_low), fc1_weight, fc2_weight, fc1_bias, Near(out_sum), Near(second_grad))
            line.last = b1b
        elif step == "K2b":
            links[1].keep, links[1].send, out_sum, b1c, middle_grad, branch, n2g, n2s, ob_grad = call(
                functools.partial(second_mlp_kernel, half + 1),
                (1,),
                [whole, whole] + mlp_specs(half + 1) + [whole] * 4 + [vd] + [pl.BlockSpec(memory_space=pl.ANY)] * 2,
                [
                    *tile_outs(1), (whole, act32), b1_out(1),
                    (whole, act32), (whole, act), (full(1, d), one), (full(1, d), one), (full(1, d), one),
                ],
                [both, pltpu.VMEM((length, d), F32), pltpu.VMEM((1, ff), F32), *saved],
                micros=7 * PACE, prefetch=1, line=line, aliases={11: 0, 12: 1},
            )(
                infos[1], Near(second), Near(mlp_low), fc1_weight, fc2_weight, fc1_bias,
                *map(Near, (out_sum, second_grad, middle, out_grad)), norm2_gain,
                Far(links[1].keep), Far(links[1].send),
            )
            line.last = ob_grad
        elif step in ("K3", "K3a", "K3b"):
            skip = FIRST if step == "K3b" else 0
            count = {"K3": groups, "K3a": FIRST, "K3b": groups - FIRST}[step]
            at = lambda g, skip=skip: (0, g + skip)
            some = block((length, WIDE), at)
            pair_out = (block((2, d, WIDE), lambda g, skip=skip: (0, 0, g + skip)), pltpu.HBM((2, d, d), BF16))
            row_out = (block((1, WIDE), at), pltpu.HBM((1, d), F32))
            earlier = [] if step != "K3b" else [links[2].keep, links[2].send, dq, dk, dv, qb_grad, vb_grad]
            links[2].keep, links[2].send, dq, dk, dv, qb_grad, vb_grad = call(
                functools.partial(attend_back_kernel, skip, len(earlier)),
                (count,),
                [
                    smem, whole, whole, whole, some, some, some,
                    block((1, length, wide), lambda g, skip=skip: (g + skip, 0, 0)),
                    block((WIDE, d), lambda g, skip=skip: (g + skip, 0)),
                ]
                + [pl.BlockSpec(memory_space=pl.ANY)] * len(earlier),
                [pair_out, pair_out, *[(some, act_far)] * 3, row_out, row_out],
                [
                    pltpu.VMEM((length, wide), F32),
                    pltpu.VMEM((length, wide), BF16),
                    pltpu.VMEM((4, d, WIDE), BF16),
                ],
                micros=4.5 * count * PACE, line=line,
                aliases={9 + n: n for n in range(len(earlier))},
            )(
                infos[2], Far(normed), Far(mixed), Near(branch), *map(Far, (q, k, v, prob)), out_weight,
                *map(Far, earlier),
            )
            line.last = dq
        elif step == "K4":
            tokens_grad, small, *picked = call(
                finish_kernel,
                (groups,),
                [
                    smem, whole, whole, strip, strip, strip,
                    block((d, WIDE), third(0)), block((d, WIDE), third(1)), block((d, WIDE), third(2)),
                    vd, whole, whole, vd, full(1, length), picks,
                ]
                + [full(1, d)] * 6 + [full(1, half * d)] + [full(1, d)] * 2,
                [
                    (whole, pltpu.HBM((length, d), BF16)),
                    (full(8 + tiles, d), sds((8 + tiles, d), F32)),
                    *[(full(per * patches, d), sds((per * patches, d), BF16))] * 4,
                ],
                [pltpu.VMEM((length, d), F32)],
                micros=7 * PACE, line=line,
            )(
                infos[0], tok, Near(middle_grad), *map(Far, (dq, dk, dv)), qkv_weight, qkv_weight, qkv_weight, norm1_gain,
                Near(middle), Near(out_sum), fc2_bias, seg, target_index,
                Far(qb_grad), Far(vb_grad), *map(Near, (ob_grad, n2g, n2s, b2_grad, b1a, b1b, b1c)),
            )
            line.last = small
        elif step == "T":
            swapped = picked[:1] + [
                lax.ppermute(picked[hop], AXES, ex.pairs((hop, hop))) for hop in range(1, mesh_blk)
            ]
        elif step == "t":
            targets = line.run(
                order_kernel,
                [infos[0], *swapped],
                [sds((images * patches, d), BF16)],
                [smem] + [full(per * patches, d)] * mesh_blk,
            )
        elif step == "S":
            small = line.run(sum_kernel, [small, small_recv], [sds(small.shape, F32)])
            small_step += 1
        elif step == "s":
            small_recv = lax.ppermute(small, AXES, ex.pairs((1 << small_step,) * 2))
        else:
            name, step = step.split()
            link = links_by_name[name]
            if step[0] != "v":
                link.do(step)
                continue
            names = ["ABCD".index(n) for n in step[1:]]
            values = [v for n in step[1:] for v in (link.quarters[n], link.others[n])]
            if name == "Q":
                shapes = [sds((d, 3 * d), F32), sds((d, d), F32)]
                qkv_out = place(None, names, link.info_ref, values, shapes, qkv_out, line)
            else:
                shapes = [sds((ff, d), F32), sds((d, ff), F32)]
                fc_out = place(int(name[1]) - 1, names, link.info_ref, values, shapes, fc_out, line)
    for _ in range(small_step, ex.bits):
        small = small + lax.ppermute(small, AXES, ex.pairs((1 << small_step,) * 2))
        small_step += 1
    fc2_full, fc1_full = fc_out
    qkv_full, out_full = qkv_out
    return (
        targets.reshape(1, images, patches, d),
        tokens_grad.reshape(count_rows, length, d),
        qkv_full,
        small[0], small[1],
        out_full,
        small[2], small[3], small[4], small[5], small[6],
        fc1_full,
        small[8:].reshape(ff),
        fc2_full,
        small[7],
    )


def solution(mesh):
    rows, blk = mesh.shape["rows"], mesh.shape["blk"]

    def body(*args):
        return local(rows, blk, *args)

    return jax.shard_map(
        body,
        mesh=mesh,
        in_specs=(
            P(("rows", "blk"), None, None),
            P(("rows", "blk"), None),
            P(("rows", "blk"), None, None),
        )
        + (P(),) * 13
        + (P("blk", "rows", None, None),),
        out_specs=(
            P("blk", "rows", None, None),
            P(("rows", "blk"), None, None),
        )
        + (P(),) * 13,
        check_vma=False,
    )
```

```python
import functools

import jax
import jax.numpy as jnp
from jax import lax
from jax.experimental import pallas as pl
from jax.experimental.pallas import tpu as pltpu
from jax.sharding import PartitionSpec as P

HEADS = 12
HEAD_DIM = 64
GROUP = 4
WIDE = GROUP * HEAD_DIM
LEVELS = 4
PIECE = 256
PACE = 2
STEP = 7
MOVE = 25
WEIGHTS = {
    "K1": 200,
    "K2a": 3,
    "K3": 80,
    "K4": 40,
    "M1 f": 10,
    "M1 j": 1,
    "M1 r0": 1,
    "M1 r1": 0,
    "M1 r3": 3,
    "M1 vABCD": 3,
    "M2 j": 3,
    "M2 r3": 20,
    "M2 vABCD": 20,
    "Q r0": 0,
    "Q r3": 3,
    "Q vAB": 80,
    "Q vCD": 200,
    "S": 0,
}
FIRST = 1
SPANS = 8
AXES = ("rows", "blk")
SCHEDULE = (
    "K0", "K1", "M1 c", "K2a", "M1 r0", "K2b", "K3", "M1 r1", "M2 c", "M2 r0", "Q c", "K4",
    "M1 r2", "s", "T", "Q r0", "M1 r3", "M2 r1", "S", "s", "M1 f", "M1 g1", "M2 r2", "Q r1",
    "M1 g0", "M2 r3", "Q r2", "M1 g2", "S", "s", "M1 j", "S", "M1 g4", "M1 g3", "M1 cA", "M2 f",
    "s", "M1 g5", "M1 cB", "S", "Q r3", "Q f", "M2 g0", "M2 g1", "M1 cD", "Q g0", "Q g2", "s",
    "Q g1", "M2 g2", "M2 j", "M2 cA", "M2 g3", "M2 g4", "M2 g5", "M1 cC", "M1 vABCD", "Q j", "Q cA", "M2 cC",
    "Q g4", "M2 cD", "Q g3", "M2 cB", "Q g5", "Q cD", "M2 vABCD", "S", "Q cB", "Q vAB", "Q cC", "Q vCD",
    "t",
)
ORDERS = (((0, 1, 2, 3), (1, 0, 2, 3)), ((0, 1, 2, 3), (1, 0, 2, 3)), ((0, 1, 2, 3), (1, 0, 2, 3)))
F32 = jnp.float32
BF16 = jnp.bfloat16

norm_eps = 1e-06
score_scale = 0.125
neg_large = -1e30


def dot(a, b):
    return lax.dot_general(a, b, (((1,), (0,)), ((), ())), preferred_element_type=F32)


def dot_nt(a, b):
    return lax.dot_general(a, b, (((1,), (1,)), ((), ())), preferred_element_type=F32)


def dot_tn(a, b):
    return lax.dot_general(a, b, (((0,), (0,)), ((), ())), preferred_element_type=F32)


def standardize(values):
    center = values - jnp.mean(values, axis=-1, keepdims=True)
    spread = jnp.mean(center * center, axis=-1, keepdims=True)
    scale = lax.rsqrt(spread + norm_eps)
    return center * scale, scale


def norm_back(grad, xhat, scale, gain):
    e = grad * gain
    mean_e = jnp.mean(e, axis=-1, keepdims=True)
    mean_ex = jnp.mean(e * xhat, axis=-1, keepdims=True)
    return (e - mean_e - xhat * mean_ex) * scale


def head_mask(rows, h):
    lane = lax.broadcasted_iota(jnp.int32, (rows, WIDE), 1)
    return (lane >= h * HEAD_DIM) & (lane < (h + 1) * HEAD_DIM)


def vec(ref):
    return ref[...].reshape(1, -1)


def stack_heads(values, length):
    return jnp.concatenate(
        [jnp.where(head_mask(length, h), values, jnp.zeros_like(values)) for h in range(GROUP)],
        axis=0,
    )


def unstack_heads(stacked, length):
    total = stacked[:length]
    for h in range(1, GROUP):
        total = jnp.where(head_mask(length, h), stacked[h * length : (h + 1) * length], total)
    return total


def attend_kernel(
    tok, seg, wq, wk, wv, wo, qb, vb, ob, g1, s1, g2, s2,
    normed_o, q_o, k_o, v_o, p_o, mixed_o, middle_o, second_o,
    acc, score_s, biases,
):
    step = pl.program_id(0)
    length, width = tok.shape
    cols = pl.ds(pl.multiple_of(step * WIDE, WIDE), WIDE)

    @pl.when(step == 0)
    def _():
        xhat, _ = standardize(tok[...].astype(F32))
        normed_o[...] = (xhat * vec(g1) + vec(s1)).astype(BF16)
        acc[...] = jnp.zeros_like(acc)
        biases[0:1, :] = vec(qb)
        biases[1:2, :] = vec(vb)

    normed = normed_o[...]
    q = (dot(normed, wq[...]) + biases[0:1, cols]).astype(BF16)
    k = dot(normed, wk[...]).astype(BF16)
    v = (dot(normed, wv[...]) + biases[1:2, cols]).astype(BF16)
    q_o[...] = q
    k_o[...] = k
    v_o[...] = v
    score_s[...] = dot_nt(q * jnp.asarray(score_scale, BF16), stack_heads(k, length))
    seg_row = seg[...]
    seg_col = jnp.broadcast_to(seg_row.astype(F32), (128, length)).T[:, :1].astype(jnp.int32)
    rows = 64
    for top in range(0, length, rows):
        at = slice(top, top + rows)
        allowed = seg_col[at] == seg_row
        for h in range(GROUP):
            span = slice(h * length, (h + 1) * length)
            scores = jnp.where(allowed, score_s[at, span], neg_large)
            raised = jnp.exp(scores - jnp.max(scores, axis=-1, keepdims=True))
            share = 1.0 / jnp.sum(raised, axis=-1, keepdims=True)
            p_o[0, at, span] = (raised * share).astype(BF16)
    mixed = dot(p_o[0], stack_heads(v, length)).astype(BF16)
    mixed_o[...] = mixed
    acc[...] += dot(mixed, wo[...])

    @pl.when(step == pl.num_programs(0) - 1)
    def _():
        middle = tok[...].astype(F32) + (acc[...] + vec(ob))
        middle_o[...] = middle
        xhat, _ = standardize(middle)
        second_o[...] = (xhat * vec(g2) + vec(s2)).astype(BF16)


def located(seg, tgt, blocks, length):
    rows = []
    starts = [
        jnp.sum(((seg[...] >= 0) & (seg[...] < image)).astype(jnp.int32))
        for image in range(tgt.shape[0])
    ]
    for block in blocks:
        for image, start in enumerate(starts):
            rows.append(tgt[image, pl.ds(block, 1), :] + start)
    row = jnp.concatenate(rows, axis=1)
    slots = lax.broadcasted_iota(jnp.int32, (length, row.shape[1]), 0)
    return (slots == row).astype(F32).astype(BF16)


def tile_bias(bias_s, skip, width):
    start = (pl.program_id(0) + skip) * width
    return bias_s[:, pl.ds(pl.multiple_of(start, width), width)]


def relative_store(info, pair, keep_o, send_o, keep_at, send_at, height):
    first = info[1] == 0
    rows = height // SPANS
    for n in range(SPANS):
        low, high = pair(slice(n * rows, (n + 1) * rows))
        keep_o[keep_at, pl.ds(pl.multiple_of((n ^ info[3]) * rows, rows), rows), :] = jnp.where(first, low, high)
        send_o[send_at, pl.ds(pl.multiple_of((n ^ info[5]) * rows, rows), rows), :] = jnp.where(first, high, low)


def mlp_steps(info, sn, low, w1, w2, bias, keep_o, send_o, out_o, grad_o, b1_o, both, active_s, hidden_s):
    width = low.shape[1]
    piece = PIECE
    for j in range(width // piece):
        cols = slice(j * piece, (j + 1) * piece)
        hidden = dot(sn, w1[:, cols]) + bias[:, cols]
        phi_cum = 0.5 + 0.5 * lax.erf(hidden * 0.7071067811865476)
        density = 0.3989422804014327 * jnp.exp(hidden * hidden * -0.5)
        active_s[:, cols] = (hidden * phi_cum).astype(BF16)
        hidden_grad = dot_nt(low, w2[cols, :]) * (phi_cum + hidden * density)
        hidden_low = hidden_grad.astype(BF16)
        b1_o[:, cols] = jnp.sum(hidden_low.astype(F32), axis=0, keepdims=True)
        hidden_s[:, cols] = hidden_low
    both[0] = dot_tn(active_s[...], low).astype(BF16)
    both[1] = dot_tn(sn, hidden_s[...]).astype(BF16)
    out_o[...] += dot(active_s[...], w2[...])
    grad_o[...] += dot_nt(hidden_s[...], w1[...])
    relative_store(info, lambda rows: (both[0, rows], both[1, rows]), keep_o, send_o, 0, 0, width)


def first_mlp_kernel(
    info, second, seg, tgt, own, got1, got2, got3, w1, w2, b1,
    keep_o, send_o, out_o, grad_o, b1_o, out_grad_o, mlp_o, bias_o,
    both, bias_s, active_s, hidden_s,
):
    @pl.when(pl.program_id(0) == 0)
    def _():
        bias_s[...] = vec(b1)
        me = info[0]
        places = located(seg, tgt, [me, me ^ 1, me ^ 2, me ^ 3], second.shape[0])
        pieces = jnp.concatenate([own[...], got1[...], got2[...], got3[...]], axis=0)
        total = dot(places, pieces)
        out_grad_o[...] = total
        low = total.astype(BF16)
        mlp_o[...] = low
        bias_o[...] = jnp.sum(low.astype(F32), axis=0, keepdims=True)
        out_o[...] = jnp.zeros_like(out_o)
        grad_o[...] = jnp.zeros_like(grad_o)

    bias = tile_bias(bias_s, 0, second.shape[1])
    mlp_steps(info, second[...], mlp_o[...], w1, w2, bias, keep_o, send_o, out_o, grad_o, b1_o, both, active_s, hidden_s)


def middle_mlp_kernel(
    first, info, second, mlp, w1, w2, b1, out_in, grad_in,
    keep_o, send_o, out_o, grad_o, b1_o,
    both, bias_s, active_s, hidden_s,
):
    @pl.when(pl.program_id(0) == 0)
    def _():
        bias_s[...] = vec(b1)
        out_o[...] = out_in[...]
        grad_o[...] = grad_in[...]

    bias = tile_bias(bias_s, first, second.shape[1])
    mlp_steps(info, second[...], mlp[...], w1, w2, bias, keep_o, send_o, out_o, grad_o, b1_o, both, active_s, hidden_s)


def second_mlp_kernel(
    first, info, second, mlp, w1, w2, b1, out_in, grad_in, middle, out_grad, gain, keep_in, send_in,
    keep_o, send_o, out_o, b1_o, middle_grad_o, branch_o, gain_o, shift_o, bias_o,
    both, grad_s, bias_s, active_s, hidden_s,
):
    step = pl.program_id(0)

    @pl.when(step == 0)
    def _():
        bias_s[...] = vec(b1)
        out_o[...] = out_in[...]
        grad_s[...] = grad_in[...]

    bias = tile_bias(bias_s, first, second.shape[1])
    mlp_steps(info, second[...], mlp[...], w1, w2, bias, keep_o, send_o, out_o, grad_s, b1_o, both, active_s, hidden_s)

    @pl.when(step == pl.num_programs(0) - 1)
    def _():
        grad = grad_s[...]
        xhat, scale = standardize(middle[...])
        gain_o[...] = jnp.sum(grad * xhat, axis=0, keepdims=True)
        shift_o[...] = jnp.sum(grad, axis=0, keepdims=True)
        middle_grad = out_grad[...] + norm_back(grad, xhat, scale, vec(gain))
        middle_grad_o[...] = middle_grad
        branch = middle_grad.astype(BF16)
        branch_o[...] = branch
        bias_o[...] = jnp.sum(branch.astype(F32), axis=0, keepdims=True)


def attend_back_kernel(
    skip, count, info, normed, mixed, branch, q, k, v, p, wo, *refs
):
    refs = refs[count:]
    (
        keep_o, send_o, dq_o, dk_o, dv_o, qb_o, vb_o,
        grad_s, score_s, both,
    ) = refs
    step = pl.program_id(0) + skip
    length = normed.shape[0]
    mixed_grad = dot_nt(branch[...], wo[...]).astype(BF16)
    cols = pl.ds(pl.multiple_of(step * WIDE, WIDE), WIDE)
    grad_s[...] = dot_nt(mixed_grad, stack_heads(v[...], length))
    both[3] = dot_tn(mixed[...], branch[:, cols]).astype(BF16)
    dv = unstack_heads(dot_tn(p[0], mixed_grad), length).astype(BF16)
    rows = 64
    for top in range(0, length, rows):
        at = slice(top, top + rows)
        for h in range(GROUP):
            span = slice(h * length, (h + 1) * length)
            prob = p[0, at, span].astype(F32)
            weighted = prob * grad_s[at, span]
            center = jnp.sum(weighted, axis=-1, keepdims=True)
            score_s[at, span] = (weighted - prob * center).astype(BF16)
    dq = (dot(score_s[...], stack_heads(k[...], length)) * score_scale).astype(BF16)
    dk = (unstack_heads(dot_tn(score_s[...], q[...]), length) * score_scale).astype(BF16)
    dq_o[...] = dq
    dk_o[...] = dk
    dv_o[...] = dv
    qb_o[...] = jnp.sum(dq.astype(F32), axis=0, keepdims=True)
    vb_o[...] = jnp.sum(dv.astype(F32), axis=0, keepdims=True)
    both[0] = dot_tn(normed[...], dq).astype(BF16)
    both[1] = dot_tn(normed[...], dk).astype(BF16)
    both[2] = dot_tn(normed[...], dv).astype(BF16)
    for t in range(2):
        relative_store(
            info, lambda rows: (both[t, rows], both[2 + t, rows]),
            keep_o, send_o, t ^ info[2], t ^ info[4], normed.shape[1],
        )


def finish_kernel(
    info, tok, middle_grad, dq, dk, dv, wq, wk, wv, g1,
    middle, out_sum, b2, seg, tgt,
    qb, vb, ob, n2g, n2s, b2g, b1a, b1b, b1c,
    tokens_o, small_o, own_o, hop1_o, hop2_o, hop3_o,
    acc,
):
    step = pl.program_id(0)

    @pl.when(step == 0)
    def _():
        acc[...] = jnp.zeros_like(acc)
        output = (middle[...] + (out_sum[...] + vec(b2))).astype(BF16)
        places = located(seg, tgt, [info[0] ^ hop for hop in range(4)], output.shape[0])
        picked = dot_tn(places, output).astype(BF16)
        for hop, out in enumerate((own_o, hop1_o, hop2_o, hop3_o)):
            out[...] = picked[hop * out.shape[0] : (hop + 1) * out.shape[0]]

    acc[...] += dot_nt(dq[...], wq[...]) + dot_nt(dk[...], wk[...]) + dot_nt(dv[...], wv[...])

    @pl.when(step == pl.num_programs(0) - 1)
    def _():
        grad = acc[...]
        xhat, scale = standardize(tok[...].astype(F32))
        tokens_o[...] = (middle_grad[...] + norm_back(grad, xhat, scale, vec(g1))).astype(BF16)
        width = grad.shape[1]
        small_o[0:1, :] = qb[...]
        small_o[1:2, :] = vb[...]
        small_o[2:3, :] = ob[...]
        small_o[3:4, :] = jnp.sum(grad * xhat, axis=0, keepdims=True)
        small_o[4:5, :] = jnp.sum(grad, axis=0, keepdims=True)
        small_o[5:6, :] = n2g[...]
        small_o[6:7, :] = n2s[...]
        small_o[7:8, :] = b2g[...]
        row = 8
        for part in (b1a, b1b, b1c):
            for j in range(part.shape[1] // width):
                small_o[row : row + 1, :] = part[:, j * width : (j + 1) * width]
                row += 1


def place_kernel(part, names, first_call, *refs):
    info = refs[0]
    count = 2 * len(names)
    quarters = refs[1 : 1 + count]
    outs = refs[1 + count + (0 if first_call else 2) :][:2]
    mark, low_s, stage, in_sems, sems = refs[-5:]
    mark[...] = jnp.zeros_like(mark)
    half, width = quarters[0].shape
    rows = 2 * half // SPANS

    def send(n, k, side, tile, span):
        source = stage.at[n, pl.ds(k * rows, rows), :]
        at = pl.ds(pl.multiple_of(span * rows, rows), rows)
        sem = sems.at[n, k]
        columns = lambda t: pl.ds(pl.multiple_of(t * width, width), width)
        if part is not None:
            if side == 0:
                start = (tile + 2 * part) * width + span * rows
                target = outs[0].at[pl.ds(pl.multiple_of(start, rows), rows), :]
            else:
                target = outs[1].at[at, columns(tile + 2 * part)]
            pltpu.make_async_copy(source, target, sem).start()
        elif side == 0:
            pltpu.make_async_copy(source, outs[0].at[at, columns(tile)], sem).start()
        else:

            @pl.when(tile == 0)
            def _():
                pltpu.make_async_copy(source, outs[0].at[at, columns(2)], sem).start()

            @pl.when(tile == 1)
            def _():
                pltpu.make_async_copy(source, outs[1].at[at, :], sem).start()

    for n in range(count):
        pltpu.make_async_copy(quarters[n], low_s.at[n], in_sems.at[n]).start()
    for n in range(count):
        name, other = names[n // 2], n % 2
        tile = (name // 2) ^ info[2 + 2 * other]
        pltpu.make_async_copy(quarters[n], low_s.at[n], in_sems.at[n]).wait()
        for k in range(half // rows):
            stage[n, k * rows : (k + 1) * rows, :] = low_s[n, k * rows : (k + 1) * rows, :].astype(F32)
            span = ((name % 2) * (SPANS // 2) + k) ^ info[3 + 2 * other]
            for side in range(2):

                @pl.when((info[1] ^ other) == side)
                def _():
                    send(n, k, side, tile, span)

    for n in range(count):
        for k in range(half // rows):
            here = stage.at[n, pl.ds(k * rows, rows), :]
            pltpu.make_async_copy(here, here, sems.at[n, k]).wait()


def cost(micros):
    return pl.CostEstimate(
        flops=int(micros * 9e8), bytes_accessed=int(micros * 3.4e6), transcendentals=0
    )


def call(kernel, grid, ins, outs, scratch=(), micros=4, vmem=26, prefetch=0, aliases={}, line=None):
    extra = [] if line is None or line.last is None else [line.last]
    known = len(ins) + prefetch
    body = (lambda *refs: kernel(*refs[:known], *refs[known + 1 :])) if extra else kernel
    inner = pl.pallas_call(
        body,
        grid_spec=pltpu.PrefetchScalarGridSpec(
            num_scalar_prefetch=prefetch,
            grid=grid,
            in_specs=list(ins) + [pl.BlockSpec(memory_space=pl.ANY)] * len(extra),
            out_specs=[spec for spec, _ in outs],
            scratch_shapes=list(scratch),
        ),
        out_shape=[shape for _, shape in outs],
        input_output_aliases=aliases,
        compiler_params=pltpu.CompilerParams(vmem_limit_bytes=vmem * 2**20),
        cost_estimate=cost(micros if line is None or line.weight is None else line.weight),
    )
    return lambda *args: inner(
        *(pltpu.with_memory_space_constraint(a.array, a.space) if isinstance(a, Far) else a for a in args),
        *extra,
    )


class Far:
    space = pltpu.HBM

    def __init__(self, array):
        self.array = array


class Near(Far):
    space = pltpu.VMEM


def full(*shape):
    return pl.BlockSpec(shape, lambda *_: (0,) * len(shape))


def block(shape, index):
    return pl.BlockSpec(shape, index)


def sds(shape, dtype):
    return jax.ShapeDtypeStruct(shape, dtype)


def place(part, names, info, values, shapes, outs, line):
    half, width = values[0].shape
    rows = 2 * half // SPANS
    anywhere = pl.BlockSpec(memory_space=pl.ANY)
    count = len(values)
    outs = call(
        functools.partial(place_kernel, part, names, not outs),
        (),
        [pl.BlockSpec(memory_space=pltpu.SMEM)]
        + [anywhere] * (count + len(outs)),
        [(anywhere, pltpu.HBM(shape.shape, shape.dtype)) for shape in shapes]
        + [(pl.BlockSpec(memory_space=pltpu.VMEM), pltpu.VMEM((8, 128), F32))],
        [
            pltpu.VMEM((count, half, width), BF16),
            pltpu.VMEM((count, half, width), F32),
            pltpu.SemaphoreType.DMA((count,)),
            pltpu.SemaphoreType.DMA((count, half // rows)),
        ],
        micros=MOVE,
        vmem=16,
        line=line,
        aliases={1 + count + n: n for n in range(len(outs))},
    )(info, *values, *outs)
    line.last = outs[2]
    return outs[:2]


class Exchange:
    def __init__(self, rows, blk):
        self.blk = blk
        self.total = rows * blk
        self.bits = self.total.bit_length() - 1
        assert self.total == 1 << self.bits and blk == 4
        self.here = lax.axis_index("rows") * blk + lax.axis_index("blk")
        self.core = self.here & 1
        self.steps = self.bits - 1

    def pairs(self, masks):
        return [(i, i ^ masks[i & 1]) for i in range(self.total)]

    def move_core(self, value):
        return lax.ppermute(value, AXES, self.pairs((1, 1)))

    def swap_blocks(self, pieces):
        mine = self.here & (self.blk - 1)
        got = [lax.dynamic_index_in_dim(pieces, mine, 0, keepdims=False)]
        for hop in range(1, self.blk):
            send = lax.dynamic_index_in_dim(pieces, mine ^ hop, 0, keepdims=False)
            got.append(lax.ppermute(send, AXES, self.pairs((hop, hop))))
        return got


class Chunk:
    def __init__(self, ex, line, perms):
        self.ex = ex
        self.line = line
        base = list(range(1, ex.bits))
        self.orders = [[base[n] for n in perm] + base[LEVELS:] for perm in perms]

    def bits_of(self, order):
        return [(self.ex.here >> bit) & 1 for bit in order]

    def info(self):
        places = []
        for order in self.orders:
            bit = self.bits_of(order)
            places.append((bit[0], bit[1] * 4 + bit[2] * 2 + bit[3]))
        core = self.ex.core
        own = [jnp.where(core == 0, a, b) for a, b in zip(*places)]
        other = [jnp.where(core == 0, b, a) for a, b in zip(*places)]
        return jnp.stack([self.ex.here & (self.ex.blk - 1), core] + own + other).astype(jnp.int32)

    def move(self, level, value):
        masks = tuple(1 << order[level] for order in self.orders)
        return lax.ppermute(value, AXES, self.ex.pairs(masks))

    def add(self, level, which):
        rows = self.keep.shape[1] >> level
        width = self.keep.shape[2]
        if level == 0:
            self.got = []
        tile = pl.BlockSpec((None, rows, width), lambda _: (int(level == 0), which if level else 0, 0))
        strip = pl.BlockSpec((rows, width), lambda _: (which, 0))
        return self.line.run(
            add_kernel,
            [self.keep, self.recv] + self.got,
            [sds((rows, width), BF16)],
            [tile] * 2 + [strip] * len(self.got),
        )

    def total(self):
        span = self.add(LEVELS - 1, 0)
        rows = span.shape[0]
        bits = [
            jnp.where(self.ex.core == 0, a, b)
            for a, b in zip(*(self.bits_of(order)[LEVELS:] for order in self.orders))
        ]
        for level, bit in enumerate(bits, LEVELS):
            rows //= 2
            recv = self.move(level, lax.dynamic_slice_in_dim(span, (1 - bit) * rows, rows, 0))
            span = add_up([lax.dynamic_slice_in_dim(span, bit * rows, rows, 0), recv])
        for level, bit in reversed(list(enumerate(bits, LEVELS))):
            recv = self.move(level, span)
            low = jnp.where(bit == 0, span, recv)
            span = jnp.concatenate([low, jnp.where(bit == 0, recv, span)], axis=0)
        self.spans = {"p": span}

    def join(self):
        spans = [self.spans[name] for name in ("p", "g0", "g1", "g2") if name in self.spans]
        rows, width = spans[0].shape
        return self.line.run(join_kernel, spans, [sds((len(spans) * rows, width), BF16)])

    def do(self, step):
        if step == "c":
            self.recv = self.ex.move_core(self.send)
        elif step[0] == "r":
            level = int(step[1])
            total = self.add(level, 1)
            self.got.append(self.move(level, total))
        elif step == "f":
            self.total()
        elif step == "g0":
            self.spans[step] = self.move(3, self.spans["p"])
        elif step in ("g1", "g2"):
            self.spans[step] = self.move(2, self.spans["p" if step == "g1" else "g0"])
        elif step == "h":
            self.spans = {"p": self.join()}
        elif step == "j":
            self.quarters = {"A": self.join()}
        elif step == "g3":
            self.quarters["B"] = self.move(1, self.quarters["A"])
        elif step == "g4":
            self.quarters["C"] = self.move(0, self.quarters["A"])
        elif step == "g5":
            self.quarters["D"] = self.move(0, self.quarters["B"])
        else:
            name = step[1]
            self.others[name] = self.ex.move_core(self.quarters[name])


class Line:
    def __init__(self):
        self.last = None
        self.weight = None

    def run(self, kernel, ins, out_shapes, specs=None, vmem=16):
        after = [] if self.last is None else [self.last]
        near = pl.BlockSpec(memory_space=pltpu.VMEM)
        outs = pl.pallas_call(
            functools.partial(skip, len(after), kernel),
            grid=() if specs is None else (1,),
            in_specs=[pl.BlockSpec(memory_space=pl.ANY)] * len(after) + (specs or [near] * len(ins)),
            out_specs=[near if specs is None else full(*shape.shape) for shape in out_shapes],
            out_shape=out_shapes,
            compiler_params=pltpu.CompilerParams(vmem_limit_bytes=vmem * 2**20),
            cost_estimate=cost(STEP if self.weight is None else self.weight),
        )(*after, *ins)
        self.last = outs[0]
        return outs[0]


def skip(count, kernel, *refs):
    kernel(*refs[count:])


def add_kernel(*refs):
    out = refs[-1]
    height = 32 if out.shape[0] % 32 == 0 else out.shape[0]

    def body(n, _):
        at = pl.ds(pl.multiple_of(n * height, height), height)
        total = refs[0][at, :].astype(F32)
        for ref in refs[1:-1]:
            total = total + ref[at, :].astype(F32)
        out[at, :] = total.astype(BF16)
        return 0

    lax.fori_loop(0, out.shape[0] // height, body, 0)


def join_kernel(*refs):
    start = 0
    for ref in refs[:-1]:
        refs[-1][start : start + ref.shape[0], :] = ref[...]
        start += ref.shape[0]


def order_kernel(info, *refs):
    rows = refs[0].shape[0]
    for hop, ref in enumerate(refs[:-1]):
        refs[-1][pl.ds(pl.multiple_of((info[0] ^ hop) * rows, rows), rows), :] = ref[...]


def sum_kernel(one, other, out):
    out[...] = one[...] + other[...]


def add_up(terms):
    total = terms[0].astype(F32)
    for term in terms[1:]:
        total = total + term.astype(F32)
    return total.astype(BF16)


def local(
    mesh_rows, mesh_blk,
    tokens, seg_ids, target_index,
    qkv_weight, q_bias, v_bias, out_weight, out_bias,
    norm1_gain, norm1_shift, norm2_gain, norm2_shift,
    fc1_weight, fc1_bias, fc2_weight, fc2_bias,
    target_grad,
):
    ex = Exchange(mesh_rows, mesh_blk)
    count_rows, length, d = tokens.shape
    assert count_rows == 1
    ff = fc1_weight.shape[1]
    tiles = ff // d
    images, patches = target_grad.shape[1], target_grad.shape[2]
    per = images // mesh_blk
    groups = d // WIDE
    pieces = target_grad.reshape(mesh_blk, per * patches, d)
    got = ex.swap_blocks(pieces)
    tok = Far(tokens.reshape(length, d))
    seg, target_index = Far(seg_ids), Far(target_index)
    qkv_weight, q_bias, v_bias, out_weight, out_bias = map(
        Far, (qkv_weight, q_bias, v_bias, out_weight, out_bias)
    )
    norm1_gain, norm1_shift, norm2_gain, norm2_shift = map(
        Far, (norm1_gain, norm1_shift, norm2_gain, norm2_shift)
    )
    fc1_weight, fc1_bias, fc2_weight, fc2_bias = map(
        Far, (fc1_weight, fc1_bias, fc2_weight, fc2_bias)
    )
    picks = full(*target_index.array.shape)
    col = lambda g: (0, g)
    third = lambda n: lambda g: (0, n * groups + g)
    act = pltpu.VMEM((length, d), BF16)
    act32 = pltpu.VMEM((length, d), F32)
    act_far = pltpu.HBM((length, d), BF16)
    one = pltpu.VMEM((1, d), F32)
    vd = full(d)
    smem = pl.BlockSpec(memory_space=pltpu.SMEM)
    whole = full(length, d)
    strip = block((length, WIDE), col)
    wide = GROUP * length
    wide_spec = block((1, length, wide), lambda g: (g, 0, 0))

    line = Line()
    links = [Chunk(ex, line, perms) for perms in ORDERS]
    infos = [link.info() for link in links]
    for link, info in zip(links, infos):
        link.info_ref = info
    half = tiles // 2

    def mlp_specs(skip):
        return [
            block((d, d), lambda j, info: (0, skip + j)),
            block((d, d), lambda j, info: (skip + j, 0)),
            full(ff),
        ]

    def tile_outs(skip):
        return [
            (block((1, d, d), lambda j, info, n=n: ((j + skip) ^ info[n], 0, 0)), pltpu.HBM((half, d, d), BF16))
            for n in (2, 4)
        ]

    def b1_out(tiles):
        return block((1, d), lambda j, info: (0, j)), pltpu.VMEM((1, tiles * d), F32)

    both = pltpu.VMEM((2, d, d), BF16)
    saved = [pltpu.VMEM((length, d), BF16)] * 2
    piece = full(per * patches, d)
    pair_out = (block((2, d, WIDE), lambda g: (0, 0, g)), pltpu.HBM((2, d, d), BF16))
    links_by_name = dict(zip(("M1", "M2", "Q"), links))
    for link in links:
        link.others = {}
    fc_out = qkv_out = ()
    small_step = 0
    for step in SCHEDULE:
        line.weight = WEIGHTS.get(step)
        if step == "K0":
            normed, q, k, v, prob, mixed, middle, second = call(
                attend_kernel,
                (groups,),
                [
                    whole, full(1, length),
                    block((d, WIDE), third(0)), block((d, WIDE), third(1)), block((d, WIDE), third(2)),
                    block((WIDE, d), lambda g: (g, 0)),
                    vd, vd, vd, vd, vd, vd, vd,
                ],
                [
                    (whole, act_far), (strip, act_far), (strip, act_far), (strip, act_far),
                    (wide_spec, pltpu.HBM((groups, length, wide), BF16)),
                    (strip, act_far), (whole, act32), (whole, act),
                ],
                [
                    pltpu.VMEM((length, d), F32),
                    pltpu.VMEM((length, wide), F32),
                    pltpu.VMEM((2, d), F32),
                ],
                micros=11 * PACE, line=line,
            )(
                tok, seg, qkv_weight, qkv_weight, qkv_weight, out_weight, q_bias, v_bias, out_bias,
                norm1_gain, norm1_shift, norm2_gain, norm2_shift,
            )
        elif step == "K1":
            links[0].keep, links[0].send, out_sum, second_grad, b1a, out_grad, mlp_low, b2_grad = call(
                first_mlp_kernel,
                (half,),
                [whole, full(1, length), picks] + [piece] * 4 + mlp_specs(0),
                [
                    *tile_outs(0), (whole, act32), (whole, act32), b1_out(half),
                    (whole, act32), (whole, act), (full(1, d), one),
                ],
                [both, pltpu.VMEM((1, ff), F32), *saved],
                micros=12 * PACE, prefetch=1, line=line,
            )(infos[0], Near(second), seg, target_index, *got, fc1_weight, fc2_weight, fc1_bias)
            line.last = b2_grad
        elif step == "K2a":
            links[1].keep, links[1].send, out_sum, second_grad, b1b = call(
                functools.partial(middle_mlp_kernel, half),
                (1,),
                [whole, whole] + mlp_specs(half) + [whole] * 2,
                [*tile_outs(0), (whole, act32), (whole, act32), b1_out(1)],
                [both, pltpu.VMEM((1, ff), F32), *saved],
                micros=6 * PACE, prefetch=1, line=line,
            )(infos[1], Near(second), Near(mlp_low), fc1_weight, fc2_weight, fc1_bias, Near(out_sum), Near(second_grad))
            line.last = b1b
        elif step == "K2b":
            links[1].keep, links[1].send, out_sum, b1c, middle_grad, branch, n2g, n2s, ob_grad = call(
                functools.partial(second_mlp_kernel, half + 1),
                (1,),
                [whole, whole] + mlp_specs(half + 1) + [whole] * 4 + [vd] + [pl.BlockSpec(memory_space=pl.ANY)] * 2,
                [
                    *tile_outs(1), (whole, act32), b1_out(1),
                    (whole, act32), (whole, act), (full(1, d), one), (full(1, d), one), (full(1, d), one),
                ],
                [both, pltpu.VMEM((length, d), F32), pltpu.VMEM((1, ff), F32), *saved],
                micros=7 * PACE, prefetch=1, line=line, aliases={11: 0, 12: 1},
            )(
                infos[1], Near(second), Near(mlp_low), fc1_weight, fc2_weight, fc1_bias,
                *map(Near, (out_sum, second_grad, middle, out_grad)), norm2_gain,
                Far(links[1].keep), Far(links[1].send),
            )
            line.last = ob_grad
        elif step in ("K3", "K3a", "K3b"):
            skip = FIRST if step == "K3b" else 0
            count = {"K3": groups, "K3a": FIRST, "K3b": groups - FIRST}[step]
            at = lambda g, skip=skip: (0, g + skip)
            some = block((length, WIDE), at)
            pair_out = (block((2, d, WIDE), lambda g, skip=skip: (0, 0, g + skip)), pltpu.HBM((2, d, d), BF16))
            row_out = (block((1, WIDE), at), pltpu.HBM((1, d), F32))
            earlier = [] if step != "K3b" else [links[2].keep, links[2].send, dq, dk, dv, qb_grad, vb_grad]
            links[2].keep, links[2].send, dq, dk, dv, qb_grad, vb_grad = call(
                functools.partial(attend_back_kernel, skip, len(earlier)),
                (count,),
                [
                    smem, whole, whole, whole, some, some, some,
                    block((1, length, wide), lambda g, skip=skip: (g + skip, 0, 0)),
                    block((WIDE, d), lambda g, skip=skip: (g + skip, 0)),
                ]
                + [pl.BlockSpec(memory_space=pl.ANY)] * len(earlier),
                [pair_out, pair_out, *[(some, act_far)] * 3, row_out, row_out],
                [
                    pltpu.VMEM((length, wide), F32),
                    pltpu.VMEM((length, wide), BF16),
                    pltpu.VMEM((4, d, WIDE), BF16),
                ],
                micros=4.5 * count * PACE, line=line,
                aliases={9 + n: n for n in range(len(earlier))},
            )(
                infos[2], Far(normed), Far(mixed), Near(branch), *map(Far, (q, k, v, prob)), out_weight,
                *map(Far, earlier),
            )
            line.last = dq
        elif step == "K4":
            tokens_grad, small, *picked = call(
                finish_kernel,
                (groups,),
                [
                    smem, whole, whole, strip, strip, strip,
                    block((d, WIDE), third(0)), block((d, WIDE), third(1)), block((d, WIDE), third(2)),
                    vd, whole, whole, vd, full(1, length), picks,
                ]
                + [full(1, d)] * 6 + [full(1, half * d)] + [full(1, d)] * 2,
                [
                    (whole, pltpu.HBM((length, d), BF16)),
                    (full(8 + tiles, d), sds((8 + tiles, d), F32)),
                    *[(full(per * patches, d), sds((per * patches, d), BF16))] * 4,
                ],
                [pltpu.VMEM((length, d), F32)],
                micros=7 * PACE, line=line,
            )(
                infos[0], tok, Near(middle_grad), *map(Far, (dq, dk, dv)), qkv_weight, qkv_weight, qkv_weight, norm1_gain,
                Near(middle), Near(out_sum), fc2_bias, seg, target_index,
                Far(qb_grad), Far(vb_grad), *map(Near, (ob_grad, n2g, n2s, b2_grad, b1a, b1b, b1c)),
            )
            line.last = small
        elif step == "T":
            swapped = picked[:1] + [
                lax.ppermute(picked[hop], AXES, ex.pairs((hop, hop))) for hop in range(1, mesh_blk)
            ]
        elif step == "t":
            targets = line.run(
                order_kernel,
                [infos[0], *swapped],
                [sds((images * patches, d), BF16)],
                [smem] + [full(per * patches, d)] * mesh_blk,
            )
        elif step == "S":
            small = line.run(sum_kernel, [small, small_recv], [sds(small.shape, F32)])
            small_step += 1
        elif step == "s":
            small_recv = lax.ppermute(small, AXES, ex.pairs((1 << small_step,) * 2))
        else:
            name, step = step.split()
            link = links_by_name[name]
            if step[0] != "v":
                link.do(step)
                continue
            names = ["ABCD".index(n) for n in step[1:]]
            values = [v for n in step[1:] for v in (link.quarters[n], link.others[n])]
            if name == "Q":
                shapes = [sds((d, 3 * d), F32), sds((d, d), F32)]
                qkv_out = place(None, names, link.info_ref, values, shapes, qkv_out, line)
            else:
                shapes = [sds((ff, d), F32), sds((d, ff), F32)]
                fc_out = place(int(name[1]) - 1, names, link.info_ref, values, shapes, fc_out, line)
    for _ in range(small_step, ex.bits):
        small = small + lax.ppermute(small, AXES, ex.pairs((1 << small_step,) * 2))
        small_step += 1
    fc2_full, fc1_full = fc_out
    qkv_full, out_full = qkv_out
    return (
        targets.reshape(1, images, patches, d),
        tokens_grad.reshape(count_rows, length, d),
        qkv_full,
        small[0], small[1],
        out_full,
        small[2], small[3], small[4], small[5], small[6],
        fc1_full,
        small[8:].reshape(ff),
        fc2_full,
        small[7],
    )


def solution(mesh):
    rows, blk = mesh.shape["rows"], mesh.shape["blk"]

    def body(*args):
        return local(rows, blk, *args)

    return jax.shard_map(
        body,
        mesh=mesh,
        in_specs=(
            P(("rows", "blk"), None, None),
            P(("rows", "blk"), None),
            P(("rows", "blk"), None, None),
        )
        + (P(),) * 13
        + (P("blk", "rows", None, None),),
        out_specs=(
            P("blk", "rows", None, None),
            P(("rows", "blk"), None, None),
        )
        + (P(),) * 13,
        check_vma=False,
    )
```

```python
import functools

import jax
import jax.numpy as jnp
from jax import lax
from jax.experimental import pallas as pl
from jax.experimental.pallas import tpu as pltpu
from jax.sharding import PartitionSpec as P

HEADS = 12
HEAD_DIM = 64
GROUP = 4
WIDE = GROUP * HEAD_DIM
LEVELS = 4
PIECE = 768
PACE = 2
STEP = 7
MOVE = 25
WEIGHTS = {
    "K1": 200,
    "K2a": 3,
    "K3": 80,
    "K4": 40,
    "M1 f": 10,
    "M1 j": 1,
    "M1 r0": 1,
    "M1 r1": 0,
    "M1 r3": 3,
    "M1 vABCD": 3,
    "M2 j": 3,
    "M2 r3": 20,
    "M2 vABCD": 20,
    "Q r0": 0,
    "Q r3": 3,
    "Q vAB": 80,
    "Q vCD": 200,
    "S": 0,
}
FIRST = 1
SPANS = 8
AXES = ("rows", "blk")
SCHEDULE = (
    "K0", "K1", "M1 c", "K2a", "M1 r0", "K2b", "K3", "M1 r1", "M2 c", "M2 r0", "Q c", "K4",
    "M1 r2", "s", "T", "Q r0", "M1 r3", "M2 r1", "S", "s", "M1 f", "M1 g1", "M2 r2", "Q r1",
    "M1 g0", "M2 r3", "Q r2", "M1 g2", "S", "s", "M1 j", "S", "M1 g4", "M1 g3", "M1 cA", "M2 f",
    "s", "M1 g5", "M1 cB", "S", "Q r3", "Q f", "M2 g0", "M2 g1", "M1 cD", "Q g0", "Q g2", "s",
    "Q g1", "M2 g2", "M2 j", "M2 cA", "M2 g3", "M2 g4", "M2 g5", "M1 cC", "M1 vABCD", "Q j", "Q cA", "M2 cC",
    "Q g4", "M2 cD", "Q g3", "M2 cB", "Q g5", "Q cD", "M2 vABCD", "S", "Q cB", "Q vAB", "Q cC", "Q vCD",
    "t",
)
ORDERS = (((0, 1, 2, 3), (1, 0, 2, 3)), ((0, 1, 2, 3), (1, 0, 2, 3)), ((0, 1, 2, 3), (1, 0, 2, 3)))
F32 = jnp.float32
BF16 = jnp.bfloat16

norm_eps = 1e-06
score_scale = 0.125
neg_large = -1e30


def dot(a, b):
    return lax.dot_general(a, b, (((1,), (0,)), ((), ())), preferred_element_type=F32)


def dot_nt(a, b):
    return lax.dot_general(a, b, (((1,), (1,)), ((), ())), preferred_element_type=F32)


def dot_tn(a, b):
    return lax.dot_general(a, b, (((0,), (0,)), ((), ())), preferred_element_type=F32)


def standardize(values):
    center = values - jnp.mean(values, axis=-1, keepdims=True)
    spread = jnp.mean(center * center, axis=-1, keepdims=True)
    scale = lax.rsqrt(spread + norm_eps)
    return center * scale, scale


def norm_back(grad, xhat, scale, gain):
    e = grad * gain
    mean_e = jnp.mean(e, axis=-1, keepdims=True)
    mean_ex = jnp.mean(e * xhat, axis=-1, keepdims=True)
    return (e - mean_e - xhat * mean_ex) * scale


def head_mask(rows, h):
    lane = lax.broadcasted_iota(jnp.int32, (rows, WIDE), 1)
    return (lane >= h * HEAD_DIM) & (lane < (h + 1) * HEAD_DIM)


def vec(ref):
    return ref[...].reshape(1, -1)


def stack_heads(values, length):
    return jnp.concatenate(
        [jnp.where(head_mask(length, h), values, jnp.zeros_like(values)) for h in range(GROUP)],
        axis=0,
    )


def unstack_heads(stacked, length):
    total = stacked[:length]
    for h in range(1, GROUP):
        total = jnp.where(head_mask(length, h), stacked[h * length : (h + 1) * length], total)
    return total


def attend_kernel(
    tok, seg, wq, wk, wv, wo, qb, vb, ob, g1, s1, g2, s2,
    normed_o, q_o, k_o, v_o, p_o, mixed_o, middle_o, second_o,
    acc, score_s, biases,
):
    step = pl.program_id(0)
    length, width = tok.shape
    cols = pl.ds(pl.multiple_of(step * WIDE, WIDE), WIDE)

    @pl.when(step == 0)
    def _():
        xhat, _ = standardize(tok[...].astype(F32))
        normed_o[...] = (xhat * vec(g1) + vec(s1)).astype(BF16)
        acc[...] = jnp.zeros_like(acc)
        biases[0:1, :] = vec(qb)
        biases[1:2, :] = vec(vb)

    normed = normed_o[...]
    q = (dot(normed, wq[...]) + biases[0:1, cols]).astype(BF16)
    k = dot(normed, wk[...]).astype(BF16)
    v = (dot(normed, wv[...]) + biases[1:2, cols]).astype(BF16)
    q_o[...] = q
    k_o[...] = k
    v_o[...] = v
    score_s[...] = dot_nt(q * jnp.asarray(score_scale, BF16), stack_heads(k, length))
    seg_row = seg[...]
    seg_col = jnp.broadcast_to(seg_row.astype(F32), (128, length)).T[:, :1].astype(jnp.int32)
    rows = 64
    for top in range(0, length, rows):
        at = slice(top, top + rows)
        allowed = seg_col[at] == seg_row
        for h in range(GROUP):
            span = slice(h * length, (h + 1) * length)
            scores = jnp.where(allowed, score_s[at, span], neg_large)
            raised = jnp.exp(scores - jnp.max(scores, axis=-1, keepdims=True))
            share = 1.0 / jnp.sum(raised, axis=-1, keepdims=True)
            p_o[0, at, span] = (raised * share).astype(BF16)
    mixed = dot(p_o[0], stack_heads(v, length)).astype(BF16)
    mixed_o[...] = mixed
    acc[...] += dot(mixed, wo[...])

    @pl.when(step == pl.num_programs(0) - 1)
    def _():
        middle = tok[...].astype(F32) + (acc[...] + vec(ob))
        middle_o[...] = middle
        xhat, _ = standardize(middle)
        second_o[...] = (xhat * vec(g2) + vec(s2)).astype(BF16)


def located(seg, tgt, blocks, length):
    rows = []
    starts = [
        jnp.sum(((seg[...] >= 0) & (seg[...] < image)).astype(jnp.int32))
        for image in range(tgt.shape[0])
    ]
    for block in blocks:
        for image, start in enumerate(starts):
            rows.append(tgt[image, pl.ds(block, 1), :] + start)
    row = jnp.concatenate(rows, axis=1)
    slots = lax.broadcasted_iota(jnp.int32, (length, row.shape[1]), 0)
    return (slots == row).astype(F32).astype(BF16)


def tile_bias(bias_s, skip, width):
    start = (pl.program_id(0) + skip) * width
    return bias_s[:, pl.ds(pl.multiple_of(start, width), width)]


def relative_store(info, pair, keep_o, send_o, keep_at, send_at, height):
    first = info[1] == 0
    rows = height // SPANS
    for n in range(SPANS):
        low, high = pair(slice(n * rows, (n + 1) * rows))
        keep_o[keep_at, pl.ds(pl.multiple_of((n ^ info[3]) * rows, rows), rows), :] = jnp.where(first, low, high)
        send_o[send_at, pl.ds(pl.multiple_of((n ^ info[5]) * rows, rows), rows), :] = jnp.where(first, high, low)


def mlp_steps(info, sn, low, w1, w2, bias, keep_o, send_o, out_o, grad_o, b1_o, both, active_s, hidden_s):
    width = low.shape[1]
    piece = PIECE
    for j in range(width // piece):
        cols = slice(j * piece, (j + 1) * piece)
        hidden = dot(sn, w1[:, cols]) + bias[:, cols]
        phi_cum = 0.5 + 0.5 * lax.erf(hidden * 0.7071067811865476)
        density = 0.3989422804014327 * jnp.exp(hidden * hidden * -0.5)
        active_s[:, cols] = (hidden * phi_cum).astype(BF16)
        hidden_grad = dot_nt(low, w2[cols, :]) * (phi_cum + hidden * density)
        hidden_low = hidden_grad.astype(BF16)
        b1_o[:, cols] = jnp.sum(hidden_low.astype(F32), axis=0, keepdims=True)
        hidden_s[:, cols] = hidden_low
    both[0] = dot_tn(active_s[...], low).astype(BF16)
    both[1] = dot_tn(sn, hidden_s[...]).astype(BF16)
    out_o[...] += dot(active_s[...], w2[...])
    grad_o[...] += dot_nt(hidden_s[...], w1[...])
    relative_store(info, lambda rows: (both[0, rows], both[1, rows]), keep_o, send_o, 0, 0, width)


def first_mlp_kernel(
    info, second, seg, tgt, own, got1, got2, got3, w1, w2, b1,
    keep_o, send_o, out_o, grad_o, b1_o, out_grad_o, mlp_o, bias_o,
    both, bias_s, active_s, hidden_s,
):
    @pl.when(pl.program_id(0) == 0)
    def _():
        bias_s[...] = vec(b1)
        me = info[0]
        places = located(seg, tgt, [me, me ^ 1, me ^ 2, me ^ 3], second.shape[0])
        pieces = jnp.concatenate([own[...], got1[...], got2[...], got3[...]], axis=0)
        total = dot(places, pieces)
        out_grad_o[...] = total
        low = total.astype(BF16)
        mlp_o[...] = low
        bias_o[...] = jnp.sum(low.astype(F32), axis=0, keepdims=True)
        out_o[...] = jnp.zeros_like(out_o)
        grad_o[...] = jnp.zeros_like(grad_o)

    bias = tile_bias(bias_s, 0, second.shape[1])
    mlp_steps(info, second[...], mlp_o[...], w1, w2, bias, keep_o, send_o, out_o, grad_o, b1_o, both, active_s, hidden_s)


def middle_mlp_kernel(
    first, info, second, mlp, w1, w2, b1, out_in, grad_in,
    keep_o, send_o, out_o, grad_o, b1_o,
    both, bias_s, active_s, hidden_s,
):
    @pl.when(pl.program_id(0) == 0)
    def _():
        bias_s[...] = vec(b1)
        out_o[...] = out_in[...]
        grad_o[...] = grad_in[...]

    bias = tile_bias(bias_s, first, second.shape[1])
    mlp_steps(info, second[...], mlp[...], w1, w2, bias, keep_o, send_o, out_o, grad_o, b1_o, both, active_s, hidden_s)


def second_mlp_kernel(
    first, info, second, mlp, w1, w2, b1, out_in, grad_in, middle, out_grad, gain, keep_in, send_in,
    keep_o, send_o, out_o, b1_o, middle_grad_o, branch_o, gain_o, shift_o, bias_o,
    both, grad_s, bias_s, active_s, hidden_s,
):
    step = pl.program_id(0)

    @pl.when(step == 0)
    def _():
        bias_s[...] = vec(b1)
        out_o[...] = out_in[...]
        grad_s[...] = grad_in[...]

    bias = tile_bias(bias_s, first, second.shape[1])
    mlp_steps(info, second[...], mlp[...], w1, w2, bias, keep_o, send_o, out_o, grad_s, b1_o, both, active_s, hidden_s)

    @pl.when(step == pl.num_programs(0) - 1)
    def _():
        grad = grad_s[...]
        xhat, scale = standardize(middle[...])
        gain_o[...] = jnp.sum(grad * xhat, axis=0, keepdims=True)
        shift_o[...] = jnp.sum(grad, axis=0, keepdims=True)
        middle_grad = out_grad[...] + norm_back(grad, xhat, scale, vec(gain))
        middle_grad_o[...] = middle_grad
        branch = middle_grad.astype(BF16)
        branch_o[...] = branch
        bias_o[...] = jnp.sum(branch.astype(F32), axis=0, keepdims=True)


def attend_back_kernel(
    skip, count, info, normed, mixed, branch, q, k, v, p, wo, *refs
):
    refs = refs[count:]
    (
        keep_o, send_o, dq_o, dk_o, dv_o, qb_o, vb_o,
        grad_s, score_s, both,
    ) = refs
    step = pl.program_id(0) + skip
    length = normed.shape[0]
    mixed_grad = dot_nt(branch[...], wo[...]).astype(BF16)
    cols = pl.ds(pl.multiple_of(step * WIDE, WIDE), WIDE)
    grad_s[...] = dot_nt(mixed_grad, stack_heads(v[...], length))
    both[3] = dot_tn(mixed[...], branch[:, cols]).astype(BF16)
    dv = unstack_heads(dot_tn(p[0], mixed_grad), length).astype(BF16)
    rows = 64
    for top in range(0, length, rows):
        at = slice(top, top + rows)
        for h in range(GROUP):
            span = slice(h * length, (h + 1) * length)
            prob = p[0, at, span].astype(F32)
            weighted = prob * grad_s[at, span]
            center = jnp.sum(weighted, axis=-1, keepdims=True)
            score_s[at, span] = (weighted - prob * center).astype(BF16)
    dq = (dot(score_s[...], stack_heads(k[...], length)) * score_scale).astype(BF16)
    dk = (unstack_heads(dot_tn(score_s[...], q[...]), length) * score_scale).astype(BF16)
    dq_o[...] = dq
    dk_o[...] = dk
    dv_o[...] = dv
    qb_o[...] = jnp.sum(dq.astype(F32), axis=0, keepdims=True)
    vb_o[...] = jnp.sum(dv.astype(F32), axis=0, keepdims=True)
    both[0] = dot_tn(normed[...], dq).astype(BF16)
    both[1] = dot_tn(normed[...], dk).astype(BF16)
    both[2] = dot_tn(normed[...], dv).astype(BF16)
    for t in range(2):
        relative_store(
            info, lambda rows: (both[t, rows], both[2 + t, rows]),
            keep_o, send_o, t ^ info[2], t ^ info[4], normed.shape[1],
        )


def finish_kernel(
    info, tok, middle_grad, dq, dk, dv, wq, wk, wv, g1,
    middle, out_sum, b2, seg, tgt,
    qb, vb, ob, n2g, n2s, b2g, b1a, b1b, b1c,
    tokens_o, small_o, own_o, hop1_o, hop2_o, hop3_o,
    acc,
):
    step = pl.program_id(0)

    @pl.when(step == 0)
    def _():
        acc[...] = jnp.zeros_like(acc)
        output = (middle[...] + (out_sum[...] + vec(b2))).astype(BF16)
        places = located(seg, tgt, [info[0] ^ hop for hop in range(4)], output.shape[0])
        picked = dot_tn(places, output).astype(BF16)
        for hop, out in enumerate((own_o, hop1_o, hop2_o, hop3_o)):
            out[...] = picked[hop * out.shape[0] : (hop + 1) * out.shape[0]]

    acc[...] += dot_nt(dq[...], wq[...]) + dot_nt(dk[...], wk[...]) + dot_nt(dv[...], wv[...])

    @pl.when(step == pl.num_programs(0) - 1)
    def _():
        grad = acc[...]
        xhat, scale = standardize(tok[...].astype(F32))
        tokens_o[...] = (middle_grad[...] + norm_back(grad, xhat, scale, vec(g1))).astype(BF16)
        width = grad.shape[1]
        small_o[0:1, :] = qb[...]
        small_o[1:2, :] = vb[...]
        small_o[2:3, :] = ob[...]
        small_o[3:4, :] = jnp.sum(grad * xhat, axis=0, keepdims=True)
        small_o[4:5, :] = jnp.sum(grad, axis=0, keepdims=True)
        small_o[5:6, :] = n2g[...]
        small_o[6:7, :] = n2s[...]
        small_o[7:8, :] = b2g[...]
        row = 8
        for part in (b1a, b1b, b1c):
            for j in range(part.shape[1] // width):
                small_o[row : row + 1, :] = part[:, j * width : (j + 1) * width]
                row += 1


def place_kernel(part, names, first_call, *refs):
    info = refs[0]
    count = 2 * len(names)
    quarters = refs[1 : 1 + count]
    outs = refs[1 + count + (0 if first_call else 2) :][:2]
    mark, low_s, stage, in_sems, sems = refs[-5:]
    mark[...] = jnp.zeros_like(mark)
    half, width = quarters[0].shape
    rows = 2 * half // SPANS

    def send(n, k, side, tile, span):
        source = stage.at[n, pl.ds(k * rows, rows), :]
        at = pl.ds(pl.multiple_of(span * rows, rows), rows)
        sem = sems.at[n, k]
        columns = lambda t: pl.ds(pl.multiple_of(t * width, width), width)
        if part is not None:
            if side == 0:
                start = (tile + 2 * part) * width + span * rows
                target = outs[0].at[pl.ds(pl.multiple_of(start, rows), rows), :]
            else:
                target = outs[1].at[at, columns(tile + 2 * part)]
            pltpu.make_async_copy(source, target, sem).start()
        elif side == 0:
            pltpu.make_async_copy(source, outs[0].at[at, columns(tile)], sem).start()
        else:

            @pl.when(tile == 0)
            def _():
                pltpu.make_async_copy(source, outs[0].at[at, columns(2)], sem).start()

            @pl.when(tile == 1)
            def _():
                pltpu.make_async_copy(source, outs[1].at[at, :], sem).start()

    for n in range(count):
        pltpu.make_async_copy(quarters[n], low_s.at[n], in_sems.at[n]).start()
    for n in range(count):
        name, other = names[n // 2], n % 2
        tile = (name // 2) ^ info[2 + 2 * other]
        pltpu.make_async_copy(quarters[n], low_s.at[n], in_sems.at[n]).wait()
        for k in range(half // rows):
            stage[n, k * rows : (k + 1) * rows, :] = low_s[n, k * rows : (k + 1) * rows, :].astype(F32)
            span = ((name % 2) * (SPANS // 2) + k) ^ info[3 + 2 * other]
            for side in range(2):

                @pl.when((info[1] ^ other) == side)
                def _():
                    send(n, k, side, tile, span)

    for n in range(count):
        for k in range(half // rows):
            here = stage.at[n, pl.ds(k * rows, rows), :]
            pltpu.make_async_copy(here, here, sems.at[n, k]).wait()


def cost(micros):
    return pl.CostEstimate(
        flops=int(micros * 9e8), bytes_accessed=int(micros * 3.4e6), transcendentals=0
    )


def call(kernel, grid, ins, outs, scratch=(), micros=4, vmem=26, prefetch=0, aliases={}, line=None):
    extra = [] if line is None or line.last is None else [line.last]
    known = len(ins) + prefetch
    body = (lambda *refs: kernel(*refs[:known], *refs[known + 1 :])) if extra else kernel
    inner = pl.pallas_call(
        body,
        grid_spec=pltpu.PrefetchScalarGridSpec(
            num_scalar_prefetch=prefetch,
            grid=grid,
            in_specs=list(ins) + [pl.BlockSpec(memory_space=pl.ANY)] * len(extra),
            out_specs=[spec for spec, _ in outs],
            scratch_shapes=list(scratch),
        ),
        out_shape=[shape for _, shape in outs],
        input_output_aliases=aliases,
        compiler_params=pltpu.CompilerParams(vmem_limit_bytes=vmem * 2**20),
        cost_estimate=cost(micros if line is None or line.weight is None else line.weight),
    )
    return lambda *args: inner(
        *(pltpu.with_memory_space_constraint(a.array, a.space) if isinstance(a, Far) else a for a in args),
        *extra,
    )


class Far:
    space = pltpu.HBM

    def __init__(self, array):
        self.array = array


class Near(Far):
    space = pltpu.VMEM


def full(*shape):
    return pl.BlockSpec(shape, lambda *_: (0,) * len(shape))


def block(shape, index):
    return pl.BlockSpec(shape, index)


def sds(shape, dtype):
    return jax.ShapeDtypeStruct(shape, dtype)


def place(part, names, info, values, shapes, outs, line):
    half, width = values[0].shape
    rows = 2 * half // SPANS
    anywhere = pl.BlockSpec(memory_space=pl.ANY)
    count = len(values)
    outs = call(
        functools.partial(place_kernel, part, names, not outs),
        (),
        [pl.BlockSpec(memory_space=pltpu.SMEM)]
        + [anywhere] * (count + len(outs)),
        [(anywhere, pltpu.HBM(shape.shape, shape.dtype)) for shape in shapes]
        + [(pl.BlockSpec(memory_space=pltpu.VMEM), pltpu.VMEM((8, 128), F32))],
        [
            pltpu.VMEM((count, half, width), BF16),
            pltpu.VMEM((count, half, width), F32),
            pltpu.SemaphoreType.DMA((count,)),
            pltpu.SemaphoreType.DMA((count, half // rows)),
        ],
        micros=MOVE,
        vmem=16,
        line=line,
        aliases={1 + count + n: n for n in range(len(outs))},
    )(info, *values, *outs)
    line.last = outs[2]
    return outs[:2]


class Exchange:
    def __init__(self, rows, blk):
        self.blk = blk
        self.total = rows * blk
        self.bits = self.total.bit_length() - 1
        assert self.total == 1 << self.bits and blk == 4
        self.here = lax.axis_index("rows") * blk + lax.axis_index("blk")
        self.core = self.here & 1
        self.steps = self.bits - 1

    def pairs(self, masks):
        return [(i, i ^ masks[i & 1]) for i in range(self.total)]

    def move_core(self, value):
        return lax.ppermute(value, AXES, self.pairs((1, 1)))

    def swap_blocks(self, pieces):
        mine = self.here & (self.blk - 1)
        got = [lax.dynamic_index_in_dim(pieces, mine, 0, keepdims=False)]
        for hop in range(1, self.blk):
            send = lax.dynamic_index_in_dim(pieces, mine ^ hop, 0, keepdims=False)
            got.append(lax.ppermute(send, AXES, self.pairs((hop, hop))))
        return got


class Chunk:
    def __init__(self, ex, line, perms):
        self.ex = ex
        self.line = line
        base = list(range(1, ex.bits))
        self.orders = [[base[n] for n in perm] + base[LEVELS:] for perm in perms]

    def bits_of(self, order):
        return [(self.ex.here >> bit) & 1 for bit in order]

    def info(self):
        places = []
        for order in self.orders:
            bit = self.bits_of(order)
            places.append((bit[0], bit[1] * 4 + bit[2] * 2 + bit[3]))
        core = self.ex.core
        own = [jnp.where(core == 0, a, b) for a, b in zip(*places)]
        other = [jnp.where(core == 0, b, a) for a, b in zip(*places)]
        return jnp.stack([self.ex.here & (self.ex.blk - 1), core] + own + other).astype(jnp.int32)

    def move(self, level, value):
        masks = tuple(1 << order[level] for order in self.orders)
        return lax.ppermute(value, AXES, self.ex.pairs(masks))

    def add(self, level, which):
        rows = self.keep.shape[1] >> level
        width = self.keep.shape[2]
        if level == 0:
            self.got = []
        tile = pl.BlockSpec((None, rows, width), lambda _: (int(level == 0), which if level else 0, 0))
        strip = pl.BlockSpec((rows, width), lambda _: (which, 0))
        return self.line.run(
            add_kernel,
            [self.keep, self.recv] + self.got,
            [sds((rows, width), BF16)],
            [tile] * 2 + [strip] * len(self.got),
        )

    def total(self):
        span = self.add(LEVELS - 1, 0)
        rows = span.shape[0]
        bits = [
            jnp.where(self.ex.core == 0, a, b)
            for a, b in zip(*(self.bits_of(order)[LEVELS:] for order in self.orders))
        ]
        for level, bit in enumerate(bits, LEVELS):
            rows //= 2
            recv = self.move(level, lax.dynamic_slice_in_dim(span, (1 - bit) * rows, rows, 0))
            span = add_up([lax.dynamic_slice_in_dim(span, bit * rows, rows, 0), recv])
        for level, bit in reversed(list(enumerate(bits, LEVELS))):
            recv = self.move(level, span)
            low = jnp.where(bit == 0, span, recv)
            span = jnp.concatenate([low, jnp.where(bit == 0, recv, span)], axis=0)
        self.spans = {"p": span}

    def join(self):
        spans = [self.spans[name] for name in ("p", "g0", "g1", "g2") if name in self.spans]
        rows, width = spans[0].shape
        return self.line.run(join_kernel, spans, [sds((len(spans) * rows, width), BF16)])

    def do(self, step):
        if step == "c":
            self.recv = self.ex.move_core(self.send)
        elif step[0] == "r":
            level = int(step[1])
            total = self.add(level, 1)
            self.got.append(self.move(level, total))
        elif step == "f":
            self.total()
        elif step == "g0":
            self.spans[step] = self.move(3, self.spans["p"])
        elif step in ("g1", "g2"):
            self.spans[step] = self.move(2, self.spans["p" if step == "g1" else "g0"])
        elif step == "h":
            self.spans = {"p": self.join()}
        elif step == "j":
            self.quarters = {"A": self.join()}
        elif step == "g3":
            self.quarters["B"] = self.move(1, self.quarters["A"])
        elif step == "g4":
            self.quarters["C"] = self.move(0, self.quarters["A"])
        elif step == "g5":
            self.quarters["D"] = self.move(0, self.quarters["B"])
        else:
            name = step[1]
            self.others[name] = self.ex.move_core(self.quarters[name])


class Line:
    def __init__(self):
        self.last = None
        self.weight = None

    def run(self, kernel, ins, out_shapes, specs=None, vmem=16):
        after = [] if self.last is None else [self.last]
        near = pl.BlockSpec(memory_space=pltpu.VMEM)
        outs = pl.pallas_call(
            functools.partial(skip, len(after), kernel),
            grid=() if specs is None else (1,),
            in_specs=[pl.BlockSpec(memory_space=pl.ANY)] * len(after) + (specs or [near] * len(ins)),
            out_specs=[near if specs is None else full(*shape.shape) for shape in out_shapes],
            out_shape=out_shapes,
            compiler_params=pltpu.CompilerParams(vmem_limit_bytes=vmem * 2**20),
            cost_estimate=cost(STEP if self.weight is None else self.weight),
        )(*after, *ins)
        self.last = outs[0]
        return outs[0]


def skip(count, kernel, *refs):
    kernel(*refs[count:])


def add_kernel(*refs):
    out = refs[-1]
    height = 32 if out.shape[0] % 32 == 0 else out.shape[0]

    def body(n, _):
        at = pl.ds(pl.multiple_of(n * height, height), height)
        total = refs[0][at, :].astype(F32)
        for ref in refs[1:-1]:
            total = total + ref[at, :].astype(F32)
        out[at, :] = total.astype(BF16)
        return 0

    lax.fori_loop(0, out.shape[0] // height, body, 0)


def join_kernel(*refs):
    start = 0
    for ref in refs[:-1]:
        refs[-1][start : start + ref.shape[0], :] = ref[...]
        start += ref.shape[0]


def order_kernel(info, *refs):
    rows = refs[0].shape[0]
    for hop, ref in enumerate(refs[:-1]):
        refs[-1][pl.ds(pl.multiple_of((info[0] ^ hop) * rows, rows), rows), :] = ref[...]


def sum_kernel(one, other, out):
    out[...] = one[...] + other[...]


def add_up(terms):
    total = terms[0].astype(F32)
    for term in terms[1:]:
        total = total + term.astype(F32)
    return total.astype(BF16)


def local(
    mesh_rows, mesh_blk,
    tokens, seg_ids, target_index,
    qkv_weight, q_bias, v_bias, out_weight, out_bias,
    norm1_gain, norm1_shift, norm2_gain, norm2_shift,
    fc1_weight, fc1_bias, fc2_weight, fc2_bias,
    target_grad,
):
    ex = Exchange(mesh_rows, mesh_blk)
    count_rows, length, d = tokens.shape
    assert count_rows == 1
    ff = fc1_weight.shape[1]
    tiles = ff // d
    images, patches = target_grad.shape[1], target_grad.shape[2]
    per = images // mesh_blk
    groups = d // WIDE
    pieces = target_grad.reshape(mesh_blk, per * patches, d)
    got = ex.swap_blocks(pieces)
    tok = Far(tokens.reshape(length, d))
    seg, target_index = Far(seg_ids), Far(target_index)
    qkv_weight, q_bias, v_bias, out_weight, out_bias = map(
        Far, (qkv_weight, q_bias, v_bias, out_weight, out_bias)
    )
    norm1_gain, norm1_shift, norm2_gain, norm2_shift = map(
        Far, (norm1_gain, norm1_shift, norm2_gain, norm2_shift)
    )
    fc1_weight, fc1_bias, fc2_weight, fc2_bias = map(
        Far, (fc1_weight, fc1_bias, fc2_weight, fc2_bias)
    )
    picks = full(*target_index.array.shape)
    col = lambda g: (0, g)
    third = lambda n: lambda g: (0, n * groups + g)
    act = pltpu.VMEM((length, d), BF16)
    act32 = pltpu.VMEM((length, d), F32)
    act_far = pltpu.HBM((length, d), BF16)
    one = pltpu.VMEM((1, d), F32)
    vd = full(d)
    smem = pl.BlockSpec(memory_space=pltpu.SMEM)
    whole = full(length, d)
    strip = block((length, WIDE), col)
    wide = GROUP * length
    wide_spec = block((1, length, wide), lambda g: (g, 0, 0))

    line = Line()
    links = [Chunk(ex, line, perms) for perms in ORDERS]
    infos = [link.info() for link in links]
    for link, info in zip(links, infos):
        link.info_ref = info
    half = tiles // 2

    def mlp_specs(skip):
        return [
            block((d, d), lambda j, info: (0, skip + j)),
            block((d, d), lambda j, info: (skip + j, 0)),
            full(ff),
        ]

    def tile_outs(skip):
        return [
            (block((1, d, d), lambda j, info, n=n: ((j + skip) ^ info[n], 0, 0)), pltpu.HBM((half, d, d), BF16))
            for n in (2, 4)
        ]

    def b1_out(tiles):
        return block((1, d), lambda j, info: (0, j)), pltpu.VMEM((1, tiles * d), F32)

    both = pltpu.VMEM((2, d, d), BF16)
    saved = [pltpu.VMEM((length, d), BF16)] * 2
    piece = full(per * patches, d)
    pair_out = (block((2, d, WIDE), lambda g: (0, 0, g)), pltpu.HBM((2, d, d), BF16))
    links_by_name = dict(zip(("M1", "M2", "Q"), links))
    for link in links:
        link.others = {}
    fc_out = qkv_out = ()
    small_step = 0
    for step in SCHEDULE:
        line.weight = WEIGHTS.get(step)
        if step == "K0":
            normed, q, k, v, prob, mixed, middle, second = call(
                attend_kernel,
                (groups,),
                [
                    whole, full(1, length),
                    block((d, WIDE), third(0)), block((d, WIDE), third(1)), block((d, WIDE), third(2)),
                    block((WIDE, d), lambda g: (g, 0)),
                    vd, vd, vd, vd, vd, vd, vd,
                ],
                [
                    (whole, act_far), (strip, act_far), (strip, act_far), (strip, act_far),
                    (wide_spec, pltpu.HBM((groups, length, wide), BF16)),
                    (strip, act_far), (whole, act32), (whole, act),
                ],
                [
                    pltpu.VMEM((length, d), F32),
                    pltpu.VMEM((length, wide), F32),
                    pltpu.VMEM((2, d), F32),
                ],
                micros=11 * PACE, line=line,
            )(
                tok, seg, qkv_weight, qkv_weight, qkv_weight, out_weight, q_bias, v_bias, out_bias,
                norm1_gain, norm1_shift, norm2_gain, norm2_shift,
            )
        elif step == "K1":
            links[0].keep, links[0].send, out_sum, second_grad, b1a, out_grad, mlp_low, b2_grad = call(
                first_mlp_kernel,
                (half,),
                [whole, full(1, length), picks] + [piece] * 4 + mlp_specs(0),
                [
                    *tile_outs(0), (whole, act32), (whole, act32), b1_out(half),
                    (whole, act32), (whole, act), (full(1, d), one),
                ],
                [both, pltpu.VMEM((1, ff), F32), *saved],
                micros=12 * PACE, prefetch=1, line=line,
            )(infos[0], Near(second), seg, target_index, *got, fc1_weight, fc2_weight, fc1_bias)
            line.last = b2_grad
        elif step == "K2a":
            links[1].keep, links[1].send, out_sum, second_grad, b1b = call(
                functools.partial(middle_mlp_kernel, half),
                (1,),
                [whole, whole] + mlp_specs(half) + [whole] * 2,
                [*tile_outs(0), (whole, act32), (whole, act32), b1_out(1)],
                [both, pltpu.VMEM((1, ff), F32), *saved],
                micros=6 * PACE, prefetch=1, line=line,
            )(infos[1], Near(second), Near(mlp_low), fc1_weight, fc2_weight, fc1_bias, Near(out_sum), Near(second_grad))
            line.last = b1b
        elif step == "K2b":
            links[1].keep, links[1].send, out_sum, b1c, middle_grad, branch, n2g, n2s, ob_grad = call(
                functools.partial(second_mlp_kernel, half + 1),
                (1,),
                [whole, whole] + mlp_specs(half + 1) + [whole] * 4 + [vd] + [pl.BlockSpec(memory_space=pl.ANY)] * 2,
                [
                    *tile_outs(1), (whole, act32), b1_out(1),
                    (whole, act32), (whole, act), (full(1, d), one), (full(1, d), one), (full(1, d), one),
                ],
                [both, pltpu.VMEM((length, d), F32), pltpu.VMEM((1, ff), F32), *saved],
                micros=7 * PACE, prefetch=1, line=line, aliases={11: 0, 12: 1},
            )(
                infos[1], Near(second), Near(mlp_low), fc1_weight, fc2_weight, fc1_bias,
                *map(Near, (out_sum, second_grad, middle, out_grad)), norm2_gain,
                Far(links[1].keep), Far(links[1].send),
            )
            line.last = ob_grad
        elif step in ("K3", "K3a", "K3b"):
            skip = FIRST if step == "K3b" else 0
            count = {"K3": groups, "K3a": FIRST, "K3b": groups - FIRST}[step]
            at = lambda g, skip=skip: (0, g + skip)
            some = block((length, WIDE), at)
            pair_out = (block((2, d, WIDE), lambda g, skip=skip: (0, 0, g + skip)), pltpu.HBM((2, d, d), BF16))
            row_out = (block((1, WIDE), at), pltpu.HBM((1, d), F32))
            earlier = [] if step != "K3b" else [links[2].keep, links[2].send, dq, dk, dv, qb_grad, vb_grad]
            links[2].keep, links[2].send, dq, dk, dv, qb_grad, vb_grad = call(
                functools.partial(attend_back_kernel, skip, len(earlier)),
                (count,),
                [
                    smem, whole, whole, whole, some, some, some,
                    block((1, length, wide), lambda g, skip=skip: (g + skip, 0, 0)),
                    block((WIDE, d), lambda g, skip=skip: (g + skip, 0)),
                ]
                + [pl.BlockSpec(memory_space=pl.ANY)] * len(earlier),
                [pair_out, pair_out, *[(some, act_far)] * 3, row_out, row_out],
                [
                    pltpu.VMEM((length, wide), F32),
                    pltpu.VMEM((length, wide), BF16),
                    pltpu.VMEM((4, d, WIDE), BF16),
                ],
                micros=4.5 * count * PACE, line=line,
                aliases={9 + n: n for n in range(len(earlier))},
            )(
                infos[2], Far(normed), Far(mixed), Near(branch), *map(Far, (q, k, v, prob)), out_weight,
                *map(Far, earlier),
            )
            line.last = dq
        elif step == "K4":
            tokens_grad, small, *picked = call(
                finish_kernel,
                (groups,),
                [
                    smem, whole, whole, strip, strip, strip,
                    block((d, WIDE), third(0)), block((d, WIDE), third(1)), block((d, WIDE), third(2)),
                    vd, whole, whole, vd, full(1, length), picks,
                ]
                + [full(1, d)] * 6 + [full(1, half * d)] + [full(1, d)] * 2,
                [
                    (whole, pltpu.HBM((length, d), BF16)),
                    (full(8 + tiles, d), sds((8 + tiles, d), F32)),
                    *[(full(per * patches, d), sds((per * patches, d), BF16))] * 4,
                ],
                [pltpu.VMEM((length, d), F32)],
                micros=7 * PACE, line=line,
            )(
                infos[0], tok, Near(middle_grad), *map(Far, (dq, dk, dv)), qkv_weight, qkv_weight, qkv_weight, norm1_gain,
                Near(middle), Near(out_sum), fc2_bias, seg, target_index,
                Far(qb_grad), Far(vb_grad), *map(Near, (ob_grad, n2g, n2s, b2_grad, b1a, b1b, b1c)),
            )
            line.last = small
        elif step == "T":
            swapped = picked[:1] + [
                lax.ppermute(picked[hop], AXES, ex.pairs((hop, hop))) for hop in range(1, mesh_blk)
            ]
        elif step == "t":
            targets = line.run(
                order_kernel,
                [infos[0], *swapped],
                [sds((images * patches, d), BF16)],
                [smem] + [full(per * patches, d)] * mesh_blk,
            )
        elif step == "S":
            small = line.run(sum_kernel, [small, small_recv], [sds(small.shape, F32)])
            small_step += 1
        elif step == "s":
            small_recv = lax.ppermute(small, AXES, ex.pairs((1 << small_step,) * 2))
        else:
            name, step = step.split()
            link = links_by_name[name]
            if step[0] != "v":
                link.do(step)
                continue
            names = ["ABCD".index(n) for n in step[1:]]
            values = [v for n in step[1:] for v in (link.quarters[n], link.others[n])]
            if name == "Q":
                shapes = [sds((d, 3 * d), F32), sds((d, d), F32)]
                qkv_out = place(None, names, link.info_ref, values, shapes, qkv_out, line)
            else:
                shapes = [sds((ff, d), F32), sds((d, ff), F32)]
                fc_out = place(int(name[1]) - 1, names, link.info_ref, values, shapes, fc_out, line)
    for _ in range(small_step, ex.bits):
        small = small + lax.ppermute(small, AXES, ex.pairs((1 << small_step,) * 2))
        small_step += 1
    fc2_full, fc1_full = fc_out
    qkv_full, out_full = qkv_out
    return (
        targets.reshape(1, images, patches, d),
        tokens_grad.reshape(count_rows, length, d),
        qkv_full,
        small[0], small[1],
        out_full,
        small[2], small[3], small[4], small[5], small[6],
        fc1_full,
        small[8:].reshape(ff),
        fc2_full,
        small[7],
    )


def solution(mesh):
    rows, blk = mesh.shape["rows"], mesh.shape["blk"]

    def body(*args):
        return local(rows, blk, *args)

    return jax.shard_map(
        body,
        mesh=mesh,
        in_specs=(
            P(("rows", "blk"), None, None),
            P(("rows", "blk"), None),
            P(("rows", "blk"), None, None),
        )
        + (P(),) * 13
        + (P("blk", "rows", None, None),),
        out_specs=(
            P("blk", "rows", None, None),
            P(("rows", "blk"), None, None),
        )
        + (P(),) * 13,
        check_vma=False,
    )
```
